32 devices in a mesh: gx: 2 (over y), gy: 4 (over x, core), gz: 4 (over z).
Axes of the slice: x: 2, y: 2, z: 4, core: 2. Of those that a mesh axis runs over, the one named last changes fastest.
Arguments:
- displacement: float32 [6, 8, 32, 512], P(None, 'gx', 'gy', 'gz'), may hold values from -6 to 6
- velocity: float32 [6, 8, 32, 512], P(None, 'gx', 'gy', 'gz'), may hold values from -6 to 6
- moments: float32 [6, 8, 32, 512], P(None, 'gx', 'gy', 'gz'), may hold values from -6 to 6
- sector_bit: int32 [2, 8, 32, 512], P(None, 'gx', 'gy', 'gz'), may hold values from 0 to 1
- weight_in: bfloat16 [32, 256], replicated, may hold values from -1 to 1
- bias_in: float32 [256], replicated, may hold values from -3 to 3
- weight_mid: bfloat16 [256, 256], replicated, may hold values from -0.375 to 0.375
- weight_out: bfloat16 [256, 4], replicated, may hold values from -0.375 to 0.375
Outputs:
- displacement_out: float32 [6, 8, 32, 512], P(None, 'gx', 'gy', 'gz')
- velocity_out: float32 [6, 8, 32, 512], P(None, 'gx', 'gy', 'gz')
- moments_out: float32 [6, 8, 32, 512], P(None, 'gx', 'gy', 'gz')
The draws below stay inside these ranges and needn't reach their ends.
All inputs are finite; a program needn't handle non-finite values.
Results may differ from the reference program's by a relative error of at most 0.0014.
Values sent between devices are 32-bit elements; how exact they have to be, the bound alone decides.
No kernel may reach another device: no remote copies, remote signals or barrier semaphores. Data moves between devices by JAX's collectives and lax.ppermute only.
A program may use at most 64 MiB of HBM per device.

```python
import jax
import jax.numpy as jnp
from jax import lax

FEAT = 32
HID = 256
NX = 8
NY = 32
NZ = 512


def touch_ends(values, rng, least, largest):
    longest = values.shape.index(max(values.shape))
    spots = []
    for shift in (0, 1):
        where = [jax.random.randint(jax.random.fold_in(rng, axis), (), 0, length) for axis, length in enumerate(values.shape)]
        where[longest] = (where[longest] + shift) % values.shape[longest]
        spots.append(tuple(where))
    return values.at[spots[0]].set(least).at[spots[1]].set(largest)


def block_levels(stream_key, extent, pieces, least, high):
    def one(dim, parts):
        steps = jax.random.uniform(jax.random.fold_in(jax.random.fold_in(stream_key, 6), dim), (parts,), jnp.float32, least / len(pieces), high / len(pieces))
        return jnp.repeat(jnp.exp(steps), extent[dim] // parts).reshape((-1,) + (1,) * (len(extent) - dim - 1))

    level = one(*pieces[0])
    for cut in pieces[1:]:
        level = level * one(*cut)
    return level


def centred(stream_key, extent, deviation, reach, shards=(), held_as=jnp.bfloat16):
    entries = jax.random.normal(stream_key, extent, jnp.float32) * deviation
    if len(shards) > 0:
        entries = block_levels(stream_key, extent, shards, -0.22, 0.18) * entries
    return jnp.clip(entries, min=-reach, max=reach).astype(held_as)


def setup_inputs(seed: int = 0) -> dict:
    splits = jax.random.split(jax.random.key(seed), 9)
    displacement = centred(splits[0], (6, NX, NY, NZ), 1.0, 6.0, ((1, 2), (2, 4), (3, 4)), jnp.float32)
    velocity = centred(splits[1], (6, NX, NY, NZ), 1.0, 6.0, ((1, 2), (2, 4), (3, 4)), jnp.float32)
    moments = centred(splits[2], (6, NX, NY, NZ), 1.0, 6.0, ((1, 2), (2, 4), (3, 4)), jnp.float32)
    sector_bit = touch_ends(jax.random.randint(splits[3], (2, NX, NY, NZ), 0, 2), jax.random.fold_in(splits[3], 1), 0, 1).astype(jnp.int32)
    weight_in = centred(splits[4], (FEAT, HID), FEAT ** -0.5, 1.0)
    bias_in = centred(splits[5], (HID,), 0.5, 3.0, (), jnp.float32)
    weight_mid = centred(splits[6], (HID, HID), HID ** -0.5, 0.375)
    weight_out = centred(splits[7], (HID, 4), HID ** -0.5, 0.375)
    return {"displacement": displacement, "velocity": velocity, "moments": moments, "sector_bit": sector_bit, "weight_in": weight_in, "bias_in": bias_in, "weight_mid": weight_mid, "weight_out": weight_out}


half_step = 0.1
lattice_step = 0.25
second_shell = 0.5

def offsets(part):
    sign = 2 * part - 1
    return [(sign * (corner >> 2 & 1), sign * (corner >> 1 & 1), sign * (corner & 1)) for corner in range(8)]

def shifted(field, offset):
    return jnp.roll(field, (-offset[0], -offset[1], -offset[2]), (1, 2, 3))

def features(displacement, moments, part):
    other = 1 - part
    own_disp = displacement[3 * part:3 * part + 3]
    own_spin = moments[3 * part:3 * part + 3]
    rows = []
    for offset in offsets(part):
        near_disp = shifted(displacement[3 * other:3 * other + 3], offset)
        near_spin = shifted(moments[3 * other:3 * other + 3], offset)
        rows.append(near_disp - own_disp)
        rows.append(lax.optimization_barrier(jnp.sum(own_spin * near_spin, axis=0, keepdims=True)))
    return jnp.concatenate(rows, 0).astype(jnp.bfloat16)

def network(block, weight_in, bias_in, weight_mid, weight_out):
    dims = (((0,), (0,)), ((), ()))
    first = lax.dot_general(weight_in, block, dims, preferred_element_type=jnp.float32)
    first = jax.nn.silu(first + bias_in[:, None]).astype(jnp.bfloat16)
    second = lax.dot_general(weight_mid, first, dims, preferred_element_type=jnp.float32)
    second = jax.nn.silu(second).astype(jnp.bfloat16)
    return lax.dot_general(weight_out, second, dims, preferred_element_type=jnp.float32)

def heads_of(table, weight_in, bias_in, weight_mid, weight_out):
    width, size_x, size_y, size_z = table.shape
    blocks = table.reshape(width, size_x * size_y, size_z).transpose(1, 0, 2)
    result = lax.map(lambda block: network(block, weight_in, bias_in, weight_mid, weight_out), blocks)
    return result.transpose(1, 0, 2).reshape(4, size_x, size_y, size_z)

def rotate(moment, field, step):
    square = lax.optimization_barrier(jnp.sum(field * field, axis=0))
    theta = step * jnp.sqrt(square)
    along = jnp.sinc(theta / jnp.pi)
    across = 0.5 * jnp.sinc(theta / (2.0 * jnp.pi)) ** 2
    cross = jnp.stack([field[1] * moment[2] - field[2] * moment[1], field[2] * moment[0] - field[0] * moment[2], field[0] * moment[1] - field[1] * moment[0]])
    inner = lax.optimization_barrier(jnp.sum(field * moment, axis=0))
    return jnp.cos(theta) * moment + step * along * cross + step * step * across * inner * field

def reference(displacement, velocity, moments, sector_bit, weight_in, bias_in, weight_mid, weight_out):
    size_x, size_y, size_z = (displacement.shape[1], displacement.shape[2], displacement.shape[3])
    heads_zero = heads_of(features(displacement, moments, 0), weight_in, bias_in, weight_mid, weight_out)
    heads_one = heads_of(features(displacement, moments, 1), weight_in, bias_in, weight_mid, weight_out)
    force = jnp.concatenate([heads_zero[0:3], heads_one[0:3]], 0)
    coupling = 1.0 + 0.5 * jnp.tanh(jnp.stack([heads_zero[3], heads_one[3]]))
    velocity_out = velocity + lattice_step * force
    displacement_out = displacement + lattice_step * velocity_out
    grid = (size_x, size_y, size_z)
    index_x = lax.broadcasted_iota(jnp.int32, grid, 0)
    index_y = lax.broadcasted_iota(jnp.int32, grid, 1)
    index_z = lax.broadcasted_iota(jnp.int32, grid, 2)
    parity = (index_x + index_y + index_z) % 2
    sector_map = 4 * jnp.arange(2, dtype=jnp.int32)[:, None, None, None] + 2 * sector_bit + parity[None]
    spins = moments
    for sector in list(range(8)) + list(range(7, -1, -1)):
        part = sector // 4
        other = 1 - part
        own = spins[3 * part:3 * part + 3]
        near = spins[3 * other:3 * other + 3]
        near_total = jnp.zeros(own.shape, jnp.float32)
        for offset in offsets(part):
            near_total = near_total + shifted(near, offset)
        shell = jnp.zeros(own.shape, jnp.float32)
        for axis_offset in ((1, 0, 0), (-1, 0, 0), (0, 1, 0), (0, -1, 0), (0, 0, 1), (0, 0, -1)):
            shell = shell + shifted(own, axis_offset)
        field = coupling[part][None] * near_total + second_shell * shell
        turned = rotate(own, field, half_step)
        updated = jnp.where((sector_map[part] == sector)[None], turned, own)
        if part == 0:
            spins = jnp.concatenate([updated, near], 0)
        else:
            spins = jnp.concatenate([near, updated], 0)
    return (displacement_out, velocity_out, spins)
```

```python
import functools

import jax
import jax.numpy as jnp
import numpy as np
from jax import lax
from jax.experimental import pallas as pl
from jax.experimental.pallas import tpu as pltpu
from jax.sharding import PartitionSpec as P

half_step = 0.1
lattice_step = 0.25
second_shell = 0.5

f32 = jnp.float32
bf16 = jnp.bfloat16
SUB, LANE = 8, 128
SLAB = 32
XL = 4
ORDER = (0, 2, 1, 3)
TILE = (SUB, LANE)


def iota(dim):
    return lax.broadcasted_iota(jnp.int32, TILE, dim)


def odd_mask(par):
    return ((iota(0) + iota(1) + par) & 1) == 1


def lane_block():
    return ((iota(1) + SLAB // 2) // SLAB) & 3


def lanes(v, shift):
    shift = shift % LANE
    return v if shift == 0 else pltpu.roll(v, shift, 1)


def rows(v, shift):
    return pltpu.roll(v, shift % SUB, 0)


def merge_blocks(tiles):
    block = lane_block()
    out = lanes(tiles[0], 0)
    for b in range(1, 4):
        out = jnp.where(block == b, lanes(tiles[b], SLAB * b), out)
    return out


def vmem_call(body, out_shapes, *args, scratch=(), name=None, cost=None):
    spec = pl.BlockSpec(memory_space=pltpu.VMEM)
    return pl.pallas_call(
        body,
        out_shape=tuple(jax.ShapeDtypeStruct(s, d) for s, d in out_shapes),
        in_specs=[spec] * len(args),
        out_specs=tuple(spec for _ in out_shapes),
        scratch_shapes=list(scratch),
        compiler_params=pltpu.CompilerParams(vmem_limit_bytes=56 << 20),
        name=name,
        cost_estimate=cost,
    )(*args)


def pack_body(disp, mom, bit, out):
    for i in range(14):
        if i < 6:
            tiles = [disp[i, x] for x in ORDER]
        elif i < 12:
            tiles = [mom[i - 6, x] for x in ORDER]
        else:
            tiles = [bit[i - 12, x].astype(f32) for x in ORDER]
        out[i] = merge_blocks(tiles)


def halo_body(disp, mom, bit, low, high, slab, brick, xup, xdn, yup, ydn):
    upper = (iota(1) & (SLAB - 1)) >= SLAB // 2
    e0 = odd_mask(0)
    for i in range(14):
        slab[i] = jnp.where(upper, low[i], high[i])
    for p in range(2):
        for k in range(4):
            i = 6 + 3 * p + k if k < 3 else 12 + p
            tiles = [mom[3 * p + k, x] if k < 3 else bit[p, x].astype(f32) for x in range(XL)]
            for xh in range(2):
                even, odd = tiles[2 * xh], tiles[2 * xh + 1]
                brick[xh, 4 * p + k] = jnp.where(e0, odd, even)
                brick[2 + xh, 4 * p + k] = jnp.where(e0, even, odd)
            h = slab[i]
            brick[4, 4 * p + k] = jnp.where(e0, lanes(h, 64), h)
    for i in range(6):
        src = disp if i < 3 else mom
        k = i % 3
        base = 0 if i < 3 else 6
        xup[2 * i] = src[3 + k, XL - 1]
        xup[2 * i + 1] = slab[base + 3 + k]
        xdn[2 * i] = src[k, 0]
        xdn[2 * i + 1] = slab[base + k]
        yup[i] = jnp.zeros(TILE, f32)
        ydn[i] = jnp.zeros(TILE, f32)
        for x in range(XL):
            yup[i, x : x + 1, :] = src[3 + k, x, SUB - 1 : SUB, :]
            ydn[i, x : x + 1, :] = src[k, x, 0:1, :]
        yup[i, XL : XL + 1, :] = slab[base + 3 + k, SUB - 1 : SUB, :]
        ydn[i, XL : XL + 1, :] = slab[base + k, 0:1, :]


def near_tiles(p, disp, mom, slab, xf, yr, xyr, near):
    q = 1 - p
    lane, sub = iota(1), iota(0)
    block = lane_block()
    edge_x = XL - 1 if p == 0 else 0
    for i in range(6):
        src = disp if i < 3 else mom
        k = i % 3
        c = [src[3 * q + k, x] for x in range(XL)]
        h = slab[(0 if i < 3 else 6) + 3 * q + k]
        fc, fh = xf[2 * i], xf[2 * i + 1]

        def wide(row):
            return jnp.broadcast_to(row, TILE)

        for dy in range(2):
            if dy:
                step = 1 if p == 0 else -1
                put = sub == (0 if p == 0 else SUB - 1)
                c = [jnp.where(put, wide(yr[i, x : x + 1, :]), rows(c[x], step)) for x in range(XL)]
                h = jnp.where(put, wide(yr[i, XL : XL + 1, :]), rows(h, step))
                fc = jnp.where(put, wide(xyr[i, edge_x : edge_x + 1, :]), rows(fc, step))
                fh = jnp.where(put, wide(xyr[i, XL : XL + 1, :]), rows(fh, step))
            for dz in range(2):
                if dz == 0:
                    cs, hs, fcs, fhs = c, h, fc, fh
                else:
                    step = 1 if p == 0 else -1
                    seam = LANE - 1 if p == 0 else 0
                    at_seam = lane == seam
                    at_seams = (lane & (SLAB - 1)) == (SLAB - 1 if p == 0 else 0)
                    cs = [
                        lanes(jnp.where(at_seam, lanes(h, -SLAB * ORDER[x]), c[x]), step)
                        for x in range(XL)
                    ]
                    hs = lanes(jnp.where(at_seams, merge_blocks([c[x] for x in ORDER]), h), step)
                    fcs = lanes(jnp.where(at_seam, lanes(fh, -SLAB * ORDER[edge_x]), fc), step)
                    fhs = lanes(jnp.where(at_seams, lanes(fc, SLAB * ORDER[edge_x]), fh), step)
                at = 2 * dy + dz
                line = [fcs] + cs if p == 0 else cs + [fcs]
                for j in range(XL + 1):
                    near[i, at, j] = line[j]
                near[i, at, XL + 1] = hs
                if p == 0:
                    moved = jnp.where(block == 0, lanes(fhs, SLAB), lanes(hs, 2 * SLAB))
                    moved = jnp.where(block == 1, lanes(hs, -SLAB), moved)
                else:
                    moved = jnp.where(block == 3, lanes(fhs, -SLAB), lanes(hs, 2 * SLAB))
                    moved = jnp.where(block == 2, lanes(hs, SLAB), moved)
                near[i, at, XL + 2] = moved


def feature_rows(p, disp, mom, slab, near, table):
    for slot in range(XL + 1):
        if slot < XL:
            own = [disp[3 * p + k, slot] for k in range(3)]
            own += [mom[3 * p + k, slot] for k in range(3)]
        else:
            own = [slab[3 * p + k] for k in range(3)] + [slab[6 + 3 * p + k] for k in range(3)]
        for o in range(8):
            dx, at = o >> 2, o & 3
            if slot == XL:
                j = XL + 1 + dx
            else:
                j = slot + 1 - dx if p == 0 else slot + dx
            for k in range(3):
                table[slot, pl.ds(4 * o + k, SUB, stride=32), :] = near[k, at, j] - own[k]
            dot = own[3] * near[3, at, j] + own[4] * near[4, at, j] + own[5] * near[5, at, j]
            table[slot, pl.ds(4 * o + 3, SUB, stride=32), :] = dot


def network_body(
    disp, mom, vel, slab, xup, xdn, yup, ydn, xyup, xydn, w_in, b_in, w_mid, w_out,
    disp_out, vel_out, cbrick, near, table, heads,
):
    e0 = odd_mask(0)
    for p in range(2):
        args = (xup, yup, xyup) if p == 0 else (xdn, ydn, xydn)
        near_tiles(p, disp, mom, slab, *args, near)
        feature_rows(p, disp, mom, slab, near, table)

        def one(slot, carry):
            for y in range(0, SUB, 2):
                block = jnp.concatenate(
                    [table[slot, 32 * (y + j) : 32 * (y + j + 1), :].astype(bf16) for j in range(2)],
                    axis=1,
                )
                bias = b_in[...]
                first = jnp.dot(w_in[...], block, preferred_element_type=f32)
                u = first + jnp.concatenate([bias, bias], axis=1)
                first = (u + u * jnp.tanh(u)).astype(bf16)
                u = jnp.dot(w_mid[...], first, preferred_element_type=f32)
                second = (u + u * jnp.tanh(u)).astype(bf16)
                out = jnp.dot(w_out[...], second, preferred_element_type=f32)
                for j in range(2):
                    heads[slot, pl.ds(y + j, SUB, stride=SUB), :] = out[:, LANE * j : LANE * (j + 1)]
            return carry

        lax.fori_loop(0, XL + 1, one, 0)
        coupling = []
        for slot in range(XL + 1):
            coupling.append(1.0 + 0.5 * jnp.tanh(heads[slot, 3 * SUB : 4 * SUB, :]))
            if slot < XL:
                for k in range(3):
                    v = vel[3 * p + k, slot] + lattice_step * heads[slot, k * SUB : (k + 1) * SUB, :]
                    vel_out[3 * p + k, slot] = v
                    disp_out[3 * p + k, slot] = disp[3 * p + k, slot] + lattice_step * v
        for xh in range(2):
            even, odd = coupling[2 * xh], coupling[2 * xh + 1]
            cbrick[xh, p] = jnp.where(e0, odd, even)
            cbrick[2 + xh, p] = jnp.where(e0, even, odd)
        cbrick[4, p] = jnp.where(e0, lanes(coupling[4], 64), coupling[4])


def even_fit(func, terms):
    edge = (np.pi / 2) ** 2 * 1.0001
    node = np.cos((np.arange(400) + 0.5) * np.pi / 400)
    w = 0.5 * edge * (1 + node)
    basis = np.stack([w**n for n in range(terms)], 1)
    return [float(c) for c in np.linalg.lstsq(basis, func(np.sqrt(w)), rcond=None)[0]]


SIN = even_fit(lambda r: np.sin(r) / r, 5)
COS = even_fit(np.cos, 5)


def horner(coeffs, w):
    out = coeffs[-1]
    for c in reversed(coeffs[:-1]):
        out = out * w + c
    return out


def rotated(s, b, h):
    square = b[0] * b[0] + b[1] * b[1] + b[2] * b[2]
    inverse = lax.rsqrt(jnp.maximum(square, 1e-30))
    half = (0.5 * h) * (square * inverse)
    turns = jnp.round(half * (1.0 / np.pi))
    rest = (half - turns * 3.140625) - turns * (np.pi - 3.140625)
    w = rest * rest
    sine = horner(SIN, w) * rest * inverse
    cosine = horner(COS, w)
    along = 2.0 * sine * cosine
    across = 2.0 * sine * sine
    inner = across * (b[0] * s[0] + b[1] * s[1] + b[2] * s[2])
    keep = 1.0 - across * square
    cross = (
        b[1] * s[2] - b[2] * s[1],
        b[2] * s[0] - b[0] * s[2],
        b[0] * s[1] - b[1] * s[0],
    )
    return [keep * s[k] + along * cross[k] + inner * b[k] for k in range(3)]


def turns_body(nx, ny, masks, *refs):
    count = len(masks)
    bricks, cbricks = refs[:count], refs[count : 2 * count]
    out = refs[2 * count]
    mc, mh, hb, cc, ch, chb, tc, th, nc, nh = refs[2 * count + 1 :]
    xh_all, groups = 2 * nx, nx // 2
    ix, iy = lax.axis_index("gx"), lax.axis_index("gy")
    lane, sub = iota(1), iota(0)
    block = lane_block()
    first_half = block < 2

    for n, (mx, my) in enumerate(masks):
        bx, by = ix ^ mx, iy ^ my
        for p in range(2):
            for par in range(2):
                for xh in range(2):
                    for k in range(4):
                        mc[p, par, k, by, 2 * bx + xh] = bricks[n][2 * par + xh, 4 * p + k]
                    cc[p, par, by, 2 * bx + xh] = cbricks[n][2 * par + xh, p]
            for k in range(4):
                hb[by, bx, 4 * p + k] = bricks[n][4, 4 * p + k]
            chb[by, bx, p] = cbricks[n][4, p]

    def joined(even, odd):
        return (
            jnp.where(first_half, even, lanes(odd, 64)),
            jnp.where(first_half, lanes(even, 64), odd),
        )

    for y in range(ny):
        for g in range(groups):
            for p in range(2):
                for k in range(4):
                    zero, one = joined(hb[y, 2 * g, 4 * p + k], hb[y, 2 * g + 1, 4 * p + k])
                    mh[p, 0, k, y, g], mh[p, 1, k, y, g] = zero, one
                zero, one = joined(chb[y, 2 * g, p], chb[y, 2 * g + 1, p])
                ch[p, 0, y, g], ch[p, 1, y, g] = zero, one

    def ring(y):
        up = jnp.where(y == ny - 1, 0, y + 1)
        down = jnp.where(y == 0, ny - 1, y - 1)
        return up, down

    def next_block(tiles, g):
        other = tiles[(g + 1) % groups]
        return lanes(jnp.where(block == 0, other, tiles[g]) if groups > 1 else tiles[g], -SLAB)

    def last_block(tiles, g):
        other = tiles[(g - 1) % groups]
        return lanes(jnp.where(block == 3, other, tiles[g]) if groups > 1 else tiles[g], SLAB)

    def z_next(c, h):
        cs = [
            lanes(jnp.where(lane == 0, lanes(h[x // 4], -SLAB * (x % 4)), c[x]), -1)
            for x in range(xh_all)
        ]
        hs = [
            lanes(jnp.where((lane & (SLAB - 1)) == 0, merge_blocks(c[4 * g : 4 * g + 4]), h[g]), -1)
            for g in range(groups)
        ]
        return cs, hs

    def z_last(c, h):
        cs = [
            lanes(jnp.where(lane == LANE - 1, lanes(h[x // 4], -SLAB * (x % 4)), c[x]), 1)
            for x in range(xh_all)
        ]
        hs = [
            lanes(
                jnp.where((lane & (SLAB - 1)) == SLAB - 1, merge_blocks(c[4 * g : 4 * g + 4]), h[g]), 1
            )
            for g in range(groups)
        ]
        return cs, hs

    def near_total(p):
        q = 1 - p
        e0 = odd_mask(0)

        def pairs(y, carry):
            for k in range(3):
                for ref, to, size in ((mc, tc, xh_all), (mh, th, groups)):
                    zero = [ref[q, 0, k, y, j] for j in range(size)]
                    one = [ref[q, 1, k, y, j] for j in range(size)]
                    even = [jnp.where(e0, one[j], zero[j]) for j in range(size)]
                    odd = [jnp.where(e0, zero[j], one[j]) for j in range(size)]
                    for j in range(size):
                        to[0, k, y, j] = zero[j] + one[j]
                        if p == 0:
                            prev = odd[(j - 1) % size] if ref is mc else last_block(odd, j)
                            to[1, k, y, j] = even[j] + prev
                        else:
                            after = even[(j + 1) % size] if ref is mc else next_block(even, j)
                            to[1, k, y, j] = odd[j] + after
            return carry

        lax.fori_loop(0, ny, pairs, 0)

        def sums(y, carry):
            up, down = ring(y)
            for k in range(3):
                got = []
                for t in range(2):
                    v = []
                    for ref, size in ((tc, xh_all), (th, groups)):
                        row = []
                        for j in range(size):
                            own = ref[t, k, y, j]
                            if p == 0:
                                moved = rows(jnp.where(sub == SUB - 1, ref[t, k, down, j], own), 1)
                            else:
                                moved = rows(jnp.where(sub == 0, ref[t, k, up, j], own), -1)
                            row.append(own + moved)
                        v.append(row)
                    cs, hs = z_last(*v) if p == 0 else z_next(*v)
                    got.append(
                        (
                            [v[0][j] + cs[j] for j in range(xh_all)],
                            [v[1][j] + hs[j] for j in range(groups)],
                        )
                    )
                for kind, to, size in ((0, nc, xh_all), (1, nh, groups)):
                    for j in range(size):
                        whole, split = got[0][kind][j], got[1][kind][j]
                        if p == 0:
                            to[0, k, y, j] = jnp.where(e0, whole, split)
                            to[1, k, y, j] = jnp.where(e0, split, whole)
                        else:
                            to[0, k, y, j] = jnp.where(e0, split, whole)
                            to[1, k, y, j] = jnp.where(e0, whole, split)
            return carry

        lax.fori_loop(0, ny, sums, 0)

    def turn(p, par, bit, h):
        opp = 1 - par
        e = odd_mask(par)

        def body(y, carry):
            up, down = ring(y)
            shell_c, shell_h = [], []
            for k in range(3):
                c = [mc[p, opp, k, y, j] for j in range(xh_all)]
                hh = [mh[p, opp, k, y, g] for g in range(groups)]
                cn, hn = z_next(c, hh)
                cl, hl = z_last(c, hh)
                sc, sh = [], []
                for j in range(xh_all):
                    x = c[j] + jnp.where(e, c[(j + 1) % xh_all], c[(j - 1) % xh_all])
                    yp = rows(jnp.where(sub == 0, mc[p, opp, k, up, j], c[j]), -1)
                    ym = rows(jnp.where(sub == SUB - 1, mc[p, opp, k, down, j], c[j]), 1)
                    sc.append(x + (yp + ym) + (cn[j] + cl[j]))
                for g in range(groups):
                    x = hh[g] + jnp.where(e, next_block(hh, g), last_block(hh, g))
                    yp = rows(jnp.where(sub == 0, mh[p, opp, k, up, g], hh[g]), -1)
                    ym = rows(jnp.where(sub == SUB - 1, mh[p, opp, k, down, g], hh[g]), 1)
                    sh.append(x + (yp + ym) + (hn[g] + hl[g]))
                shell_c.append(sc)
                shell_h.append(sh)
            for state, couple, near, shell, size in (
                (mc, cc, nc, shell_c, xh_all),
                (mh, ch, nh, shell_h, groups),
            ):
                for j in range(size):
                    cpl = couple[p, par, y, j]
                    field = [
                        cpl * near[par, k, y, j] + second_shell * shell[k][j] for k in range(3)
                    ]
                    own = [state[p, par, k, y, j] for k in range(3)]
                    new = rotated(own, field, h)
                    hit = state[p, par, 3, y, j] == bit
                    for k in range(3):
                        state[p, par, k, y, j] = jnp.where(hit, new[k], own[k])
            return carry

        lax.fori_loop(0, ny, body, 0)

    def sweep(p, sector, h):
        turn(p, sector & 1, (sector >> 1).astype(f32), h)

    def climb(i, carry):
        sweep(0, i, half_step)
        return carry

    def middle(i, carry):
        sector = 3 - jnp.abs(3 - i)
        sweep(1, sector, jnp.where(i == 3, 2 * half_step, half_step).astype(f32))
        return carry

    def descend(i, carry):
        sweep(0, 3 - i, half_step)
        return carry

    near_total(0)
    lax.fori_loop(0, 4, climb, 0)
    near_total(1)
    lax.fori_loop(0, 7, middle, 0)
    near_total(0)
    lax.fori_loop(0, 4, descend, 0)

    e0 = odd_mask(0)
    for p in range(2):
        for k in range(3):
            for xh in range(2):
                zero = mc[p, 0, k, iy, 2 * ix + xh]
                one = mc[p, 1, k, iy, 2 * ix + xh]
                out[3 * p + k, 2 * xh] = jnp.where(e0, one, zero)
                out[3 * p + k, 2 * xh + 1] = jnp.where(e0, zero, one)


def on_device(nx, ny, nz, displacement, velocity, moments, sector_bit, weight_in, bias_in, weight_mid, weight_out):
    assert displacement.shape == (6, XL, SUB, LANE)
    assert nx % 2 == 0 and nx & (nx - 1) == 0 and ny & (ny - 1) == 0 and ny % 2 == 0
    plane = ("gx", "gy")

    def pairs(move):
        out = []
        for x in range(nx):
            for y in range(ny):
                tx, ty = move(x, y)
                out.append((x * ny + y, tx % nx * ny + ty % ny))
        return out

    def shift(v, dx, dy):
        return lax.ppermute(v, plane, pairs(lambda x, y: (x + dx, y + dy)))

    def swap(v, mx, my):
        return lax.ppermute(v, plane, pairs(lambda x, y: (x ^ mx, y ^ my)))

    def along_z(v, step):
        return lax.ppermute(v, "gz", [(i, (i + step) % nz) for i in range(nz)])

    w_in = (weight_in.T.astype(f32) * 0.5).astype(bf16)
    w_mid = (weight_mid.T.astype(f32) * 0.5).astype(bf16)
    w_out = jnp.pad(weight_out.T, ((0, SUB - 4), (0, 0)))
    hidden = weight_mid.shape[0]
    b_in = jnp.broadcast_to((0.5 * bias_in)[:, None], (hidden, LANE))

    (packed,) = vmem_call(
        pack_body, [((14, *TILE), f32)], displacement, moments, sector_bit, name="pack"
    )
    low, high = along_z(packed, 1), along_z(packed, -1)
    slab, brick, xup, xdn, yup, ydn = vmem_call(
        halo_body,
        [((14, *TILE), f32), ((5, 8, *TILE), f32)] + [((12, *TILE), f32)] * 2 + [((6, *TILE), f32)] * 2,
        displacement, moments, sector_bit, low, high,
        name="halo",
    )
    xup, xdn = shift(xup, 1, 0), shift(xdn, -1, 0)
    xyup, xydn = shift(yup, 1, 1), shift(ydn, -1, -1)
    yup, ydn = shift(yup, 0, 1), shift(ydn, 0, -1)

    far = [(mx, my) for mx in range(nx) for my in range(0, ny, 2) if mx or my]
    held = {(0, 0): brick}
    for mask in far:
        held[mask] = swap(brick, *mask)
    for mx, my in [(0, 0)] + far:
        held[mx, my + 1] = swap(held[mx, my], 0, 1)

    disp_out, vel_out, cbrick = vmem_call(
        network_body,
        [((6, XL, *TILE), f32), ((6, XL, *TILE), f32), ((5, 2, *TILE), f32)],
        displacement, moments, velocity, slab, xup, xdn, yup, ydn, xyup, xydn, w_in, b_in, w_mid, w_out,
        scratch=[
            pltpu.VMEM((6, 4, XL + 3, *TILE), f32),
            pltpu.VMEM((XL + 1, 32 * SUB, LANE), f32),
            pltpu.VMEM((XL + 1, SUB * SUB, LANE), f32),
        ],
        name="network",
    )
    cheld = {(0, 0): cbrick}
    for mask in far:
        cheld[mask] = swap(cbrick, *mask)
    for mx, my in [(0, 0)] + far:
        cheld[mx, my + 1] = swap(cheld[mx, my], 0, 1)

    masks = sorted(held)
    xh_all, groups = 2 * nx, nx // 2
    (moments_out,) = vmem_call(
        functools.partial(turns_body, nx, ny, masks),
        [((6, XL, *TILE), f32)],
        *[held[m] for m in masks],
        *[cheld[m] for m in masks],
        scratch=[
            pltpu.VMEM((2, 2, 4, ny, xh_all, *TILE), f32),
            pltpu.VMEM((2, 2, 4, ny, groups, *TILE), f32),
            pltpu.VMEM((ny, nx, 8, *TILE), f32),
            pltpu.VMEM((2, 2, ny, xh_all, *TILE), f32),
            pltpu.VMEM((2, 2, ny, groups, *TILE), f32),
            pltpu.VMEM((ny, nx, 2, *TILE), f32),
            pltpu.VMEM((2, 3, ny, xh_all, *TILE), f32),
            pltpu.VMEM((2, 3, ny, groups, *TILE), f32),
            pltpu.VMEM((2, 3, ny, xh_all, *TILE), f32),
            pltpu.VMEM((2, 3, ny, groups, *TILE), f32),
        ],
        name="turns",
    )
    return disp_out, vel_out, moments_out


def solution(mesh):
    placed = P(None, "gx", "gy", "gz")
    sizes = [mesh.shape[axis] for axis in ("gx", "gy", "gz")]
    return jax.shard_map(
        functools.partial(on_device, *sizes),
        mesh=mesh,
        in_specs=(placed,) * 4 + (P(),) * 4,
        out_specs=(placed,) * 3,
        check_vma=False,
    )
```

```python
import functools

import jax
import jax.numpy as jnp
import numpy as np
from jax import lax
from jax.experimental import pallas as pl
from jax.experimental.pallas import tpu as pltpu
from jax.sharding import PartitionSpec as P


half_step = 0.1
lattice_step = 0.25
second_shell = 0.5

f32 = jnp.float32
bf16 = jnp.bfloat16
SUB, LANE = 8, 128
SLAB = 32
XL = 4
ORDER = (0, 2, 1, 3)
TILE = (SUB, LANE)


def iota(dim):
    return lax.broadcasted_iota(jnp.int32, TILE, dim)


def odd_mask(par):
    return ((iota(0) + iota(1) + par) & 1) == 1


def lane_block():
    return ((iota(1) + SLAB // 2) // SLAB) & 3


def lanes(v, shift):
    shift = shift % LANE
    return v if shift == 0 else pltpu.roll(v, shift, 1)


def rows(v, shift):
    return pltpu.roll(v, shift % SUB, 0)


def merge_blocks(tiles):
    block = lane_block()
    out = lanes(tiles[0], 0)
    for b in range(1, 4):
        out = jnp.where(block == b, lanes(tiles[b], SLAB * b), out)
    return out


def vmem_call(body, out_shapes, *args, scratch=(), name=None, cost=None):
    spec = pl.BlockSpec(memory_space=pltpu.VMEM)
    return pl.pallas_call(
        body,
        out_shape=tuple(jax.ShapeDtypeStruct(s, d) for s, d in out_shapes),
        in_specs=[spec] * len(args),
        out_specs=tuple(spec for _ in out_shapes),
        scratch_shapes=list(scratch),
        compiler_params=pltpu.CompilerParams(vmem_limit_bytes=24 << 20),
        name=name,
        cost_estimate=cost,
    )(*args)


def pack_body(disp, mom, bit, out):
    for i in range(14):
        if i < 6:
            tiles = [disp[i, x] for x in ORDER]
        elif i < 12:
            tiles = [mom[i - 6, x] for x in ORDER]
        else:
            tiles = [bit[i - 12, x].astype(f32) for x in ORDER]
        out[i] = merge_blocks(tiles)


def halo_body(disp, mom, bit, low, high, slab, brick, faces, yup, ydn):
    upper = (iota(1) & (SLAB - 1)) >= SLAB // 2
    e0 = odd_mask(0)
    for i in range(14):
        slab[i] = jnp.where(upper, low[i], high[i])
    for p in range(2):
        for k in range(4):
            i = 6 + 3 * p + k if k < 3 else 12 + p
            tiles = [mom[3 * p + k, x] if k < 3 else bit[p, x].astype(f32) for x in range(XL)]
            for xh in range(2):
                even, odd = tiles[2 * xh], tiles[2 * xh + 1]
                brick[xh, 4 * p + k] = jnp.where(e0, odd, even)
                brick[2 + xh, 4 * p + k] = jnp.where(e0, even, odd)
            h = slab[i]
            brick[4, 4 * p + k] = jnp.where(e0, lanes(h, 64), h)
    for i in range(6):
        src = disp if i < 3 else mom
        k = i % 3
        base = 0 if i < 3 else 6
        faces[0, 2 * i] = src[3 + k, XL - 1]
        faces[0, 2 * i + 1] = slab[base + 3 + k]
        faces[1, 2 * i] = src[k, 0]
        faces[1, 2 * i + 1] = slab[base + k]
        yup[i] = jnp.zeros(TILE, f32)
        ydn[i] = jnp.zeros(TILE, f32)
        for x in range(XL):
            yup[i, x : x + 1, :] = src[3 + k, x, SUB - 1 : SUB, :]
            ydn[i, x : x + 1, :] = src[k, x, 0:1, :]
        yup[i, XL : XL + 1, :] = slab[base + 3 + k, SUB - 1 : SUB, :]
        ydn[i, XL : XL + 1, :] = slab[base + k, 0:1, :]


def near_tiles(p, disp, mom, slab, xf, yr, xyr, near):
    q = 1 - p
    lane, sub = iota(1), iota(0)
    block = lane_block()
    edge_x = XL - 1 if p == 0 else 0
    for i in range(6):
        src = disp if i < 3 else mom
        k = i % 3
        c = [src[3 * q + k, x] for x in range(XL)]
        h = slab[(0 if i < 3 else 6) + 3 * q + k]
        fc, fh = xf[2 * i], xf[2 * i + 1]

        def wide(row):
            return jnp.broadcast_to(row, TILE)

        for dy in range(2):
            if dy:
                step = 1 if p == 0 else -1
                put = sub == (0 if p == 0 else SUB - 1)
                c = [jnp.where(put, wide(yr[i, x : x + 1, :]), rows(c[x], step)) for x in range(XL)]
                h = jnp.where(put, wide(yr[i, XL : XL + 1, :]), rows(h, step))
                fc = jnp.where(put, wide(xyr[i, edge_x : edge_x + 1, :]), rows(fc, step))
                fh = jnp.where(put, wide(xyr[i, XL : XL + 1, :]), rows(fh, step))
            for dz in range(2):
                if dz == 0:
                    cs, hs, fcs, fhs = c, h, fc, fh
                else:
                    step = 1 if p == 0 else -1
                    seam = LANE - 1 if p == 0 else 0
                    at_seam = lane == seam
                    at_seams = (lane & (SLAB - 1)) == (SLAB - 1 if p == 0 else 0)
                    cs = [
                        lanes(jnp.where(at_seam, lanes(h, -SLAB * ORDER[x]), c[x]), step)
                        for x in range(XL)
                    ]
                    hs = lanes(jnp.where(at_seams, merge_blocks([c[x] for x in ORDER]), h), step)
                    fcs = lanes(jnp.where(at_seam, lanes(fh, -SLAB * ORDER[edge_x]), fc), step)
                    fhs = lanes(jnp.where(at_seams, lanes(fc, SLAB * ORDER[edge_x]), fh), step)
                at = 2 * dy + dz
                line = [fcs] + cs if p == 0 else cs + [fcs]
                for j in range(XL + 1):
                    near[i, at, j] = line[j]
                near[i, at, XL + 1] = hs
                if p == 0:
                    moved = jnp.where(block == 0, lanes(fhs, SLAB), lanes(hs, 2 * SLAB))
                    moved = jnp.where(block == 1, lanes(hs, -SLAB), moved)
                else:
                    moved = jnp.where(block == 3, lanes(fhs, -SLAB), lanes(hs, 2 * SLAB))
                    moved = jnp.where(block == 2, lanes(hs, SLAB), moved)
                near[i, at, XL + 2] = moved


def feature_rows(p, disp, mom, slab, near, table):
    for slot in range(XL + 1):
        if slot < XL:
            own = [disp[3 * p + k, slot] for k in range(3)]
            own += [mom[3 * p + k, slot] for k in range(3)]
        else:
            own = [slab[3 * p + k] for k in range(3)] + [slab[6 + 3 * p + k] for k in range(3)]
        for o in range(8):
            dx, at = o >> 2, o & 3
            if slot == XL:
                j = XL + 1 + dx
            else:
                j = slot + 1 - dx if p == 0 else slot + dx
            for k in range(3):
                table[slot, pl.ds(4 * o + k, SUB, stride=32), :] = near[k, at, j] - own[k]
            dot = own[3] * near[3, at, j] + own[4] * near[4, at, j] + own[5] * near[5, at, j]
            table[slot, pl.ds(4 * o + 3, SUB, stride=32), :] = dot


def silu_half(u):
    return (u + u * jnp.tanh(u)).astype(bf16)


def perceptron(table, heads, w_in, b_in, w_mid, w_out, one, two, count):
    def step(slot, carry):
        source = jnp.minimum(slot, count - 1)
        before = jnp.where(slot == 0, count, slot - 1)
        for c in range(4):
            block = jnp.concatenate(
                [table[source, 32 * (2 * c + j) : 32 * (2 * c + j + 1), :] for j in range(2)], axis=1
            ).astype(bf16)
            bias = b_in[...]
            hidden, last = one[...], two[...]
            u = jnp.dot(w_in[...], block, preferred_element_type=f32)
            u = u + jnp.concatenate([bias, bias], axis=1)
            v = jnp.dot(w_mid[...], hidden, preferred_element_type=f32)
            out = jnp.dot(w_out[...], last, preferred_element_type=f32)
            one[...] = silu_half(u)
            two[...] = silu_half(v)
            done = 2 * c - 4 if c >= 2 else 2 * c + 4
            target = slot if c >= 2 else before
            for j in range(2):
                heads[target, pl.ds(done + j, SUB, stride=SUB), :] = out[:, LANE * j : LANE * (j + 1)]
        return carry

    one[...] = jnp.zeros(one.shape, bf16)
    two[...] = jnp.zeros(two.shape, bf16)
    lax.fori_loop(0, count + 1, step, 0)


def network_body(
    disp, mom, vel, slab, xup, xdn, yup, ydn, xyup, xydn, w_in, b_in, w_mid, w_out,
    disp_out, vel_out, cbrick, near, table, heads, one, two,
):
    e0 = odd_mask(0)
    slots = XL + 1
    for p in range(2):
        args = (xup.at[0], yup, xyup) if p == 0 else (xdn.at[xdn.shape[0] - 1], ydn, xydn)
        near_tiles(p, disp, mom, slab, *args, near)
        feature_rows(p, disp, mom, slab, near, table.at[pl.ds(slots * p, slots)])
    perceptron(table, heads, w_in, b_in, w_mid, w_out, one, two, 2 * slots)
    for p in range(2):
        coupling = []
        for slot in range(slots):
            at = slots * p + slot
            coupling.append(1.0 + 0.5 * jnp.tanh(heads[at, 3 * SUB : 4 * SUB, :]))
            if slot < XL:
                for k in range(3):
                    v = vel[3 * p + k, slot] + lattice_step * heads[at, k * SUB : (k + 1) * SUB, :]
                    vel_out[3 * p + k, slot] = v
                    disp_out[3 * p + k, slot] = disp[3 * p + k, slot] + lattice_step * v
        for xh in range(2):
            even, odd = coupling[2 * xh], coupling[2 * xh + 1]
            cbrick[xh, p] = jnp.where(e0, odd, even)
            cbrick[2 + xh, p] = jnp.where(e0, even, odd)
        cbrick[4, p] = jnp.where(e0, lanes(coupling[4], 64), coupling[4])


def even_fit(func, terms):
    edge = (np.pi / 2) ** 2 * 1.0001
    node = np.cos((np.arange(400) + 0.5) * np.pi / 400)
    w = 0.5 * edge * (1 + node)
    basis = np.stack([w**n for n in range(terms)], 1)
    return [float(c) for c in np.linalg.lstsq(basis, func(np.sqrt(w)), rcond=None)[0]]


ROOT = float(np.sqrt(2.0))
SIN = [ROOT * c * np.pi ** (2 * n + 1) for n, c in enumerate(even_fit(lambda r: np.sin(r) / r, 5))]
COS = [ROOT * c * np.pi ** (2 * n) for n, c in enumerate(even_fit(np.cos, 5))]


def horner(coeffs, w):
    out = float(coeffs[-1])
    for c in reversed(coeffs[:-1]):
        out = out * w + float(c)
    return out


def crossed(a, b):
    return (a[1] * b[2] - a[2] * b[1], a[2] * b[0] - a[0] * b[2], a[0] * b[1] - a[1] * b[0])


def rotated(s, b, half_turns, hit):
    square = b[0] * b[0] + b[1] * b[1] + b[2] * b[2]
    inverse = lax.rsqrt(jnp.maximum(square, 1e-30))
    angle = (square * inverse) * half_turns
    angle = angle - jnp.round(angle)
    w = angle * angle
    sine = jnp.where(hit, horner(SIN, w) * (angle * inverse), 0.0)
    cosine = horner(COS, w)
    axis = [sine * b[k] for k in range(3)]
    first = crossed(axis, s)
    second = crossed(axis, [cosine * s[k] + first[k] for k in range(3)])
    return [s[k] + second[k] for k in range(3)]


def turns_body(nx, ny, masks, *refs):
    count = len(masks)
    bricks, cbricks = refs[:count], refs[count : 2 * count]
    out = refs[2 * count]
    mc, mh, sc, sh, cc, ch, tc, th, nc, nh = refs[2 * count + 1 :]
    xh_all, groups = 2 * nx, nx // 2
    ix, iy = lax.axis_index("gx"), lax.axis_index("gy")
    lane = iota(1)
    block = lane_block()
    first_half = block < 2
    e0 = odd_mask(0)

    def row_mask(r, par):
        return ((lane + (r + par)) & 1) == 1

    def place(source, comps):
        for n, (mx, my) in enumerate(masks):
            bx, by = ix ^ mx, iy ^ my
            own_rows = pl.ds(pl.multiple_of(by * SUB, SUB), SUB)
            for k in range(comps):
                for par in range(2):
                    for xh in range(2):
                        sc[par, k, 2 * bx + xh, own_rows, :] = source[n][2 * par + xh, k]
                sh[k, bx, own_rows, :] = source[n][4, k]

    def spread(comps, put_c, put_h):
        for k in range(comps):
            for r in range(ny):
                part = pl.ds(r, SUB, stride=ny)
                for par in range(2):
                    for j in range(xh_all):
                        put_c(k, par, r, j, sc[par, k, j, part, :])
                for g in range(groups):
                    even, odd = sh[k, 2 * g, part, :], sh[k, 2 * g + 1, part, :]
                    put_h(k, 0, r, g, jnp.where(first_half, even, lanes(odd, 64)))
                    put_h(k, 1, r, g, jnp.where(first_half, lanes(even, 64), odd))

    def put_mc(k, par, r, j, v):
        mc[k // 4, par, k % 4, r, j] = v

    def put_mh(k, par, r, g, v):
        mh[k // 4, par, k % 4, r, g] = v

    def put_cc(k, par, r, j, v):
        cc[k, par, r, j] = v * (1.0 / second_shell)

    def put_ch(k, par, r, g, v):
        ch[k, par, r, g] = v * (1.0 / second_shell)

    def next_block(tiles, g):
        other = tiles[(g + 1) % groups]
        return lanes(jnp.where(block == 0, other, tiles[g]) if groups > 1 else tiles[g], -SLAB)

    def last_block(tiles, g):
        other = tiles[(g - 1) % groups]
        return lanes(jnp.where(block == 3, other, tiles[g]) if groups > 1 else tiles[g], SLAB)

    def seams(c, h):
        return (
            [lanes(h[x // 4], -SLAB * (x % 4)) for x in range(xh_all)],
            [merge_blocks(c[4 * g : 4 * g + 4]) for g in range(groups)],
        )

    def z_next(c, h, seam):
        cs = [lanes(jnp.where(lane == 0, seam[0][x], c[x]), -1) for x in range(xh_all)]
        at = (lane & (SLAB - 1)) == 0
        return cs, [lanes(jnp.where(at, seam[1][g], h[g]), -1) for g in range(groups)]

    def z_last(c, h, seam):
        cs = [lanes(jnp.where(lane == LANE - 1, seam[0][x], c[x]), 1) for x in range(xh_all)]
        at = (lane & (SLAB - 1)) == SLAB - 1
        return cs, [lanes(jnp.where(at, seam[1][g], h[g]), 1) for g in range(groups)]

    def y_next(ref, head, r, j):
        return rows(ref[*head, 0, j], -1) if r == ny - 1 else ref[*head, r + 1, j]

    def y_last(ref, head, r, j):
        return rows(ref[*head, ny - 1, j], 1) if r == 0 else ref[*head, r - 1, j]

    def near_total(p):
        q = 1 - p
        y_move = y_last if p == 0 else y_next
        z_move = z_last if p == 0 else z_next
        for k in range(3):
            for r in range(ny):
                e = row_mask(r, 0)
                for ref, to, size in ((mc, tc, xh_all), (mh, th, groups)):
                    zero = [ref[q, 0, k, r, j] for j in range(size)]
                    one = [ref[q, 1, k, r, j] for j in range(size)]
                    even = [jnp.where(e, one[j], zero[j]) for j in range(size)]
                    odd = [jnp.where(e, zero[j], one[j]) for j in range(size)]
                    for j in range(size):
                        to[0, r, j] = zero[j] + one[j]
                        if p == 0:
                            prev = odd[(j - 1) % size] if ref is mc else last_block(odd, j)
                            to[1, r, j] = even[j] + prev
                        else:
                            after = even[(j + 1) % size] if ref is mc else next_block(even, j)
                            to[1, r, j] = odd[j] + after
            for r in range(ny):
                e = row_mask(r, 0)
                got = []
                for t in range(2):
                    c = [tc[t, r, j] + y_move(tc, (t,), r, j) for j in range(xh_all)]
                    h = [th[t, r, j] + y_move(th, (t,), r, j) for j in range(groups)]
                    cs, hs = z_move(c, h, seams(c, h))
                    got.append(
                        ([c[j] + cs[j] for j in range(xh_all)], [h[j] + hs[j] for j in range(groups)])
                    )
                for kind, to, size in ((0, nc, xh_all), (1, nh, groups)):
                    for j in range(size):
                        whole, split = got[0][kind][j], got[1][kind][j]
                        if p == 1:
                            whole, split = split, whole
                        to[0, k, r, j] = jnp.where(e, whole, split)
                        to[1, k, r, j] = jnp.where(e, split, whole)

    def turn(p, par, bit, half_turns):
        opp = 1 - par
        for r in range(ny):
            e = row_mask(r, par)
            shell_c, shell_h = [], []
            for k in range(3):
                head = (p, opp, k)
                c = [mc[*head, r, j] for j in range(xh_all)]
                h = [mh[*head, r, g] for g in range(groups)]
                seam = seams(c, h)
                cn, hn = z_next(c, h, seam)
                cl, hl = z_last(c, h, seam)
                one, two = [], []
                for j in range(xh_all):
                    x = c[j] + jnp.where(e, c[(j + 1) % xh_all], c[(j - 1) % xh_all])
                    y = y_next(mc, head, r, j) + y_last(mc, head, r, j)
                    one.append(x + y + (cn[j] + cl[j]))
                for g in range(groups):
                    x = h[g] + jnp.where(e, next_block(h, g), last_block(h, g))
                    y = y_next(mh, head, r, g) + y_last(mh, head, r, g)
                    two.append(x + y + (hn[g] + hl[g]))
                shell_c.append(one)
                shell_h.append(two)
            for state, couple, near, shell, size in (
                (mc, cc, nc, shell_c, xh_all),
                (mh, ch, nh, shell_h, groups),
            ):
                for j in range(size):
                    cpl = couple[p, par, r, j]
                    field = [cpl * near[par, k, r, j] + shell[k][j] for k in range(3)]
                    own = [state[p, par, k, r, j] for k in range(3)]
                    new = rotated(own, field, half_turns, state[p, par, 3, r, j] == bit)
                    for k in range(3):
                        state[p, par, k, r, j] = new[k]

    unit = second_shell * half_step / (2.0 * np.pi)

    def sweep(p, sector, half_turns):
        turn(p, sector & 1, (sector >> 1).astype(f32), half_turns)

    def climb(i, carry):
        sweep(0, i, unit)
        return carry

    def middle(i, carry):
        sector = 3 - jnp.abs(3 - i)
        sweep(1, sector, jnp.where(i == 3, 2 * unit, unit).astype(f32))
        return carry

    def descend(i, carry):
        sweep(0, 3 - i, unit)
        return carry

    place(bricks, 8)
    spread(8, put_mc, put_mh)
    place(cbricks, 2)
    spread(2, put_cc, put_ch)
    near_total(0)
    lax.fori_loop(0, 4, climb, 0)
    near_total(1)
    lax.fori_loop(0, 7, middle, 0)
    near_total(0)
    lax.fori_loop(0, 4, descend, 0)

    for p in range(2):
        for k in range(3):
            for par in range(2):
                for xh in range(2):
                    for r in range(ny):
                        sc[par, k, xh, pl.ds(r, SUB, stride=ny), :] = mc[p, par, k, r, 2 * ix + xh]
            own_rows = pl.ds(pl.multiple_of(iy * SUB, SUB), SUB)
            for xh in range(2):
                zero, one = sc[0, k, xh, own_rows, :], sc[1, k, xh, own_rows, :]
                out[3 * p + k, 2 * xh] = jnp.where(e0, one, zero)
                out[3 * p + k, 2 * xh + 1] = jnp.where(e0, zero, one)


def on_device(nx, ny, nz, displacement, velocity, moments, sector_bit, weight_in, bias_in, weight_mid, weight_out):
    assert displacement.shape == (6, XL, SUB, LANE)
    assert nx % 2 == 0 and nx & (nx - 1) == 0 and ny & (ny - 1) == 0 and ny % 2 == 0
    plane = ("gx", "gy")

    def pairs(move):
        out = []
        for x in range(nx):
            for y in range(ny):
                tx, ty = move(x, y)
                out.append((x * ny + y, tx % nx * ny + ty % ny))
        return out

    def shift(v, dx, dy):
        return lax.ppermute(v, plane, pairs(lambda x, y: (x + dx, y + dy)))

    def swap(v, mx, my):
        return lax.ppermute(v, plane, pairs(lambda x, y: (x ^ mx, y ^ my)))

    def along_z(v, step):
        return lax.ppermute(v, "gz", [(i, (i + step) % nz) for i in range(nz)])

    w_in = (weight_in.T.astype(f32) * 0.5).astype(bf16)
    w_mid = (weight_mid.T.astype(f32) * 0.5).astype(bf16)
    w_out = jnp.pad(weight_out.T, ((0, SUB - 4), (0, 0)))
    hidden = weight_mid.shape[0]
    b_in = jnp.broadcast_to((0.5 * bias_in)[:, None], (hidden, LANE))

    (packed,) = vmem_call(
        pack_body, [((14, *TILE), f32)], displacement, moments, sector_bit, name="pack"
    )
    low, high = along_z(packed, 1), along_z(packed, -1)
    slab, brick, faces, yup, ydn = vmem_call(
        halo_body,
        [((14, *TILE), f32), ((5, 8, *TILE), f32)] + [((2, 12, *TILE), f32)] + [((6, *TILE), f32)] * 2,
        displacement, moments, sector_bit, low, high,
        name="halo",
    )
    if nx == 2:
        faces = shift(faces, 1, 0)
        xup, xdn = faces, faces
    else:
        xup, xdn = shift(faces[:1], 1, 0), shift(faces[1:], -1, 0)
    xyup, xydn = shift(yup, 1, 1), shift(ydn, -1, -1)
    yup, ydn = shift(yup, 0, 1), shift(ydn, 0, -1)

    far = [(mx, my) for mx in range(nx) for my in range(0, ny, 2) if mx or my]
    held = {(0, 0): brick}
    for n, mask in enumerate(far):
        with jax.named_scope(f"wide{n}"):
            held[mask] = swap(brick, *mask)

    disp_out, vel_out, cbrick = vmem_call(
        network_body,
        [((6, XL, *TILE), f32), ((6, XL, *TILE), f32), ((5, 2, *TILE), f32)],
        displacement, moments, velocity, slab, xup, xdn, yup, ydn, xyup, xydn, w_in, b_in, w_mid, w_out,
        scratch=[
            pltpu.VMEM((6, 4, XL + 3, *TILE), f32),
            pltpu.VMEM((2 * XL + 2, 32 * SUB, LANE), f32),
            pltpu.VMEM((2 * XL + 3, SUB * SUB, LANE), f32),
            pltpu.VMEM((hidden, 2 * LANE), bf16),
            pltpu.VMEM((hidden, 2 * LANE), bf16),
        ],
        name="network",
    )
    near_masks = [(0, 0)] + far
    late = lax.optimization_barrier((cbrick, *[held[m] for m in near_masks]))
    cbrick = late[0]
    held.update(zip(near_masks, late[1:]))
    cheld = {(0, 0): cbrick}
    for n, mask in enumerate(far):
        with jax.named_scope(f"field{n}"):
            cheld[mask] = swap(cbrick, *mask)
    for n, (mx, my) in enumerate(near_masks):
        with jax.named_scope(f"pair{n}"):
            held[mx, my + 1] = swap(held[mx, my], 0, 1)
    for mx, my in near_masks:
        cheld[mx, my + 1] = swap(cheld[mx, my], 0, 1)

    masks = sorted(held)
    xh_all, groups = 2 * nx, nx // 2
    (moments_out,) = vmem_call(
        functools.partial(turns_body, nx, ny, masks),
        [((6, XL, *TILE), f32)],
        *[held[m] for m in masks],
        *[cheld[m] for m in masks],
        scratch=[
            pltpu.VMEM((2, 2, 4, ny, xh_all, *TILE), f32),
            pltpu.VMEM((2, 2, 4, ny, groups, *TILE), f32),
            pltpu.VMEM((2, 8, xh_all, ny * SUB, LANE), f32),
            pltpu.VMEM((8, nx, ny * SUB, LANE), f32),
            pltpu.VMEM((2, 2, ny, xh_all, *TILE), f32),
            pltpu.VMEM((2, 2, ny, groups, *TILE), f32),
            pltpu.VMEM((2, ny, xh_all, *TILE), f32),
            pltpu.VMEM((2, ny, groups, *TILE), f32),
            pltpu.VMEM((2, 3, ny, xh_all, *TILE), f32),
            pltpu.VMEM((2, 3, ny, groups, *TILE), f32),
        ],
        name="turns",
    )
    return disp_out, vel_out, moments_out


def solution(mesh):
    placed = P(None, "gx", "gy", "gz")
    sizes = [mesh.shape[axis] for axis in ("gx", "gy", "gz")]
    return jax.shard_map(
        functools.partial(on_device, *sizes),
        mesh=mesh,
        in_specs=(placed,) * 4 + (P(),) * 4,
        out_specs=(placed,) * 3,
        check_vma=False,
    )
```

```python
import functools

import jax
import jax.numpy as jnp
import numpy as np
from jax import lax
from jax.experimental import pallas as pl
from jax.experimental.pallas import tpu as pltpu
from jax.sharding import PartitionSpec as P


half_step = 0.1
lattice_step = 0.25
second_shell = 0.5

f32 = jnp.float32
bf16 = jnp.bfloat16
SUB, LANE = 8, 128
SLAB = 32
XL = 4
ORDER = (0, 2, 1, 3)
TILE = (SUB, LANE)


def iota(dim):
    return lax.broadcasted_iota(jnp.int32, TILE, dim)


def odd_mask(par):
    return ((iota(0) + iota(1) + par) & 1) == 1


def lane_block():
    return ((iota(1) + SLAB // 2) // SLAB) & 3


def lanes(v, shift):
    shift = shift % LANE
    return v if shift == 0 else pltpu.roll(v, shift, 1)


def rows(v, shift):
    return pltpu.roll(v, shift % SUB, 0)


def merge_blocks(tiles):
    block = lane_block()
    out = lanes(tiles[0], 0)
    for b in range(1, 4):
        out = jnp.where(block == b, lanes(tiles[b], SLAB * b), out)
    return out


def vmem_call(body, out_shapes, *args, scratch=(), cost=None, space=None, grant=24 << 20):
    spec = pl.BlockSpec(memory_space=pltpu.VMEM)
    given = pl.BlockSpec(memory_space=space or pltpu.VMEM)
    return pl.pallas_call(
        body,
        out_shape=tuple(jax.ShapeDtypeStruct(s, d) for s, d in out_shapes),
        in_specs=[given] * len(args),
        out_specs=tuple(spec for _ in out_shapes),
        scratch_shapes=list(scratch),
        compiler_params=pltpu.CompilerParams(vmem_limit_bytes=grant),
        cost_estimate=cost,
    )(*args)


def pack_body(disp_in, mom_in, bit_in, out, disp, mom, bit, sems):
    copies = [
        pltpu.make_async_copy(source, target, sems.at[n])
        for n, (source, target) in enumerate(((disp_in, disp), (mom_in, mom), (bit_in, bit)))
    ]
    for copy in copies:
        copy.start()
    for copy in copies:
        copy.wait()
    for i in range(14):
        if i < 6:
            tiles = [disp[i, x] for x in ORDER]
        elif i < 12:
            tiles = [mom[i - 6, x] for x in ORDER]
        else:
            tiles = [bit[i - 12, x].astype(f32) for x in ORDER]
        out[i] = merge_blocks(tiles)


def halo_body(disp, mom, bit, low, high, slab, brick, faces, yup, ydn):
    upper = (iota(1) & (SLAB - 1)) >= SLAB // 2
    e0 = odd_mask(0)
    for i in range(14):
        slab[i] = jnp.where(upper, low[i], high[i])
    for p in range(2):
        for k in range(4):
            i = 6 + 3 * p + k if k < 3 else 12 + p
            tiles = [mom[3 * p + k, x] if k < 3 else bit[p, x].astype(f32) for x in range(XL)]
            for xh in range(2):
                even, odd = tiles[2 * xh], tiles[2 * xh + 1]
                brick[xh, 4 * p + k] = jnp.where(e0, odd, even)
                brick[2 + xh, 4 * p + k] = jnp.where(e0, even, odd)
            h = slab[i]
            brick[4, 4 * p + k] = jnp.where(e0, lanes(h, 64), h)
    for i in range(6):
        src = disp if i < 3 else mom
        k = i % 3
        base = 0 if i < 3 else 6
        faces[0, 2 * i] = src[3 + k, XL - 1]
        faces[0, 2 * i + 1] = slab[base + 3 + k]
        faces[1, 2 * i] = src[k, 0]
        faces[1, 2 * i + 1] = slab[base + k]
        yup[i] = jnp.zeros(TILE, f32)
        ydn[i] = jnp.zeros(TILE, f32)
        for x in range(XL):
            yup[i, x : x + 1, :] = src[3 + k, x, SUB - 1 : SUB, :]
            ydn[i, x : x + 1, :] = src[k, x, 0:1, :]
        yup[i, XL : XL + 1, :] = slab[base + 3 + k, SUB - 1 : SUB, :]
        ydn[i, XL : XL + 1, :] = slab[base + k, 0:1, :]


def near_tiles(p, disp, mom, slab, xf, yr, xyr, near):
    q = 1 - p
    lane, sub = iota(1), iota(0)
    block = lane_block()
    edge_x = XL - 1 if p == 0 else 0
    for i in range(6):
        src = disp if i < 3 else mom
        k = i % 3
        c = [src[3 * q + k, x] for x in range(XL)]
        h = slab[(0 if i < 3 else 6) + 3 * q + k]
        fc, fh = xf[2 * i], xf[2 * i + 1]

        def wide(row):
            return jnp.broadcast_to(row, TILE)

        for dy in range(2):
            if dy:
                step = 1 if p == 0 else -1
                put = sub == (0 if p == 0 else SUB - 1)
                c = [jnp.where(put, wide(yr[i, x : x + 1, :]), rows(c[x], step)) for x in range(XL)]
                h = jnp.where(put, wide(yr[i, XL : XL + 1, :]), rows(h, step))
                fc = jnp.where(put, wide(xyr[i, edge_x : edge_x + 1, :]), rows(fc, step))
                fh = jnp.where(put, wide(xyr[i, XL : XL + 1, :]), rows(fh, step))
            for dz in range(2):
                if dz == 0:
                    cs, hs, fcs, fhs = c, h, fc, fh
                else:
                    step = 1 if p == 0 else -1
                    seam = LANE - 1 if p == 0 else 0
                    at_seam = lane == seam
                    at_seams = (lane & (SLAB - 1)) == (SLAB - 1 if p == 0 else 0)
                    cs = [
                        lanes(jnp.where(at_seam, lanes(h, -SLAB * ORDER[x]), c[x]), step)
                        for x in range(XL)
                    ]
                    hs = lanes(jnp.where(at_seams, merge_blocks([c[x] for x in ORDER]), h), step)
                    fcs = lanes(jnp.where(at_seam, lanes(fh, -SLAB * ORDER[edge_x]), fc), step)
                    fhs = lanes(jnp.where(at_seams, lanes(fc, SLAB * ORDER[edge_x]), fh), step)
                at = 2 * dy + dz
                line = [fcs] + cs if p == 0 else cs + [fcs]
                for j in range(XL + 1):
                    near[i, at, j] = line[j]
                near[i, at, XL + 1] = hs
                if p == 0:
                    moved = jnp.where(block == 0, lanes(fhs, SLAB), lanes(hs, 2 * SLAB))
                    moved = jnp.where(block == 1, lanes(hs, -SLAB), moved)
                else:
                    moved = jnp.where(block == 3, lanes(fhs, -SLAB), lanes(hs, 2 * SLAB))
                    moved = jnp.where(block == 2, lanes(hs, SLAB), moved)
                near[i, at, XL + 2] = moved


def feature_rows(p, disp, mom, slab, near, table):
    for slot in range(XL + 1):
        if slot < XL:
            own = [disp[3 * p + k, slot] for k in range(3)]
            own += [mom[3 * p + k, slot] for k in range(3)]
        else:
            own = [slab[3 * p + k] for k in range(3)] + [slab[6 + 3 * p + k] for k in range(3)]
        for o in range(8):
            dx, at = o >> 2, o & 3
            if slot == XL:
                j = XL + 1 + dx
            else:
                j = slot + 1 - dx if p == 0 else slot + dx
            for k in range(3):
                table[slot, SUB * (4 * o + k) : SUB * (4 * o + k + 1), :] = near[k, at, j] - own[k]
            dot = own[3] * near[3, at, j] + own[4] * near[4, at, j] + own[5] * near[5, at, j]
            table[slot, SUB * (4 * o + 3) : SUB * (4 * o + 4), :] = dot


def silu_half(u):
    return (u + u * jnp.tanh(u)).astype(bf16)


def perceptron(table, heads, w_in, b_in, w_mid, w_out, one, two, count):
    def step(slot, carry):
        source = jnp.minimum(slot, count - 1)
        before = jnp.where(slot == 0, count, slot - 1)
        for c in range(4):
            block = jnp.concatenate(
                [
                    jnp.concatenate(
                        [
                            table[source, pl.ds(SUB * SUB * m + 2 * c + j, SUB, stride=SUB), :]
                            for m in range(4)
                        ],
                        axis=0,
                    )
                    for j in range(2)
                ],
                axis=1,
            ).astype(bf16)
            bias = b_in[...]
            hidden, last = one[...], two[...]
            u = jnp.dot(w_in[...], block, preferred_element_type=f32)
            u = u + jnp.concatenate([bias, bias], axis=1)
            v = jnp.dot(w_mid[...], hidden, preferred_element_type=f32)
            out = jnp.dot(w_out[...], last, preferred_element_type=f32)
            one[...] = silu_half(u)
            two[...] = silu_half(v)
            done = 2 * c - 4 if c >= 2 else 2 * c + 4
            target = slot if c >= 2 else before
            for j in range(2):
                heads[target, pl.ds(done + j, SUB, stride=SUB), :] = out[:, LANE * j : LANE * (j + 1)]
        return carry

    one[...] = jnp.zeros(one.shape, bf16)
    two[...] = jnp.zeros(two.shape, bf16)
    lax.fori_loop(0, count + 1, step, 0)


def network_body(
    disp, mom, vel, slab, xup, xdn, yup, ydn, xyup, xydn, w_in, b_in, w_mid, w_out,
    disp_out, vel_out, cbrick, near, table, heads, one, two,
):
    e0 = odd_mask(0)
    slots = XL + 1
    for p in range(2):
        args = (xup.at[0], yup, xyup) if p == 0 else (xdn.at[xdn.shape[0] - 1], ydn, xydn)
        near_tiles(p, disp, mom, slab, *args, near)
        feature_rows(p, disp, mom, slab, near, table.at[pl.ds(slots * p, slots)])
    perceptron(table, heads, w_in, b_in, w_mid, w_out, one, two, 2 * slots)
    for p in range(2):
        coupling = []
        for slot in range(slots):
            at = slots * p + slot
            coupling.append(1.0 + 0.5 * jnp.tanh(heads[at, 3 * SUB : 4 * SUB, :]))
            if slot < XL:
                for k in range(3):
                    v = vel[3 * p + k, slot] + lattice_step * heads[at, k * SUB : (k + 1) * SUB, :]
                    vel_out[3 * p + k, slot] = v
                    disp_out[3 * p + k, slot] = disp[3 * p + k, slot] + lattice_step * v
        for xh in range(2):
            even, odd = coupling[2 * xh], coupling[2 * xh + 1]
            cbrick[xh, p] = jnp.where(e0, odd, even)
            cbrick[2 + xh, p] = jnp.where(e0, even, odd)
        cbrick[4, p] = jnp.where(e0, lanes(coupling[4], 64), coupling[4])


def even_fit(func, terms):
    edge = (np.pi / 2) ** 2 * 1.0001
    node = np.cos((np.arange(400) + 0.5) * np.pi / 400)
    w = 0.5 * edge * (1 + node)
    basis = np.stack([w**n for n in range(terms)], 1)
    return [float(c) for c in np.linalg.lstsq(basis, func(np.sqrt(w)), rcond=None)[0]]


ROOT = float(np.sqrt(2.0))
SIN = [ROOT * c * np.pi ** (2 * n + 1) for n, c in enumerate(even_fit(lambda r: np.sin(r) / r, 5))]
COS = [ROOT * c * np.pi ** (2 * n) for n, c in enumerate(even_fit(np.cos, 5))]


def horner(coeffs, w):
    out = float(coeffs[-1])
    for c in reversed(coeffs[:-1]):
        out = out * w + float(c)
    return out


def crossed(a, b):
    return (a[1] * b[2] - a[2] * b[1], a[2] * b[0] - a[0] * b[2], a[0] * b[1] - a[1] * b[0])


def rotated(s, b, half_turns, hit):
    square = b[0] * b[0] + b[1] * b[1] + b[2] * b[2]
    inverse = lax.rsqrt(jnp.maximum(square, 1e-30))
    angle = (square * inverse) * half_turns
    angle = angle - jnp.round(angle)
    w = angle * angle
    sine = jnp.where(hit, horner(SIN, w) * (angle * inverse), 0.0)
    cosine = horner(COS, w)
    axis = [sine * b[k] for k in range(3)]
    first = crossed(axis, s)
    second = crossed(axis, [cosine * s[k] + first[k] for k in range(3)])
    return [s[k] + second[k] for k in range(3)]


def turns_body(nx, ny, masks, *refs):
    count = len(masks)
    bricks, cbricks = refs[:count], refs[count : 2 * count]
    out = refs[2 * count]
    mc, mh, sc, sh, cc, ch, tc, th, nc, nh = refs[2 * count + 1 :]
    xh_all, groups = 2 * nx, nx // 2
    ix, iy = lax.axis_index("gx"), lax.axis_index("gy")
    lane = iota(1)
    block = lane_block()
    first_half = block < 2
    e0 = odd_mask(0)

    def row_mask(r, par):
        return ((lane + (r + par)) & 1) == 1

    def place(source, comps):
        for n, (mx, my) in enumerate(masks):
            bx, by = ix ^ mx, iy ^ my
            own_rows = pl.ds(pl.multiple_of(by * SUB, SUB), SUB)
            for k in range(comps):
                for par in range(2):
                    for xh in range(2):
                        sc[par, k, 2 * bx + xh, own_rows, :] = source[n][2 * par + xh, k]
                sh[k, bx, own_rows, :] = source[n][4, k]

    def spread(comps, put_c, put_h):
        for k in range(comps):
            for r in range(ny):
                part = pl.ds(r, SUB, stride=ny)
                for par in range(2):
                    for j in range(xh_all):
                        put_c(k, par, r, j, sc[par, k, j, part, :])
                for g in range(groups):
                    even, odd = sh[k, 2 * g, part, :], sh[k, 2 * g + 1, part, :]
                    put_h(k, 0, r, g, jnp.where(first_half, even, lanes(odd, 64)))
                    put_h(k, 1, r, g, jnp.where(first_half, lanes(even, 64), odd))

    def put_mc(k, par, r, j, v):
        mc[k // 4, par, k % 4, r, j] = v

    def put_mh(k, par, r, g, v):
        mh[k // 4, par, k % 4, r, g] = v

    def put_cc(k, par, r, j, v):
        cc[k, par, r, j] = v * (1.0 / second_shell)

    def put_ch(k, par, r, g, v):
        ch[k, par, r, g] = v * (1.0 / second_shell)

    def next_block(tiles, g):
        other = tiles[(g + 1) % groups]
        return lanes(jnp.where(block == 0, other, tiles[g]) if groups > 1 else tiles[g], -SLAB)

    def last_block(tiles, g):
        other = tiles[(g - 1) % groups]
        return lanes(jnp.where(block == 3, other, tiles[g]) if groups > 1 else tiles[g], SLAB)

    def seams(c, h):
        return (
            [lanes(h[x // 4], -SLAB * (x % 4)) for x in range(xh_all)],
            [merge_blocks(c[4 * g : 4 * g + 4]) for g in range(groups)],
        )

    def z_next(c, h, seam):
        cs = [lanes(jnp.where(lane == 0, seam[0][x], c[x]), -1) for x in range(xh_all)]
        at = (lane & (SLAB - 1)) == 0
        return cs, [lanes(jnp.where(at, seam[1][g], h[g]), -1) for g in range(groups)]

    def z_last(c, h, seam):
        cs = [lanes(jnp.where(lane == LANE - 1, seam[0][x], c[x]), 1) for x in range(xh_all)]
        at = (lane & (SLAB - 1)) == SLAB - 1
        return cs, [lanes(jnp.where(at, seam[1][g], h[g]), 1) for g in range(groups)]

    def y_next(ref, head, r, j):
        return rows(ref[*head, 0, j], -1) if r == ny - 1 else ref[*head, r + 1, j]

    def y_last(ref, head, r, j):
        return rows(ref[*head, ny - 1, j], 1) if r == 0 else ref[*head, r - 1, j]

    def near_total(p):
        q = 1 - p
        y_move = y_last if p == 0 else y_next
        z_move = z_last if p == 0 else z_next
        for k in range(3):
            for r in range(ny):
                e = row_mask(r, 0)
                for ref, to, size in ((mc, tc, xh_all), (mh, th, groups)):
                    zero = [ref[q, 0, k, r, j] for j in range(size)]
                    one = [ref[q, 1, k, r, j] for j in range(size)]
                    even = [jnp.where(e, one[j], zero[j]) for j in range(size)]
                    odd = [jnp.where(e, zero[j], one[j]) for j in range(size)]
                    for j in range(size):
                        to[k, 0, r, j] = zero[j] + one[j]
                        if p == 0:
                            prev = odd[(j - 1) % size] if ref is mc else last_block(odd, j)
                            to[k, 1, r, j] = even[j] + prev
                        else:
                            after = even[(j + 1) % size] if ref is mc else next_block(even, j)
                            to[k, 1, r, j] = odd[j] + after
            for r in range(ny):
                e = row_mask(r, 0)
                got = []
                for t in range(2):
                    c = [tc[k, t, r, j] + y_move(tc, (k, t), r, j) for j in range(xh_all)]
                    h = [th[k, t, r, j] + y_move(th, (k, t), r, j) for j in range(groups)]
                    cs, hs = z_move(c, h, seams(c, h))
                    got.append(
                        ([c[j] + cs[j] for j in range(xh_all)], [h[j] + hs[j] for j in range(groups)])
                    )
                for kind, to, size in ((0, nc, xh_all), (1, nh, groups)):
                    for j in range(size):
                        whole, split = got[0][kind][j], got[1][kind][j]
                        if p == 1:
                            whole, split = split, whole
                        to[0, k, r, j] = jnp.where(e, whole, split)
                        to[1, k, r, j] = jnp.where(e, split, whole)

    def turn(p, par, bit, half_turns):
        opp = 1 - par
        for r in range(ny):
            e = row_mask(r, par)
            shell_c, shell_h = [], []
            for k in range(3):
                head = (p, opp, k)
                c = [mc[*head, r, j] for j in range(xh_all)]
                h = [mh[*head, r, g] for g in range(groups)]
                seam = seams(c, h)
                cn, hn = z_next(c, h, seam)
                cl, hl = z_last(c, h, seam)
                one, two = [], []
                for j in range(xh_all):
                    x = c[j] + jnp.where(e, c[(j + 1) % xh_all], c[(j - 1) % xh_all])
                    y = y_next(mc, head, r, j) + y_last(mc, head, r, j)
                    one.append(x + y + (cn[j] + cl[j]))
                for g in range(groups):
                    x = h[g] + jnp.where(e, next_block(h, g), last_block(h, g))
                    y = y_next(mh, head, r, g) + y_last(mh, head, r, g)
                    two.append(x + y + (hn[g] + hl[g]))
                shell_c.append(one)
                shell_h.append(two)
            for state, couple, near, shell, size in (
                (mc, cc, nc, shell_c, xh_all),
                (mh, ch, nh, shell_h, groups),
            ):
                for j in range(size):
                    cpl = couple[p, par, r, j]
                    field = [cpl * near[par, k, r, j] + shell[k][j] for k in range(3)]
                    own = [state[p, par, k, r, j] for k in range(3)]
                    new = rotated(own, field, half_turns, state[p, par, 3, r, j] == bit)
                    for k in range(3):
                        state[p, par, k, r, j] = new[k]

    unit = second_shell * half_step / (2.0 * np.pi)

    def sweep(p, sector, half_turns):
        turn(p, sector & 1, (sector >> 1).astype(f32), half_turns)

    def climb(i, carry):
        sweep(0, i, unit)
        return carry

    def middle(i, carry):
        sector = 3 - jnp.abs(3 - i)
        sweep(1, sector, jnp.where(i == 3, 2 * unit, unit).astype(f32))
        return carry

    def descend(i, carry):
        sweep(0, 3 - i, unit)
        return carry

    place(bricks, 8)
    spread(8, put_mc, put_mh)
    place(cbricks, 2)
    spread(2, put_cc, put_ch)
    near_total(0)
    lax.fori_loop(0, 4, climb, 0)
    near_total(1)
    lax.fori_loop(0, 7, middle, 0)
    near_total(0)
    lax.fori_loop(0, 4, descend, 0)

    for p in range(2):
        for k in range(3):
            for par in range(2):
                for xh in range(2):
                    for r in range(ny):
                        sc[par, k, xh, pl.ds(r, SUB, stride=ny), :] = mc[p, par, k, r, 2 * ix + xh]
            own_rows = pl.ds(pl.multiple_of(iy * SUB, SUB), SUB)
            for xh in range(2):
                zero, one = sc[0, k, xh, own_rows, :], sc[1, k, xh, own_rows, :]
                out[3 * p + k, 2 * xh] = jnp.where(e0, one, zero)
                out[3 * p + k, 2 * xh + 1] = jnp.where(e0, zero, one)


def on_device(nx, ny, nz, displacement, velocity, moments, sector_bit, weight_in, bias_in, weight_mid, weight_out):
    assert displacement.shape == (6, XL, SUB, LANE)
    assert nx % 2 == 0 and nx & (nx - 1) == 0 and ny & (ny - 1) == 0 and ny % 2 == 0
    plane = ("gx", "gy")

    def pairs(move):
        out = []
        for x in range(nx):
            for y in range(ny):
                tx, ty = move(x, y)
                out.append((x * ny + y, tx % nx * ny + ty % ny))
        return out

    def shift(v, dx, dy):
        return lax.ppermute(v, plane, pairs(lambda x, y: (x + dx, y + dy)))

    def swap(v, mx, my):
        return lax.ppermute(v, plane, pairs(lambda x, y: (x ^ mx, y ^ my)))

    def along_z(v, step):
        return lax.ppermute(v, "gz", [(i, (i + step) % nz) for i in range(nz)])

    w_in = (weight_in.T.astype(f32) * 0.5).astype(bf16)
    w_mid = (weight_mid.T.astype(f32) * 0.5).astype(bf16)
    w_out = jnp.pad(weight_out.T, ((0, SUB - 4), (0, 0)))
    hidden = weight_mid.shape[0]
    b_in = jnp.broadcast_to((0.5 * bias_in)[:, None], (hidden, LANE))

    (packed,) = vmem_call(
        pack_body, [((14, *TILE), f32)], displacement, moments, sector_bit,
        space=pltpu.HBM,
        grant=60 << 20,
        scratch=[
            pltpu.VMEM(displacement.shape, f32),
            pltpu.VMEM(moments.shape, f32),
            pltpu.VMEM(sector_bit.shape, sector_bit.dtype),
            pltpu.SemaphoreType.DMA((3,)),
        ],
    )
    low, high = along_z(packed, 1), along_z(packed, -1)
    slab, brick, faces, yup, ydn = vmem_call(
        halo_body,
        [((14, *TILE), f32), ((5, 8, *TILE), f32)] + [((2, 12, *TILE), f32)] + [((6, *TILE), f32)] * 2,
        displacement, moments, sector_bit, low, high,
    )
    if nx == 2:
        faces = shift(faces, 1, 0)
        xup, xdn = faces, faces
    else:
        xup, xdn = shift(faces[:1], 1, 0), shift(faces[1:], -1, 0)
    xyup, xydn = shift(yup, 1, 1), shift(ydn, -1, -1)
    yup, ydn = shift(yup, 0, 1), shift(ydn, 0, -1)

    far = [(mx, my) for mx in range(nx) for my in range(0, ny, 2) if mx or my]
    held = {(0, 0): brick}
    for mask in far:
        held[mask] = swap(brick, *mask)

    disp_out, vel_out, cbrick = vmem_call(
        network_body,
        [((6, XL, *TILE), f32), ((6, XL, *TILE), f32), ((5, 2, *TILE), f32)],
        displacement, moments, velocity, slab, xup, xdn, yup, ydn, xyup, xydn, w_in, b_in, w_mid, w_out,
        scratch=[
            pltpu.VMEM((6, 4, XL + 3, *TILE), f32),
            pltpu.VMEM((2 * XL + 2, 32 * SUB, LANE), f32),
            pltpu.VMEM((2 * XL + 3, SUB * SUB, LANE), f32),
            pltpu.VMEM((hidden, 2 * LANE), bf16),
            pltpu.VMEM((hidden, 2 * LANE), bf16),
        ],
    )
    near_masks = [(0, 0)] + far
    late = lax.optimization_barrier((cbrick, *[held[m] for m in near_masks]))
    cbrick = late[0]
    held.update(zip(near_masks, late[1:]))
    cheld = {(0, 0): cbrick}
    for mask in far:
        cheld[mask] = swap(cbrick, *mask)
    for mx, my in near_masks:
        held[mx, my + 1] = swap(held[mx, my], 0, 1)
    for mx, my in near_masks:
        cheld[mx, my + 1] = swap(cheld[mx, my], 0, 1)

    masks = sorted(held)
    xh_all, groups = 2 * nx, nx // 2
    (moments_out,) = vmem_call(
        functools.partial(turns_body, nx, ny, masks),
        [((6, XL, *TILE), f32)],
        *[held[m] for m in masks],
        *[cheld[m] for m in masks],
        scratch=[
            pltpu.VMEM((2, 2, 4, ny, xh_all, *TILE), f32),
            pltpu.VMEM((2, 2, 4, ny, groups, *TILE), f32),
            pltpu.VMEM((2, 8, xh_all, ny * SUB, LANE), f32),
            pltpu.VMEM((8, nx, ny * SUB, LANE), f32),
            pltpu.VMEM((2, 2, ny, xh_all, *TILE), f32),
            pltpu.VMEM((2, 2, ny, groups, *TILE), f32),
            pltpu.VMEM((3, 2, ny, xh_all, *TILE), f32),
            pltpu.VMEM((3, 2, ny, groups, *TILE), f32),
            pltpu.VMEM((2, 3, ny, xh_all, *TILE), f32),
            pltpu.VMEM((2, 3, ny, groups, *TILE), f32),
        ],
    )
    return disp_out, vel_out, moments_out


def solution(mesh):
    placed = P(None, "gx", "gy", "gz")
    sizes = [mesh.shape[axis] for axis in ("gx", "gy", "gz")]
    return jax.shard_map(
        functools.partial(on_device, *sizes),
        mesh=mesh,
        in_specs=(placed,) * 4 + (P(),) * 4,
        out_specs=(placed,) * 3,
        check_vma=False,
    )
```

```python
import functools

import jax
import jax.numpy as jnp
import numpy as np
from jax import lax
from jax.experimental import pallas as pl
from jax.experimental.pallas import tpu as pltpu
from jax.sharding import PartitionSpec as P


half_step = 0.1
lattice_step = 0.25
second_shell = 0.5

f32 = jnp.float32
bf16 = jnp.bfloat16
SUB, LANE = 8, 128
SLAB = 32
XL = 4
ORDER = (0, 2, 1, 3)
TILE = (SUB, LANE)


def iota(dim):
    return lax.broadcasted_iota(jnp.int32, TILE, dim)


def odd_mask(par):
    return ((iota(0) + iota(1) + par) & 1) == 1


def lane_block():
    return ((iota(1) + SLAB // 2) // SLAB) & 3


def lanes(v, shift):
    shift = shift % LANE
    return v if shift == 0 else pltpu.roll(v, shift, 1)


def rows(v, shift):
    return pltpu.roll(v, shift % SUB, 0)


def merge_blocks(tiles):
    block = lane_block()
    out = lanes(tiles[0], 0)
    for b in range(1, 4):
        out = jnp.where(block == b, lanes(tiles[b], SLAB * b), out)
    return out


def vmem_call(body, out_shapes, *args, scratch=(), cost=None, space=None, grant=24 << 20):
    spec = pl.BlockSpec(memory_space=pltpu.VMEM)
    given = pl.BlockSpec(memory_space=space or pltpu.VMEM)
    return pl.pallas_call(
        body,
        out_shape=tuple(jax.ShapeDtypeStruct(s, d) for s, d in out_shapes),
        in_specs=[given] * len(args),
        out_specs=tuple(spec for _ in out_shapes),
        scratch_shapes=list(scratch),
        compiler_params=pltpu.CompilerParams(vmem_limit_bytes=grant),
        cost_estimate=cost,
    )(*args)


def pack_body(disp_in, mom_in, bit_in, out, brick, disp, mom, bit, sems):
    copies = [
        pltpu.make_async_copy(source, target, sems.at[n])
        for n, (source, target) in enumerate(((disp_in, disp), (mom_in, mom), (bit_in, bit)))
    ]
    for copy in copies:
        copy.start()
    for copy in copies:
        copy.wait()
    for i in range(14):
        if i < 6:
            tiles = [disp[i, x] for x in ORDER]
        elif i < 12:
            tiles = [mom[i - 6, x] for x in ORDER]
        else:
            tiles = [bit[i - 12, x].astype(f32) for x in ORDER]
        out[i] = merge_blocks(tiles)
    e0 = odd_mask(0)
    for p in range(2):
        for k in range(4):
            tiles = [mom[3 * p + k, x] if k < 3 else bit[p, x].astype(f32) for x in range(XL)]
            for xh in range(2):
                even, odd = tiles[2 * xh], tiles[2 * xh + 1]
                brick[xh, 4 * p + k] = jnp.where(e0, odd, even)
                brick[2 + xh, 4 * p + k] = jnp.where(e0, even, odd)


def halo_body(disp, mom, low, high, slab, faces, yup, ydn):
    upper = (iota(1) & (SLAB - 1)) >= SLAB // 2
    for i in range(14):
        slab[i] = jnp.where(upper, low[i], high[i])
    for i in range(6):
        src = disp if i < 3 else mom
        k = i % 3
        base = 0 if i < 3 else 6
        faces[0, 2 * i] = src[3 + k, XL - 1]
        faces[0, 2 * i + 1] = slab[base + 3 + k]
        faces[1, 2 * i] = src[k, 0]
        faces[1, 2 * i + 1] = slab[base + k]
        yup[i] = jnp.zeros(TILE, f32)
        ydn[i] = jnp.zeros(TILE, f32)
        for x in range(XL):
            yup[i, x : x + 1, :] = src[3 + k, x, SUB - 1 : SUB, :]
            ydn[i, x : x + 1, :] = src[k, x, 0:1, :]
        yup[i, XL : XL + 1, :] = slab[base + 3 + k, SUB - 1 : SUB, :]
        ydn[i, XL : XL + 1, :] = slab[base + k, 0:1, :]


def near_tiles(p, disp, mom, slab, halo, near):
    xf, yr, xyr = halo or (None, None, None)
    q = 1 - p
    lane, sub = iota(1), iota(0)
    block = lane_block()
    edge_x = XL - 1 if p == 0 else 0
    for i in range(6):
        src = disp if i < 3 else mom
        k = i % 3
        c = [src[3 * q + k, x] for x in range(XL)]
        h = slab[(0 if i < 3 else 6) + 3 * q + k]
        fc, fh = (xf[2 * i], xf[2 * i + 1]) if halo else (None, None)

        def wide(row):
            return jnp.broadcast_to(row, TILE)

        for dy in range(2):
            if dy:
                step = 1 if p == 0 else -1
                put = sub == (0 if p == 0 else SUB - 1)
                c = [rows(c[x], step) for x in range(XL)]
                h = rows(h, step)
                if halo:
                    c = [jnp.where(put, wide(yr[i, x : x + 1, :]), c[x]) for x in range(XL)]
                    h = jnp.where(put, wide(yr[i, XL : XL + 1, :]), h)
                    fc = jnp.where(put, wide(xyr[i, edge_x : edge_x + 1, :]), rows(fc, step))
                    fh = jnp.where(put, wide(xyr[i, XL : XL + 1, :]), rows(fh, step))
            for dz in range(2):
                if dz == 0:
                    cs, hs, fcs, fhs = c, h, fc, fh
                else:
                    step = 1 if p == 0 else -1
                    seam = LANE - 1 if p == 0 else 0
                    at_seam = lane == seam
                    at_seams = (lane & (SLAB - 1)) == (SLAB - 1 if p == 0 else 0)
                    cs = [
                        lanes(jnp.where(at_seam, lanes(h, -SLAB * ORDER[x]), c[x]), step)
                        for x in range(XL)
                    ]
                    if halo:
                        hs = lanes(jnp.where(at_seams, merge_blocks([c[x] for x in ORDER]), h), step)
                        fcs = lanes(jnp.where(at_seam, lanes(fh, -SLAB * ORDER[edge_x]), fc), step)
                        fhs = lanes(jnp.where(at_seams, lanes(fc, SLAB * ORDER[edge_x]), fh), step)
                at = 2 * dy + dz
                for x in range(XL):
                    near[i, at, x + 1 - p] = cs[x]
                if not halo:
                    continue
                near[i, at, XL * p] = fcs
                near[i, at, XL + 1] = hs
                if p == 0:
                    moved = jnp.where(block == 0, lanes(fhs, SLAB), lanes(hs, 2 * SLAB))
                    moved = jnp.where(block == 1, lanes(hs, -SLAB), moved)
                else:
                    moved = jnp.where(block == 3, lanes(fhs, -SLAB), lanes(hs, 2 * SLAB))
                    moved = jnp.where(block == 2, lanes(hs, SLAB), moved)
                near[i, at, XL + 2] = moved


def feature_rows(p, disp, mom, slab, near, table, slots):
    for slot in slots:
        if slot < XL:
            own = [disp[3 * p + k, slot] for k in range(3)]
            own += [mom[3 * p + k, slot] for k in range(3)]
        else:
            own = [slab[3 * p + k] for k in range(3)] + [slab[6 + 3 * p + k] for k in range(3)]
        for o in range(8):
            dx, at = o >> 2, o & 3
            if slot == XL:
                j = XL + 1 + dx
            else:
                j = slot + 1 - dx if p == 0 else slot + dx
            for k in range(3):
                table[slot, SUB * (4 * o + k) : SUB * (4 * o + k + 1), :] = near[k, at, j] - own[k]
            dot = own[3] * near[3, at, j] + own[4] * near[4, at, j] + own[5] * near[5, at, j]
            table[slot, SUB * (4 * o + 3) : SUB * (4 * o + 4), :] = dot


def silu_half(u):
    return (u + u * jnp.tanh(u)).astype(bf16)


def perceptron(table, heads, w_in, b_in, w_mid, w_out, one, two, row_of, total, unroll):
    slots = 2 * XL + 2
    chunks = total // 2

    def step(i, carry):
        for c in range(unroll):
            now = i * unroll + c
            source = jnp.minimum(now, chunks - 1)
            parts = []
            for j in range(2):
                slot, y = row_of(2 * source + j)
                parts.append(
                    jnp.concatenate(
                        [table[slot, pl.ds(SUB * SUB * m + y, SUB, stride=SUB), :] for m in range(4)],
                        axis=0,
                    )
                )
            block = jnp.concatenate(parts, axis=1).astype(bf16)
            bias = b_in[...]
            hidden, last = one[...], two[...]
            u = jnp.dot(w_in[...], block, preferred_element_type=f32)
            u = u + jnp.concatenate([bias, bias], axis=1)
            v = jnp.dot(w_mid[...], hidden, preferred_element_type=f32)
            out = jnp.dot(w_out[...], last, preferred_element_type=f32)
            one[...] = silu_half(u)
            two[...] = silu_half(v)
            done = now - 2
            for j in range(2):
                slot, y = row_of(2 * jnp.clip(done, 0, chunks - 1) + j)
                slot = jnp.where((done >= 0) & (done < chunks), slot, slots)
                heads[slot, pl.ds(y, SUB, stride=SUB), :] = out[:, LANE * j : LANE * (j + 1)]
        return carry

    one[...] = jnp.zeros(one.shape, bf16)
    two[...] = jnp.zeros(two.shape, bf16)
    lax.fori_loop(0, -(-(chunks + 2) // unroll), step, 0)


def inner_row(n):
    slot, y = n // (SUB - 1), n % (SUB - 1)
    p = (slot >= XL - 1).astype(jnp.int32)
    return slot + 1 + p, y + 1 - p


def outer_row(n):
    each = 2 * SUB + XL - 1
    p = (n >= each).astype(jnp.int32)
    t = n - p * each
    face, slab = t < SUB, t < 2 * SUB
    slot = jnp.where(face, (XL - 1) * p, jnp.where(slab, XL, t - 2 * SUB + 1 - p))
    y = jnp.where(face, t, jnp.where(slab, t - SUB, (SUB - 1) * p))
    return slot + (XL + 1) * p, y


def inner_body(disp, mom, slab, w_in, b_in, w_mid, w_out, heads, near, table, one, two):
    for p in range(2):
        near_tiles(p, disp, mom, slab, None, near)
        inner = range(1, XL) if p == 0 else range(XL - 1)
        feature_rows(p, disp, mom, slab, near, table.at[pl.ds((XL + 1) * p, XL + 1)], inner)
    total = 2 * (XL - 1) * (SUB - 1)
    perceptron(table, heads, w_in, b_in, w_mid, w_out, one, two, inner_row, total, 4)


def outer_body(
    disp, mom, vel, slab, xup, xdn, yup, ydn, xyup, xydn, w_in, b_in, w_mid, w_out, inner,
    disp_out, vel_out, cbrick, near, table, heads, one, two,
):
    e0 = odd_mask(0)
    slots = XL + 1
    for n in range(2 * slots):
        heads[n] = inner[n]
    for p in range(2):
        args = (xup.at[0], yup, xyup) if p == 0 else (xdn.at[xdn.shape[0] - 1], ydn, xydn)
        near_tiles(p, disp, mom, slab, args, near)
        part = table.at[pl.ds(slots * p, slots)]
        feature_rows(p, disp, mom, slab, near, part, range(slots))
    total = 2 * (2 * SUB + XL - 1)
    perceptron(table, heads, w_in, b_in, w_mid, w_out, one, two, outer_row, total, 3)
    for p in range(2):
        coupling = []
        for slot in range(slots):
            at = slots * p + slot
            coupling.append(1.0 + 0.5 * jnp.tanh(heads[at, 3 * SUB : 4 * SUB, :]))
            if slot < XL:
                for k in range(3):
                    v = vel[3 * p + k, slot] + lattice_step * heads[at, k * SUB : (k + 1) * SUB, :]
                    vel_out[3 * p + k, slot] = v
                    disp_out[3 * p + k, slot] = disp[3 * p + k, slot] + lattice_step * v
        for xh in range(2):
            even, odd = coupling[2 * xh], coupling[2 * xh + 1]
            cbrick[2 * xh + p] = jnp.where(e0, odd, even)
            cbrick[2 * (2 + xh) + p] = jnp.where(e0, even, odd)
        cbrick[8 + p] = jnp.where(e0, lanes(coupling[4], 64), coupling[4])
        for k in range(4):
            h = slab[6 + 3 * p + k if k < 3 else 12 + p]
            cbrick[10 + 4 * p + k] = jnp.where(e0, lanes(h, 64), h)


def even_fit(func, terms):
    edge = (np.pi / 2) ** 2 * 1.0001
    node = np.cos((np.arange(400) + 0.5) * np.pi / 400)
    w = 0.5 * edge * (1 + node)
    basis = np.stack([w**n for n in range(terms)], 1)
    return [float(c) for c in np.linalg.lstsq(basis, func(np.sqrt(w)), rcond=None)[0]]


ROOT = float(np.sqrt(2.0))
SIN = [ROOT * c * np.pi ** (2 * n + 1) for n, c in enumerate(even_fit(lambda r: np.sin(r) / r, 5))]
COS = [ROOT * c * np.pi ** (2 * n) for n, c in enumerate(even_fit(np.cos, 5))]


def horner(coeffs, w):
    out = float(coeffs[-1])
    for c in reversed(coeffs[:-1]):
        out = out * w + float(c)
    return out


def crossed(a, b):
    return (a[1] * b[2] - a[2] * b[1], a[2] * b[0] - a[0] * b[2], a[0] * b[1] - a[1] * b[0])


def rotated(s, b, half_turns, hit):
    square = b[0] * b[0] + b[1] * b[1] + b[2] * b[2]
    inverse = lax.rsqrt(jnp.maximum(square, 1e-30))
    angle = (square * inverse) * half_turns
    angle = angle - jnp.round(angle)
    w = angle * angle
    sine = jnp.where(hit, horner(SIN, w) * (angle * inverse), 0.0)
    cosine = horner(COS, w)
    axis = [sine * b[k] for k in range(3)]
    first = crossed(axis, s)
    second = crossed(axis, [cosine * s[k] + first[k] for k in range(3)])
    return [s[k] + second[k] for k in range(3)]


def turns_body(nx, ny, masks, *refs):
    count = len(masks)
    bricks, cbricks = refs[:count], refs[count : 2 * count]
    out = refs[2 * count]
    mc, mh, sc, sh, cc, ch, tc, th, nc, nh = refs[2 * count + 1 :]
    xh_all, groups = 2 * nx, nx // 2
    ix, iy = lax.axis_index("gx"), lax.axis_index("gy")
    lane = iota(1)
    block = lane_block()
    first_half = block < 2
    e0 = odd_mask(0)

    def row_mask(r, par):
        return ((lane + (r + par)) & 1) == 1

    def own_rows(by):
        return pl.ds(pl.multiple_of(by * SUB, SUB), SUB)

    def place(comps, cell, slab):
        for n, (mx, my) in enumerate(masks):
            bx, by = ix ^ mx, iy ^ my
            for k in range(comps):
                for par in range(2):
                    for xh in range(2):
                        sc[par, k, 2 * bx + xh, own_rows(by), :] = cell(n, 2 * par + xh, k)
                sh[k, bx, own_rows(by), :] = slab(n, k)

    def spread(comps, put_c, put_h):
        for k in range(comps):
            for r in range(ny):
                part = pl.ds(r, SUB, stride=ny)
                for par in range(2):
                    for j in range(xh_all):
                        put_c(k, par, r, j, sc[par, k, j, part, :])
                for g in range(groups):
                    even, odd = sh[k, 2 * g, part, :], sh[k, 2 * g + 1, part, :]
                    put_h(k, 0, r, g, jnp.where(first_half, even, lanes(odd, 64)))
                    put_h(k, 1, r, g, jnp.where(first_half, lanes(even, 64), odd))

    def put_mc(k, par, r, j, v):
        mc[k // 4, par, k % 4, r, j] = v

    def put_mh(k, par, r, g, v):
        mh[k // 4, par, k % 4, r, g] = v

    def put_cc(k, par, r, j, v):
        cc[k, par, r, j] = v * (1.0 / second_shell)

    def put_ch(k, par, r, g, v):
        ch[k, par, r, g] = v * (1.0 / second_shell)

    def next_block(tiles, g):
        other = tiles[(g + 1) % groups]
        return lanes(jnp.where(block == 0, other, tiles[g]) if groups > 1 else tiles[g], -SLAB)

    def last_block(tiles, g):
        other = tiles[(g - 1) % groups]
        return lanes(jnp.where(block == 3, other, tiles[g]) if groups > 1 else tiles[g], SLAB)

    def seams(c, h):
        return (
            [lanes(h[x // 4], -SLAB * (x % 4)) for x in range(xh_all)],
            [merge_blocks(c[4 * g : 4 * g + 4]) for g in range(groups)],
        )

    def z_next(c, h, seam):
        cs = [lanes(jnp.where(lane == 0, seam[0][x], c[x]), -1) for x in range(xh_all)]
        at = (lane & (SLAB - 1)) == 0
        return cs, [lanes(jnp.where(at, seam[1][g], h[g]), -1) for g in range(groups)]

    def z_last(c, h, seam):
        cs = [lanes(jnp.where(lane == LANE - 1, seam[0][x], c[x]), 1) for x in range(xh_all)]
        at = (lane & (SLAB - 1)) == SLAB - 1
        return cs, [lanes(jnp.where(at, seam[1][g], h[g]), 1) for g in range(groups)]

    def y_next(ref, head, r, j):
        return rows(ref[*head, 0, j], -1) if r == ny - 1 else ref[*head, r + 1, j]

    def y_last(ref, head, r, j):
        return rows(ref[*head, ny - 1, j], 1) if r == 0 else ref[*head, r - 1, j]

    def near_total(p):
        q = 1 - p
        y_move = y_last if p == 0 else y_next
        z_move = z_last if p == 0 else z_next
        for k in range(3):
            for r in range(ny):
                e = row_mask(r, 0)
                for ref, to, size in ((mc, tc, xh_all), (mh, th, groups)):
                    zero = [ref[q, 0, k, r, j] for j in range(size)]
                    one = [ref[q, 1, k, r, j] for j in range(size)]
                    even = [jnp.where(e, one[j], zero[j]) for j in range(size)]
                    odd = [jnp.where(e, zero[j], one[j]) for j in range(size)]
                    for j in range(size):
                        to[k, 0, r, j] = zero[j] + one[j]
                        if p == 0:
                            prev = odd[(j - 1) % size] if ref is mc else last_block(odd, j)
                            to[k, 1, r, j] = even[j] + prev
                        else:
                            after = even[(j + 1) % size] if ref is mc else next_block(even, j)
                            to[k, 1, r, j] = odd[j] + after
            for r in range(ny):
                e = row_mask(r, 0)
                got = []
                for t in range(2):
                    c = [tc[k, t, r, j] + y_move(tc, (k, t), r, j) for j in range(xh_all)]
                    h = [th[k, t, r, j] + y_move(th, (k, t), r, j) for j in range(groups)]
                    cs, hs = z_move(c, h, seams(c, h))
                    got.append(
                        ([c[j] + cs[j] for j in range(xh_all)], [h[j] + hs[j] for j in range(groups)])
                    )
                for kind, to, size in ((0, nc, xh_all), (1, nh, groups)):
                    for j in range(size):
                        whole, split = got[0][kind][j], got[1][kind][j]
                        if p == 1:
                            whole, split = split, whole
                        to[0, k, r, j] = jnp.where(e, whole, split)
                        to[1, k, r, j] = jnp.where(e, split, whole)

    def turn(p, par, bit, half_turns):
        opp = 1 - par
        for r in range(ny):
            e = row_mask(r, par)
            shell_c, shell_h = [], []
            for k in range(3):
                head = (p, opp, k)
                c = [mc[*head, r, j] for j in range(xh_all)]
                h = [mh[*head, r, g] for g in range(groups)]
                seam = seams(c, h)
                cn, hn = z_next(c, h, seam)
                cl, hl = z_last(c, h, seam)
                one, two = [], []
                for j in range(xh_all):
                    x = c[j] + jnp.where(e, c[(j + 1) % xh_all], c[(j - 1) % xh_all])
                    y = y_next(mc, head, r, j) + y_last(mc, head, r, j)
                    one.append(x + y + (cn[j] + cl[j]))
                for g in range(groups):
                    x = h[g] + jnp.where(e, next_block(h, g), last_block(h, g))
                    y = y_next(mh, head, r, g) + y_last(mh, head, r, g)
                    two.append(x + y + (hn[g] + hl[g]))
                shell_c.append(one)
                shell_h.append(two)
            for state, couple, near, shell, size in (
                (mc, cc, nc, shell_c, xh_all),
                (mh, ch, nh, shell_h, groups),
            ):
                for j in range(size):
                    cpl = couple[p, par, r, j]
                    field = [cpl * near[par, k, r, j] + shell[k][j] for k in range(3)]
                    own = [state[p, par, k, r, j] for k in range(3)]
                    new = rotated(own, field, half_turns, state[p, par, 3, r, j] == bit)
                    for k in range(3):
                        state[p, par, k, r, j] = new[k]

    unit = second_shell * half_step / (2.0 * np.pi)

    def sweep(p, sector, half_turns):
        turn(p, sector & 1, (sector >> 1).astype(f32), half_turns)

    def climb(i, carry):
        sweep(0, i, unit)
        return carry

    def middle(i, carry):
        sector = 3 - jnp.abs(3 - i)
        sweep(1, sector, jnp.where(i == 3, 2 * unit, unit).astype(f32))
        return carry

    def descend(i, carry):
        sweep(0, 3 - i, unit)
        return carry

    place(8, lambda n, at, k: bricks[n][at, k], lambda n, k: cbricks[n][10 + k])
    spread(8, put_mc, put_mh)
    place(2, lambda n, at, k: cbricks[n][2 * at + k], lambda n, k: cbricks[n][8 + k])
    spread(2, put_cc, put_ch)
    near_total(0)
    lax.fori_loop(0, 4, climb, 0)
    near_total(1)
    lax.fori_loop(0, 7, middle, 0)
    near_total(0)
    lax.fori_loop(0, 4, descend, 0)

    for p in range(2):
        for k in range(3):
            for par in range(2):
                for xh in range(2):
                    for r in range(ny):
                        sc[par, k, xh, pl.ds(r, SUB, stride=ny), :] = mc[p, par, k, r, 2 * ix + xh]
            for xh in range(2):
                zero, one = sc[0, k, xh, own_rows(iy), :], sc[1, k, xh, own_rows(iy), :]
                out[3 * p + k, 2 * xh] = jnp.where(e0, one, zero)
                out[3 * p + k, 2 * xh + 1] = jnp.where(e0, zero, one)


def on_device(nx, ny, nz, displacement, velocity, moments, sector_bit, weight_in, bias_in, weight_mid, weight_out):
    assert displacement.shape == (6, XL, SUB, LANE)
    assert nx % 2 == 0 and nx & (nx - 1) == 0 and ny & (ny - 1) == 0 and ny % 2 == 0
    plane = ("gx", "gy")

    def pairs(move):
        out = []
        for x in range(nx):
            for y in range(ny):
                tx, ty = move(x, y)
                out.append((x * ny + y, tx % nx * ny + ty % ny))
        return out

    def shift(v, dx, dy):
        return lax.ppermute(v, plane, pairs(lambda x, y: (x + dx, y + dy)))

    def swap(v, mx, my):
        return lax.ppermute(v, plane, pairs(lambda x, y: (x ^ mx, y ^ my)))

    def along_z(v, step):
        return lax.ppermute(v, "gz", [(i, (i + step) % nz) for i in range(nz)])

    w_in = (weight_in.T.astype(f32) * 0.5).astype(bf16)
    w_mid = (weight_mid.T.astype(f32) * 0.5).astype(bf16)
    w_out = jnp.pad(weight_out.T, ((0, SUB - 4), (0, 0)))
    hidden = weight_mid.shape[0]
    b_in = jnp.broadcast_to((0.5 * bias_in)[:, None], (hidden, LANE))

    packed, brick = vmem_call(
        pack_body, [((14, *TILE), f32), ((4, 8, *TILE), f32)], displacement, moments, sector_bit,
        space=pltpu.HBM,
        grant=60 << 20,
        scratch=[
            pltpu.VMEM(displacement.shape, f32),
            pltpu.VMEM(moments.shape, f32),
            pltpu.VMEM(sector_bit.shape, sector_bit.dtype),
            pltpu.SemaphoreType.DMA((3,)),
        ],
    )
    low, high = along_z(packed, 1), along_z(packed, -1)
    far = [(mx, my) for mx in range(nx) for my in range(0, ny, 2) if mx or my]
    held = {(0, 0): brick}
    for mask in far:
        held[mask] = swap(brick, *mask)
    slab, faces, yup, ydn = vmem_call(
        halo_body,
        [((14, *TILE), f32), ((2, 12, *TILE), f32)] + [((6, *TILE), f32)] * 2,
        displacement, moments, low, high,
    )
    if nx == 2:
        faces = shift(faces, 1, 0)
        xup, xdn = faces, faces
    else:
        xup, xdn = shift(faces[:1], 1, 0), shift(faces[1:], -1, 0)
    xyup, xydn = shift(yup, 1, 1), shift(ydn, -1, -1)
    yup, ydn = shift(yup, 0, 1), shift(ydn, 0, -1)

    weights = (w_in, b_in, w_mid, w_out)
    work = [
        pltpu.VMEM((6, 4, XL + 3, *TILE), f32),
        pltpu.VMEM((2 * XL + 2, 32 * SUB, LANE), f32),
        pltpu.VMEM((2 * XL + 3, SUB * SUB, LANE), f32),
        pltpu.VMEM((hidden, 2 * LANE), bf16),
        pltpu.VMEM((hidden, 2 * LANE), bf16),
    ]
    (inner,) = vmem_call(
        inner_body, [((2 * XL + 3, SUB * SUB, LANE), f32)], displacement, moments, slab, *weights,
        scratch=work[:2] + work[3:],
        cost=pl.CostEstimate(flops=10**9, bytes_accessed=2 << 20, transcendentals=3 << 20),
    )
    disp_out, vel_out, cbrick = vmem_call(
        outer_body,
        [((6, XL, *TILE), f32), ((6, XL, *TILE), f32), ((18, *TILE), f32)],
        displacement, moments, velocity, slab, xup, xdn, yup, ydn, xyup, xydn, *weights, inner,
        scratch=work,
    )
    near_masks = [(0, 0)] + far
    late = lax.optimization_barrier((cbrick, *[held[m] for m in near_masks]))
    cbrick = late[0]
    held.update(zip(near_masks, late[1:]))
    cheld = {(0, 0): cbrick}
    for mask in far:
        cheld[mask] = swap(cbrick, *mask)
    for mx, my in near_masks:
        held[mx, my + 1] = swap(held[mx, my], 0, 1)
    for mx, my in near_masks:
        cheld[mx, my + 1] = swap(cheld[mx, my], 0, 1)

    masks = sorted(held)
    xh_all, groups = 2 * nx, nx // 2
    (moments_out,) = vmem_call(
        functools.partial(turns_body, nx, ny, masks),
        [((6, XL, *TILE), f32)],
        *[held[m] for m in masks],
        *[cheld[m] for m in masks],
        scratch=[
            pltpu.VMEM((2, 2, 4, ny, xh_all, *TILE), f32),
            pltpu.VMEM((2, 2, 4, ny, groups, *TILE), f32),
            pltpu.VMEM((2, 8, xh_all, ny * SUB, LANE), f32),
            pltpu.VMEM((8, nx, ny * SUB, LANE), f32),
            pltpu.VMEM((2, 2, ny, xh_all, *TILE), f32),
            pltpu.VMEM((2, 2, ny, groups, *TILE), f32),
            pltpu.VMEM((3, 2, ny, xh_all, *TILE), f32),
            pltpu.VMEM((3, 2, ny, groups, *TILE), f32),
            pltpu.VMEM((2, 3, ny, xh_all, *TILE), f32),
            pltpu.VMEM((2, 3, ny, groups, *TILE), f32),
        ],
    )
    return disp_out, vel_out, moments_out


def solution(mesh):
    placed = P(None, "gx", "gy", "gz")
    sizes = [mesh.shape[axis] for axis in ("gx", "gy", "gz")]
    return jax.shard_map(
        functools.partial(on_device, *sizes),
        mesh=mesh,
        in_specs=(placed,) * 4 + (P(),) * 4,
        out_specs=(placed,) * 3,
        check_vma=False,
    )
```

```python
import functools

import jax
import jax.numpy as jnp
import numpy as np
from jax import lax
from jax.experimental import pallas as pl
from jax.experimental.pallas import tpu as pltpu
from jax.sharding import PartitionSpec as P


half_step = 0.1
lattice_step = 0.25
second_shell = 0.5

f32 = jnp.float32
bf16 = jnp.bfloat16
SUB, LANE = 8, 128
SLAB = 32
XL = 4
ORDER = (0, 2, 1, 3)
TILE = (SUB, LANE)


def iota(dim):
    return lax.broadcasted_iota(jnp.int32, TILE, dim)


def odd_mask(par):
    return ((iota(0) + iota(1) + par) & 1) == 1


def lane_block():
    return ((iota(1) + SLAB // 2) // SLAB) & 3


def lanes(v, shift):
    shift = shift % LANE
    return v if shift == 0 else pltpu.roll(v, shift, 1)


def rows(v, shift):
    return pltpu.roll(v, shift % SUB, 0)


def merge_blocks(tiles):
    block = lane_block()
    out = lanes(tiles[0], 0)
    for b in range(1, 4):
        out = jnp.where(block == b, lanes(tiles[b], SLAB * b), out)
    return out


def vmem_call(body, out_shapes, *args, scratch=(), cost=None, space=None, grant=24 << 20):
    spec = pl.BlockSpec(memory_space=pltpu.VMEM)
    given = pl.BlockSpec(memory_space=space or pltpu.VMEM)
    return pl.pallas_call(
        body,
        out_shape=tuple(jax.ShapeDtypeStruct(s, d) for s, d in out_shapes),
        in_specs=[given] * len(args),
        out_specs=tuple(spec for _ in out_shapes),
        scratch_shapes=list(scratch),
        compiler_params=pltpu.CompilerParams(vmem_limit_bytes=grant),
        cost_estimate=cost,
    )(*args)


def pack_body(disp_in, mom_in, bit_in, out, brick, disp, mom, bit, sems):
    copies = [
        pltpu.make_async_copy(source, target, sems.at[n])
        for n, (source, target) in enumerate(((disp_in, disp), (mom_in, mom), (bit_in, bit)))
    ]
    for copy in copies:
        copy.start()
    for copy in copies:
        copy.wait()
    for i in range(14):
        if i < 6:
            tiles = [disp[i, x] for x in ORDER]
        elif i < 12:
            tiles = [mom[i - 6, x] for x in ORDER]
        else:
            tiles = [bit[i - 12, x].astype(f32) for x in ORDER]
        out[i] = merge_blocks(tiles)
    e0 = odd_mask(0)
    for p in range(2):
        for k in range(4):
            tiles = [mom[3 * p + k, x] if k < 3 else bit[p, x].astype(f32) for x in range(XL)]
            for xh in range(2):
                even, odd = tiles[2 * xh], tiles[2 * xh + 1]
                brick[xh, 4 * p + k] = jnp.where(e0, odd, even)
                brick[2 + xh, 4 * p + k] = jnp.where(e0, even, odd)


def halo_body(disp, mom, low, high, slab, faces, yup, ydn):
    upper = (iota(1) & (SLAB - 1)) >= SLAB // 2
    for i in range(14):
        slab[i] = jnp.where(upper, low[i], high[i])
    for i in range(6):
        src = disp if i < 3 else mom
        k = i % 3
        base = 0 if i < 3 else 6
        faces[0, 2 * i] = src[3 + k, XL - 1]
        faces[0, 2 * i + 1] = slab[base + 3 + k]
        faces[1, 2 * i] = src[k, 0]
        faces[1, 2 * i + 1] = slab[base + k]
        yup[i] = jnp.zeros(TILE, f32)
        ydn[i] = jnp.zeros(TILE, f32)
        for x in range(XL):
            yup[i, x : x + 1, :] = src[3 + k, x, SUB - 1 : SUB, :]
            ydn[i, x : x + 1, :] = src[k, x, 0:1, :]
        yup[i, XL : XL + 1, :] = slab[base + 3 + k, SUB - 1 : SUB, :]
        ydn[i, XL : XL + 1, :] = slab[base + k, 0:1, :]


def near_tiles(p, disp, mom, slab, halo, near):
    xf, yr, xyr = halo or (None, None, None)
    q = 1 - p
    lane, sub = iota(1), iota(0)
    block = lane_block()
    edge_x = XL - 1 if p == 0 else 0
    for i in range(6):
        src = disp if i < 3 else mom
        k = i % 3
        c = [src[3 * q + k, x] for x in range(XL)]
        h = slab[(0 if i < 3 else 6) + 3 * q + k]
        fc, fh = (xf[2 * i], xf[2 * i + 1]) if halo else (None, None)

        def wide(row):
            return jnp.broadcast_to(row, TILE)

        for dy in range(2):
            if dy:
                step = 1 if p == 0 else -1
                put = sub == (0 if p == 0 else SUB - 1)
                c = [rows(c[x], step) for x in range(XL)]
                h = rows(h, step)
                if halo:
                    c = [jnp.where(put, wide(yr[i, x : x + 1, :]), c[x]) for x in range(XL)]
                    h = jnp.where(put, wide(yr[i, XL : XL + 1, :]), h)
                    fc = jnp.where(put, wide(xyr[i, edge_x : edge_x + 1, :]), rows(fc, step))
                    fh = jnp.where(put, wide(xyr[i, XL : XL + 1, :]), rows(fh, step))
            for dz in range(2):
                if dz == 0:
                    cs, hs, fcs, fhs = c, h, fc, fh
                else:
                    step = 1 if p == 0 else -1
                    seam = LANE - 1 if p == 0 else 0
                    at_seam = lane == seam
                    at_seams = (lane & (SLAB - 1)) == (SLAB - 1 if p == 0 else 0)
                    cs = [
                        lanes(jnp.where(at_seam, lanes(h, -SLAB * ORDER[x]), c[x]), step)
                        for x in range(XL)
                    ]
                    if halo:
                        hs = lanes(jnp.where(at_seams, merge_blocks([c[x] for x in ORDER]), h), step)
                        fcs = lanes(jnp.where(at_seam, lanes(fh, -SLAB * ORDER[edge_x]), fc), step)
                        fhs = lanes(jnp.where(at_seams, lanes(fc, SLAB * ORDER[edge_x]), fh), step)
                at = 2 * dy + dz
                for x in range(XL):
                    near[i, at, x + 1 - p] = cs[x]
                if not halo:
                    continue
                near[i, at, XL * p] = fcs
                near[i, at, XL + 1] = hs
                if p == 0:
                    moved = jnp.where(block == 0, lanes(fhs, SLAB), lanes(hs, 2 * SLAB))
                    moved = jnp.where(block == 1, lanes(hs, -SLAB), moved)
                else:
                    moved = jnp.where(block == 3, lanes(fhs, -SLAB), lanes(hs, 2 * SLAB))
                    moved = jnp.where(block == 2, lanes(hs, SLAB), moved)
                near[i, at, XL + 2] = moved


def feature_rows(p, disp, mom, slab, near, table, slots):
    for slot in slots:
        if slot < XL:
            own = [disp[3 * p + k, slot] for k in range(3)]
            own += [mom[3 * p + k, slot] for k in range(3)]
        else:
            own = [slab[3 * p + k] for k in range(3)] + [slab[6 + 3 * p + k] for k in range(3)]
        for o in range(8):
            dx, at = o >> 2, o & 3
            if slot == XL:
                j = XL + 1 + dx
            else:
                j = slot + 1 - dx if p == 0 else slot + dx
            for k in range(3):
                table[slot, SUB * (4 * o + k) : SUB * (4 * o + k + 1), :] = near[k, at, j] - own[k]
            dot = own[3] * near[3, at, j] + own[4] * near[4, at, j] + own[5] * near[5, at, j]
            table[slot, SUB * (4 * o + 3) : SUB * (4 * o + 4), :] = dot


def silu_half(u):
    return (u + u * jnp.tanh(u)).astype(bf16)


def perceptron(table, heads, w_in, b_in, w_mid, w_out, one, two, row_of, total, unroll):
    slots = 2 * XL + 2
    chunks = total // 2

    def step(i, carry):
        for c in range(unroll):
            now = i * unroll + c
            source = jnp.minimum(now, chunks - 1)
            parts = []
            for j in range(2):
                slot, y = row_of(2 * source + j)
                parts.append(
                    jnp.concatenate(
                        [table[slot, pl.ds(SUB * SUB * m + y, SUB, stride=SUB), :] for m in range(4)],
                        axis=0,
                    )
                )
            block = jnp.concatenate(parts, axis=1).astype(bf16)
            bias = b_in[...]
            hidden, last = one[...], two[...]
            u = jnp.dot(w_in[...], block, preferred_element_type=f32)
            u = u + jnp.concatenate([bias, bias], axis=1)
            v = jnp.dot(w_mid[...], hidden, preferred_element_type=f32)
            out = jnp.dot(w_out[...], last, preferred_element_type=f32)
            one[...] = silu_half(u)
            two[...] = silu_half(v)
            done = now - 2
            for j in range(2):
                slot, y = row_of(2 * jnp.clip(done, 0, chunks - 1) + j)
                slot = jnp.where((done >= 0) & (done < chunks), slot, slots)
                heads[slot, pl.ds(y, SUB, stride=SUB), :] = out[:, LANE * j : LANE * (j + 1)]
        return carry

    one[...] = jnp.zeros(one.shape, bf16)
    two[...] = jnp.zeros(two.shape, bf16)
    lax.fori_loop(0, -(-(chunks + 2) // unroll), step, 0)


def inner_row(n):
    slot, y = n // (SUB - 1), n % (SUB - 1)
    p = (slot >= XL - 1).astype(jnp.int32)
    return slot + 1 + p, y + 1 - p


def outer_row(n):
    each = 2 * SUB + XL - 1
    p = (n >= each).astype(jnp.int32)
    t = n - p * each
    face, slab = t < SUB, t < 2 * SUB
    slot = jnp.where(face, (XL - 1) * p, jnp.where(slab, XL, t - 2 * SUB + 1 - p))
    y = jnp.where(face, t, jnp.where(slab, t - SUB, (SUB - 1) * p))
    return slot + (XL + 1) * p, y


def inner_body(disp, mom, slab, w_in, b_in, w_mid, w_out, heads, near, table, one, two):
    for p in range(2):
        near_tiles(p, disp, mom, slab, None, near)
        inner = range(1, XL) if p == 0 else range(XL - 1)
        feature_rows(p, disp, mom, slab, near, table.at[pl.ds((XL + 1) * p, XL + 1)], inner)
    total = 2 * (XL - 1) * (SUB - 1)
    perceptron(table, heads, w_in, b_in, w_mid, w_out, one, two, inner_row, total, 4)


def outer_body(
    disp, mom, slab, xup, xdn, yup, ydn, xyup, xydn, w_in, b_in, w_mid, w_out, inner,
    cbrick, force, near, table, heads, one, two,
):
    e0 = odd_mask(0)
    slots = XL + 1
    for n in range(2 * slots):
        heads[n] = inner[n]
    for p in range(2):
        args = (xup.at[0], yup, xyup) if p == 0 else (xdn.at[xdn.shape[0] - 1], ydn, xydn)
        near_tiles(p, disp, mom, slab, args, near)
        part = table.at[pl.ds(slots * p, slots)]
        feature_rows(p, disp, mom, slab, near, part, range(slots))
    total = 2 * (2 * SUB + XL - 1)
    perceptron(table, heads, w_in, b_in, w_mid, w_out, one, two, outer_row, total, 3)
    for p in range(2):
        coupling = []
        for slot in range(slots):
            at = slots * p + slot
            coupling.append(1.0 + 0.5 * jnp.tanh(heads[at, 3 * SUB : 4 * SUB, :]))
            if slot < XL:
                for k in range(3):
                    force[3 * p + k, slot] = heads[at, k * SUB : (k + 1) * SUB, :]
        for xh in range(2):
            even, odd = coupling[2 * xh], coupling[2 * xh + 1]
            cbrick[2 * xh + p] = jnp.where(e0, odd, even)
            cbrick[2 * (2 + xh) + p] = jnp.where(e0, even, odd)
        cbrick[8 + p] = jnp.where(e0, lanes(coupling[4], 64), coupling[4])
        for k in range(4):
            h = slab[6 + 3 * p + k if k < 3 else 12 + p]
            cbrick[10 + 4 * p + k] = jnp.where(e0, lanes(h, 64), h)


def move_body(disp, vel, force, disp_out, vel_out):
    v = vel[...] + lattice_step * force[...]
    vel_out[...] = v
    disp_out[...] = disp[...] + lattice_step * v


def even_fit(func, terms):
    edge = (np.pi / 2) ** 2 * 1.0001
    node = np.cos((np.arange(400) + 0.5) * np.pi / 400)
    w = 0.5 * edge * (1 + node)
    basis = np.stack([w**n for n in range(terms)], 1)
    return [float(c) for c in np.linalg.lstsq(basis, func(np.sqrt(w)), rcond=None)[0]]


ROOT = float(np.sqrt(2.0))
SIN = [ROOT * c * np.pi ** (2 * n + 1) for n, c in enumerate(even_fit(lambda r: np.sin(r) / r, 5))]
COS = [ROOT * c * np.pi ** (2 * n) for n, c in enumerate(even_fit(np.cos, 5))]


def horner(coeffs, w):
    out = float(coeffs[-1])
    for c in reversed(coeffs[:-1]):
        out = out * w + float(c)
    return out


def crossed(a, b):
    return (a[1] * b[2] - a[2] * b[1], a[2] * b[0] - a[0] * b[2], a[0] * b[1] - a[1] * b[0])


def rotated(s, b, half_turns, hit):
    square = b[0] * b[0] + b[1] * b[1] + b[2] * b[2]
    inverse = lax.rsqrt(jnp.maximum(square, 1e-30))
    angle = (square * inverse) * half_turns
    angle = angle - jnp.round(angle)
    w = angle * angle
    sine = jnp.where(hit, horner(SIN, w) * (angle * inverse), 0.0)
    cosine = horner(COS, w)
    axis = [sine * b[k] for k in range(3)]
    first = crossed(axis, s)
    second = crossed(axis, [cosine * s[k] + first[k] for k in range(3)])
    return [s[k] + second[k] for k in range(3)]


def turns_body(nx, ny, masks, *refs):
    count = len(masks)
    bricks, cbricks = refs[:count], refs[count : 2 * count]
    out = refs[2 * count]
    mc, mh, sc, sh, cc, ch, tc, th, nc, nh = refs[2 * count + 1 :]
    xh_all, groups = 2 * nx, nx // 2
    ix, iy = lax.axis_index("gx"), lax.axis_index("gy")
    lane = iota(1)
    block = lane_block()
    first_half = block < 2
    e0 = odd_mask(0)

    def row_mask(r, par):
        return ((lane + (r + par)) & 1) == 1

    def own_rows(by):
        return pl.ds(pl.multiple_of(by * SUB, SUB), SUB)

    def place(comps, cell, slab):
        for n, (mx, my) in enumerate(masks):
            bx, by = ix ^ mx, iy ^ my
            for k in range(comps):
                for par in range(2):
                    for xh in range(2):
                        sc[par, k, 2 * bx + xh, own_rows(by), :] = cell(n, 2 * par + xh, k)
                sh[k, bx, own_rows(by), :] = slab(n, k)

    def spread(comps, put_c, put_h):
        for k in range(comps):
            for r in range(ny):
                part = pl.ds(r, SUB, stride=ny)
                for par in range(2):
                    for j in range(xh_all):
                        put_c(k, par, r, j, sc[par, k, j, part, :])
                for g in range(groups):
                    even, odd = sh[k, 2 * g, part, :], sh[k, 2 * g + 1, part, :]
                    put_h(k, 0, r, g, jnp.where(first_half, even, lanes(odd, 64)))
                    put_h(k, 1, r, g, jnp.where(first_half, lanes(even, 64), odd))

    def put_mc(k, par, r, j, v):
        mc[k // 4, par, k % 4, r, j] = v

    def put_mh(k, par, r, g, v):
        mh[k // 4, par, k % 4, r, g] = v

    def put_cc(k, par, r, j, v):
        cc[k, par, r, j] = v * (1.0 / second_shell)

    def put_ch(k, par, r, g, v):
        ch[k, par, r, g] = v * (1.0 / second_shell)

    def next_block(tiles, g):
        other = tiles[(g + 1) % groups]
        return lanes(jnp.where(block == 0, other, tiles[g]) if groups > 1 else tiles[g], -SLAB)

    def last_block(tiles, g):
        other = tiles[(g - 1) % groups]
        return lanes(jnp.where(block == 3, other, tiles[g]) if groups > 1 else tiles[g], SLAB)

    def seams(c, h):
        return (
            [lanes(h[x // 4], -SLAB * (x % 4)) for x in range(xh_all)],
            [merge_blocks(c[4 * g : 4 * g + 4]) for g in range(groups)],
        )

    def z_next(c, h, seam):
        cs = [lanes(jnp.where(lane == 0, seam[0][x], c[x]), -1) for x in range(xh_all)]
        at = (lane & (SLAB - 1)) == 0
        return cs, [lanes(jnp.where(at, seam[1][g], h[g]), -1) for g in range(groups)]

    def z_last(c, h, seam):
        cs = [lanes(jnp.where(lane == LANE - 1, seam[0][x], c[x]), 1) for x in range(xh_all)]
        at = (lane & (SLAB - 1)) == SLAB - 1
        return cs, [lanes(jnp.where(at, seam[1][g], h[g]), 1) for g in range(groups)]

    def y_next(ref, head, r, j):
        return rows(ref[*head, 0, j], -1) if r == ny - 1 else ref[*head, r + 1, j]

    def y_last(ref, head, r, j):
        return rows(ref[*head, ny - 1, j], 1) if r == 0 else ref[*head, r - 1, j]

    def near_total(p):
        q = 1 - p
        y_move = y_last if p == 0 else y_next
        z_move = z_last if p == 0 else z_next
        for k in range(3):
            for r in range(ny):
                e = row_mask(r, 0)
                for ref, to, size in ((mc, tc, xh_all), (mh, th, groups)):
                    zero = [ref[q, 0, k, r, j] for j in range(size)]
                    one = [ref[q, 1, k, r, j] for j in range(size)]
                    even = [jnp.where(e, one[j], zero[j]) for j in range(size)]
                    odd = [jnp.where(e, zero[j], one[j]) for j in range(size)]
                    for j in range(size):
                        to[k, 0, r, j] = zero[j] + one[j]
                        if p == 0:
                            prev = odd[(j - 1) % size] if ref is mc else last_block(odd, j)
                            to[k, 1, r, j] = even[j] + prev
                        else:
                            after = even[(j + 1) % size] if ref is mc else next_block(even, j)
                            to[k, 1, r, j] = odd[j] + after
            for r in range(ny):
                e = row_mask(r, 0)
                got = []
                for t in range(2):
                    c = [tc[k, t, r, j] + y_move(tc, (k, t), r, j) for j in range(xh_all)]
                    h = [th[k, t, r, j] + y_move(th, (k, t), r, j) for j in range(groups)]
                    cs, hs = z_move(c, h, seams(c, h))
                    got.append(
                        ([c[j] + cs[j] for j in range(xh_all)], [h[j] + hs[j] for j in range(groups)])
                    )
                for kind, to, size in ((0, nc, xh_all), (1, nh, groups)):
                    for j in range(size):
                        whole, split = got[0][kind][j], got[1][kind][j]
                        if p == 1:
                            whole, split = split, whole
                        to[0, k, r, j] = jnp.where(e, whole, split)
                        to[1, k, r, j] = jnp.where(e, split, whole)

    def turn(p, par, bit, half_turns):
        opp = 1 - par
        for r in range(ny):
            e = row_mask(r, par)
            shell_c, shell_h = [], []
            for k in range(3):
                head = (p, opp, k)
                c = [mc[*head, r, j] for j in range(xh_all)]
                h = [mh[*head, r, g] for g in range(groups)]
                seam = seams(c, h)
                cn, hn = z_next(c, h, seam)
                cl, hl = z_last(c, h, seam)
                one, two = [], []
                for j in range(xh_all):
                    x = c[j] + jnp.where(e, c[(j + 1) % xh_all], c[(j - 1) % xh_all])
                    y = y_next(mc, head, r, j) + y_last(mc, head, r, j)
                    one.append(x + y + (cn[j] + cl[j]))
                for g in range(groups):
                    x = h[g] + jnp.where(e, next_block(h, g), last_block(h, g))
                    y = y_next(mh, head, r, g) + y_last(mh, head, r, g)
                    two.append(x + y + (hn[g] + hl[g]))
                shell_c.append(one)
                shell_h.append(two)
            for state, couple, near, shell, size in (
                (mc, cc, nc, shell_c, xh_all),
                (mh, ch, nh, shell_h, groups),
            ):
                for j in range(size):
                    cpl = couple[p, par, r, j]
                    field = [cpl * near[par, k, r, j] + shell[k][j] for k in range(3)]
                    own = [state[p, par, k, r, j] for k in range(3)]
                    new = rotated(own, field, half_turns, state[p, par, 3, r, j] == bit)
                    for k in range(3):
                        state[p, par, k, r, j] = new[k]

    def last_turn(p, par, bit, half_turns):
        opp = 1 - par
        first = 2 * ix
        before = jnp.where(ix == 0, xh_all - 1, first - 1)
        after = jnp.where(ix == nx - 1, 0, first + 2)
        near_x = (before, first, first + 1, after)
        for r in range(ny):
            e = row_mask(r, par)
            fields = [[], []]
            for k in range(3):
                head = (p, opp, k)
                c = [mc[*head, r, x] for x in near_x]
                for n in (1, 2):
                    x = near_x[n]
                    seam = pltpu.roll(mh[*head, r, x // 4], (LANE - SLAB * (x % 4)) % LANE, 1)
                    up = lanes(jnp.where(lane == 0, seam, c[n]), -1)
                    down = lanes(jnp.where(lane == LANE - 1, seam, c[n]), 1)
                    shell = c[n] + jnp.where(e, c[n + 1], c[n - 1]) + (up + down)
                    shell += y_next(mc, head, r, x) + y_last(mc, head, r, x)
                    fields[n - 1].append(cc[p, par, r, x] * nc[par, k, r, x] + shell)
            for n in (1, 2):
                x = near_x[n]
                own = [mc[p, par, k, r, x] for k in range(3)]
                new = rotated(own, fields[n - 1], half_turns, mc[p, par, 3, r, x] == bit)
                for k in range(3):
                    mc[p, par, k, r, x] = new[k]

    unit = second_shell * half_step / (2.0 * np.pi)

    def sweep(p, sector, half_turns):
        turn(p, sector & 1, (sector >> 1).astype(f32), half_turns)

    def climb(i, carry):
        sweep(0, i, unit)
        return carry

    def middle(i, carry):
        sector = 3 - jnp.abs(3 - i)
        sweep(1, sector, jnp.where(i == 3, 2 * unit, unit).astype(f32))
        return carry

    def descend(i, carry):
        sweep(0, 3 - i, unit)
        return carry

    place(8, lambda n, at, k: bricks[n][at, k], lambda n, k: cbricks[n][10 + k])
    spread(8, put_mc, put_mh)
    place(2, lambda n, at, k: cbricks[n][2 * at + k], lambda n, k: cbricks[n][8 + k])
    spread(2, put_cc, put_ch)
    near_total(0)
    lax.fori_loop(0, 4, climb, 0)
    near_total(1)
    lax.fori_loop(0, 7, middle, 0)
    near_total(0)
    lax.fori_loop(0, 3, descend, 0)
    last_turn(0, 0, 0.0, unit)

    for p in range(2):
        for k in range(3):
            for par in range(2):
                for xh in range(2):
                    for r in range(ny):
                        sc[par, k, xh, pl.ds(r, SUB, stride=ny), :] = mc[p, par, k, r, 2 * ix + xh]
            for xh in range(2):
                zero, one = sc[0, k, xh, own_rows(iy), :], sc[1, k, xh, own_rows(iy), :]
                out[3 * p + k, 2 * xh] = jnp.where(e0, one, zero)
                out[3 * p + k, 2 * xh + 1] = jnp.where(e0, zero, one)


def on_device(nx, ny, nz, displacement, velocity, moments, sector_bit, weight_in, bias_in, weight_mid, weight_out):
    assert displacement.shape == (6, XL, SUB, LANE)
    assert nx % 2 == 0 and nx & (nx - 1) == 0 and ny & (ny - 1) == 0 and ny % 2 == 0
    plane = ("gx", "gy")

    def pairs(move):
        out = []
        for x in range(nx):
            for y in range(ny):
                tx, ty = move(x, y)
                out.append((x * ny + y, tx % nx * ny + ty % ny))
        return out

    def shift(v, dx, dy):
        return lax.ppermute(v, plane, pairs(lambda x, y: (x + dx, y + dy)))

    def swap(v, mx, my):
        return lax.ppermute(v, plane, pairs(lambda x, y: (x ^ mx, y ^ my)))

    def along_z(v, step):
        return lax.ppermute(v, "gz", [(i, (i + step) % nz) for i in range(nz)])

    w_in = (weight_in.T.astype(f32) * 0.5).astype(bf16)
    w_mid = (weight_mid.T.astype(f32) * 0.5).astype(bf16)
    w_out = jnp.pad(weight_out.T, ((0, SUB - 4), (0, 0)))
    hidden = weight_mid.shape[0]
    b_in = jnp.broadcast_to((0.5 * bias_in)[:, None], (hidden, LANE))

    packed, brick = vmem_call(
        pack_body, [((14, *TILE), f32), ((4, 8, *TILE), f32)], displacement, moments, sector_bit,
        space=pltpu.HBM,
        grant=60 << 20,
        scratch=[
            pltpu.VMEM(displacement.shape, f32),
            pltpu.VMEM(moments.shape, f32),
            pltpu.VMEM(sector_bit.shape, sector_bit.dtype),
            pltpu.SemaphoreType.DMA((3,)),
        ],
    )
    low, high = along_z(packed, 1), along_z(packed, -1)
    far = [(mx, my) for mx in range(nx) for my in range(0, ny, 2) if mx or my]
    held = {(0, 0): brick}
    for mask in far:
        held[mask] = swap(brick, *mask)
    slab, faces, yup, ydn = vmem_call(
        halo_body,
        [((14, *TILE), f32), ((2, 12, *TILE), f32)] + [((6, *TILE), f32)] * 2,
        displacement, moments, low, high,
    )
    if nx == 2:
        faces = shift(faces, 1, 0)
        xup, xdn = faces, faces
    else:
        xup, xdn = shift(faces[:1], 1, 0), shift(faces[1:], -1, 0)
    xyup, xydn = shift(yup, 1, 1), shift(ydn, -1, -1)
    yup, ydn = shift(yup, 0, 1), shift(ydn, 0, -1)

    weights = (w_in, b_in, w_mid, w_out)
    work = [
        pltpu.VMEM((6, 4, XL + 3, *TILE), f32),
        pltpu.VMEM((2 * XL + 2, 32 * SUB, LANE), f32),
        pltpu.VMEM((2 * XL + 3, SUB * SUB, LANE), f32),
        pltpu.VMEM((hidden, 2 * LANE), bf16),
        pltpu.VMEM((hidden, 2 * LANE), bf16),
    ]
    (inner,) = vmem_call(
        inner_body, [((2 * XL + 3, SUB * SUB, LANE), f32)], displacement, moments, slab, *weights,
        scratch=work[:2] + work[3:],
        cost=pl.CostEstimate(flops=10**9, bytes_accessed=2 << 20, transcendentals=3 << 20),
    )
    cbrick, force = vmem_call(
        outer_body,
        [((18, *TILE), f32), ((6, XL, *TILE), f32)],
        displacement, moments, slab, xup, xdn, yup, ydn, xyup, xydn, *weights, inner,
        scratch=work,
    )
    disp_out, vel_out = vmem_call(
        move_body, [((6, XL, *TILE), f32)] * 2, displacement, velocity, force,
    )
    near_masks = [(0, 0)] + far
    late = lax.optimization_barrier((cbrick, *[held[m] for m in near_masks]))
    cbrick = late[0]
    held.update(zip(near_masks, late[1:]))
    cheld = {(0, 0): cbrick}
    for mask in far:
        cheld[mask] = swap(cbrick, *mask)
    for mx, my in near_masks:
        held[mx, my + 1] = swap(held[mx, my], 0, 1)
    for mx, my in near_masks:
        cheld[mx, my + 1] = swap(cheld[mx, my], 0, 1)

    masks = sorted(held)
    xh_all, groups = 2 * nx, nx // 2
    (moments_out,) = vmem_call(
        functools.partial(turns_body, nx, ny, masks),
        [((6, XL, *TILE), f32)],
        *[held[m] for m in masks],
        *[cheld[m] for m in masks],
        scratch=[
            pltpu.VMEM((2, 2, 4, ny, xh_all, *TILE), f32),
            pltpu.VMEM((2, 2, 4, ny, groups, *TILE), f32),
            pltpu.VMEM((2, 8, xh_all, ny * SUB, LANE), f32),
            pltpu.VMEM((8, nx, ny * SUB, LANE), f32),
            pltpu.VMEM((2, 2, ny, xh_all, *TILE), f32),
            pltpu.VMEM((2, 2, ny, groups, *TILE), f32),
            pltpu.VMEM((3, 2, ny, xh_all, *TILE), f32),
            pltpu.VMEM((3, 2, ny, groups, *TILE), f32),
            pltpu.VMEM((2, 3, ny, xh_all, *TILE), f32),
            pltpu.VMEM((2, 3, ny, groups, *TILE), f32),
        ],
    )
    return disp_out, vel_out, moments_out


def solution(mesh):
    placed = P(None, "gx", "gy", "gz")
    sizes = [mesh.shape[axis] for axis in ("gx", "gy", "gz")]
    return jax.shard_map(
        functools.partial(on_device, *sizes),
        mesh=mesh,
        in_specs=(placed,) * 4 + (P(),) * 4,
        out_specs=(placed,) * 3,
        check_vma=False,
    )
```

```python
import functools

import jax
import jax.numpy as jnp
import numpy as np
from jax import lax
from jax.experimental import pallas as pl
from jax.experimental.pallas import tpu as pltpu
from jax.sharding import PartitionSpec as P


half_step = 0.1
lattice_step = 0.25
second_shell = 0.5

f32 = jnp.float32
bf16 = jnp.bfloat16
SUB, LANE = 8, 128
SLAB = 32
XL = 4
ORDER = (0, 2, 1, 3)
TILE = (SUB, LANE)


def iota(dim):
    return lax.broadcasted_iota(jnp.int32, TILE, dim)


def odd_mask(par):
    return ((iota(0) + iota(1) + par) & 1) == 1


def lane_block():
    return ((iota(1) + SLAB // 2) // SLAB) & 3


def lanes(v, shift):
    shift = shift % LANE
    return v if shift == 0 else pltpu.roll(v, shift, 1)


def rows(v, shift):
    return pltpu.roll(v, shift % SUB, 0)


def merge_blocks(tiles):
    block = lane_block()
    out = lanes(tiles[0], 0)
    for b in range(1, 4):
        out = jnp.where(block == b, lanes(tiles[b], SLAB * b), out)
    return out


def vmem_call(body, out_shapes, *args, scratch=(), cost=None, space=None, grant=24 << 20):
    spec = pl.BlockSpec(memory_space=pltpu.VMEM)
    given = pl.BlockSpec(memory_space=space or pltpu.VMEM)
    return pl.pallas_call(
        body,
        out_shape=tuple(jax.ShapeDtypeStruct(s, d) for s, d in out_shapes),
        in_specs=[given] * len(args),
        out_specs=tuple(spec for _ in out_shapes),
        scratch_shapes=list(scratch),
        compiler_params=pltpu.CompilerParams(vmem_limit_bytes=grant),
        cost_estimate=cost,
    )(*args)


def pack_body(disp_in, mom_in, bit_in, out, brick, disp, mom, bit, sems):
    copies = [
        pltpu.make_async_copy(source, target, sems.at[n])
        for n, (source, target) in enumerate(((disp_in, disp), (mom_in, mom), (bit_in, bit)))
    ]
    for copy in copies:
        copy.start()
    for copy in copies:
        copy.wait()
    for i in range(14):
        if i < 6:
            tiles = [disp[i, x] for x in ORDER]
        elif i < 12:
            tiles = [mom[i - 6, x] for x in ORDER]
        else:
            tiles = [bit[i - 12, x].astype(f32) for x in ORDER]
        out[i] = merge_blocks(tiles)
    e0 = odd_mask(0)
    for p in range(2):
        for k in range(4):
            tiles = [mom[3 * p + k, x] if k < 3 else bit[p, x].astype(f32) for x in range(XL)]
            for xh in range(2):
                even, odd = tiles[2 * xh], tiles[2 * xh + 1]
                brick[xh, 4 * p + k] = jnp.where(e0, odd, even)
                brick[2 + xh, 4 * p + k] = jnp.where(e0, even, odd)


def halo_body(disp, mom, low, high, slab, faces, yup, ydn):
    upper = (iota(1) & (SLAB - 1)) >= SLAB // 2
    for i in range(14):
        slab[i] = jnp.where(upper, low[i], high[i])
    for i in range(6):
        src = disp if i < 3 else mom
        k = i % 3
        base = 0 if i < 3 else 6
        faces[0, 2 * i] = src[3 + k, XL - 1]
        faces[0, 2 * i + 1] = slab[base + 3 + k]
        faces[1, 2 * i] = src[k, 0]
        faces[1, 2 * i + 1] = slab[base + k]
        yup[i] = jnp.zeros(TILE, f32)
        ydn[i] = jnp.zeros(TILE, f32)
        for x in range(XL):
            yup[i, x : x + 1, :] = src[3 + k, x, SUB - 1 : SUB, :]
            ydn[i, x : x + 1, :] = src[k, x, 0:1, :]
        yup[i, XL : XL + 1, :] = slab[base + 3 + k, SUB - 1 : SUB, :]
        ydn[i, XL : XL + 1, :] = slab[base + k, 0:1, :]


def near_tiles(p, disp, mom, slab, halo, near):
    xf, yr, xyr = halo or (None, None, None)
    q = 1 - p
    lane, sub = iota(1), iota(0)
    block = lane_block()
    edge_x = XL - 1 if p == 0 else 0

    def component(k, carry):
        for half in range(2):
            i = 3 * half + k
            src = mom if half else disp
            c = [src[3 * q + k, x] for x in range(XL)]
            h = slab[6 * half + 3 * q + k]
            fc, fh = (xf[2 * i], xf[2 * i + 1]) if halo else (None, None)

            def wide(row):
                return jnp.broadcast_to(row, TILE)

            for dy in range(2):
                if dy:
                    step = 1 if p == 0 else -1
                    put = sub == (0 if p == 0 else SUB - 1)
                    c = [rows(c[x], step) for x in range(XL)]
                    h = rows(h, step)
                    if halo:
                        c = [jnp.where(put, wide(yr[i, x : x + 1, :]), c[x]) for x in range(XL)]
                        h = jnp.where(put, wide(yr[i, XL : XL + 1, :]), h)
                        fc = jnp.where(put, wide(xyr[i, edge_x : edge_x + 1, :]), rows(fc, step))
                        fh = jnp.where(put, wide(xyr[i, XL : XL + 1, :]), rows(fh, step))
                for dz in range(2):
                    if dz == 0:
                        cs, hs, fcs, fhs = c, h, fc, fh
                    else:
                        step = 1 if p == 0 else -1
                        seam = LANE - 1 if p == 0 else 0
                        at_seam = lane == seam
                        at_seams = (lane & (SLAB - 1)) == (SLAB - 1 if p == 0 else 0)
                        cs = [
                            lanes(jnp.where(at_seam, lanes(h, -SLAB * ORDER[x]), c[x]), step)
                            for x in range(XL)
                        ]
                        if halo:
                            hs = lanes(jnp.where(at_seams, merge_blocks([c[x] for x in ORDER]), h), step)
                            fcs = lanes(jnp.where(at_seam, lanes(fh, -SLAB * ORDER[edge_x]), fc), step)
                            fhs = lanes(jnp.where(at_seams, lanes(fc, SLAB * ORDER[edge_x]), fh), step)
                    at = 2 * dy + dz
                    for x in range(XL):
                        near[i, at, x + 1 - p] = cs[x]
                    if not halo:
                        continue
                    near[i, at, XL * p] = fcs
                    near[i, at, XL + 1] = hs
                    if p == 0:
                        moved = jnp.where(block == 0, lanes(fhs, SLAB), lanes(hs, 2 * SLAB))
                        moved = jnp.where(block == 1, lanes(hs, -SLAB), moved)
                    else:
                        moved = jnp.where(block == 3, lanes(fhs, -SLAB), lanes(hs, 2 * SLAB))
                        moved = jnp.where(block == 2, lanes(hs, SLAB), moved)
                    near[i, at, XL + 2] = moved
        return carry

    if halo:
        lax.fori_loop(0, 3, component, 0)
    else:
        for k in range(3):
            component(k, 0)


def feature_rows(p, disp, mom, slab, near, table, slots):
    for slot in slots:
        if slot < XL:
            own = [disp[3 * p + k, slot] for k in range(3)]
            own += [mom[3 * p + k, slot] for k in range(3)]
        else:
            own = [slab[3 * p + k] for k in range(3)] + [slab[6 + 3 * p + k] for k in range(3)]
        for o in range(8):
            dx, at = o >> 2, o & 3
            if slot == XL:
                j = XL + 1 + dx
            else:
                j = slot + 1 - dx if p == 0 else slot + dx
            for k in range(3):
                table[slot, SUB * (4 * o + k) : SUB * (4 * o + k + 1), :] = near[k, at, j] - own[k]
            dot = own[3] * near[3, at, j] + own[4] * near[4, at, j] + own[5] * near[5, at, j]
            table[slot, SUB * (4 * o + 3) : SUB * (4 * o + 4), :] = dot


def silu_half(u):
    return (u + u * jnp.tanh(u)).astype(bf16)


def perceptron(table, heads, w_in, b_in, w_mid, w_out, one, two, row_of, total, unroll):
    slots = 2 * XL + 2
    chunks = total // 2

    def step(i, carry):
        for c in range(unroll):
            now = i * unroll + c
            source = jnp.minimum(now, chunks - 1)
            parts = []
            for j in range(2):
                slot, y = row_of(2 * source + j)
                parts.append(
                    jnp.concatenate(
                        [table[slot, pl.ds(SUB * SUB * m + y, SUB, stride=SUB), :] for m in range(4)],
                        axis=0,
                    )
                )
            block = jnp.concatenate(parts, axis=1).astype(bf16)
            bias = b_in[...]
            hidden, last = one[...], two[...]
            u = jnp.dot(w_in[...], block, preferred_element_type=f32)
            u = u + jnp.concatenate([bias, bias], axis=1)
            v = jnp.dot(w_mid[...], hidden, preferred_element_type=f32)
            out = jnp.dot(w_out[...], last, preferred_element_type=f32)
            one[...] = silu_half(u)
            two[...] = silu_half(v)
            done = now - 2
            for j in range(2):
                slot, y = row_of(2 * jnp.clip(done, 0, chunks - 1) + j)
                slot = jnp.where((done >= 0) & (done < chunks), slot, slots)
                heads[slot, pl.ds(y, SUB, stride=SUB), :] = out[:, LANE * j : LANE * (j + 1)]
        return carry

    one[...] = jnp.zeros(one.shape, bf16)
    two[...] = jnp.zeros(two.shape, bf16)
    lax.fori_loop(0, -(-(chunks + 2) // unroll), step, 0)


def inner_row(n):
    slot, y = n // (SUB - 1), n % (SUB - 1)
    p = (slot >= XL - 1).astype(jnp.int32)
    return slot + 1 + p, y + 1 - p


def outer_row(n):
    each = 2 * SUB + XL - 1
    p = (n >= each).astype(jnp.int32)
    t = n - p * each
    face, slab = t < SUB, t < 2 * SUB
    slot = jnp.where(face, (XL - 1) * p, jnp.where(slab, XL, t - 2 * SUB + 1 - p))
    y = jnp.where(face, t, jnp.where(slab, t - SUB, (SUB - 1) * p))
    return slot + (XL + 1) * p, y


def inner_body(disp, mom, slab, w_in, b_in, w_mid, w_out, heads, near, table, one, two):
    for p in range(2):
        near_tiles(p, disp, mom, slab, None, near)
        inner = range(1, XL) if p == 0 else range(XL - 1)
        feature_rows(p, disp, mom, slab, near, table.at[pl.ds((XL + 1) * p, XL + 1)], inner)
    total = 2 * (XL - 1) * (SUB - 1)
    perceptron(table, heads, w_in, b_in, w_mid, w_out, one, two, inner_row, total, 4)


def outer_body(
    disp, mom, slab, xup, xdn, yup, ydn, xyup, xydn, w_in, b_in, w_mid, w_out, inner,
    cbrick, force, near, table, heads, one, two,
):
    e0 = odd_mask(0)
    slots = XL + 1
    for n in range(2 * slots):
        heads[n] = inner[n]
    for p in range(2):
        args = (xup.at[0], yup, xyup) if p == 0 else (xdn.at[xdn.shape[0] - 1], ydn, xydn)
        near_tiles(p, disp, mom, slab, args, near)
        part = table.at[pl.ds(slots * p, slots)]
        feature_rows(p, disp, mom, slab, near, part, range(slots))
    total = 2 * (2 * SUB + XL - 1)
    perceptron(table, heads, w_in, b_in, w_mid, w_out, one, two, outer_row, total, 3)
    for p in range(2):
        coupling = []
        for slot in range(slots):
            at = slots * p + slot
            coupling.append(1.0 + 0.5 * jnp.tanh(heads[at, 3 * SUB : 4 * SUB, :]))
            if slot < XL:
                for k in range(3):
                    force[3 * p + k, slot] = heads[at, k * SUB : (k + 1) * SUB, :]
        for xh in range(2):
            even, odd = coupling[2 * xh], coupling[2 * xh + 1]
            cbrick[2 * xh + p] = jnp.where(e0, odd, even)
            cbrick[2 * (2 + xh) + p] = jnp.where(e0, even, odd)
        cbrick[8 + p] = jnp.where(e0, lanes(coupling[4], 64), coupling[4])
        for k in range(4):
            h = slab[6 + 3 * p + k if k < 3 else 12 + p]
            cbrick[10 + 4 * p + k] = jnp.where(e0, lanes(h, 64), h)


def move_body(disp, vel, force, disp_out, vel_out):
    v = vel[...] + lattice_step * force[...]
    vel_out[...] = v
    disp_out[...] = disp[...] + lattice_step * v


def even_fit(func, terms):
    edge = (np.pi / 2) ** 2 * 1.0001
    node = np.cos((np.arange(400) + 0.5) * np.pi / 400)
    w = 0.5 * edge * (1 + node)
    basis = np.stack([w**n for n in range(terms)], 1)
    return [float(c) for c in np.linalg.lstsq(basis, func(np.sqrt(w)), rcond=None)[0]]


ROOT = float(np.sqrt(2.0))
SIN = [ROOT * c * np.pi ** (2 * n + 1) for n, c in enumerate(even_fit(lambda r: np.sin(r) / r, 5))]
COS = [ROOT * c * np.pi ** (2 * n) for n, c in enumerate(even_fit(np.cos, 5))]


def horner(coeffs, w):
    out = float(coeffs[-1])
    for c in reversed(coeffs[:-1]):
        out = out * w + float(c)
    return out


def crossed(a, b):
    return (a[1] * b[2] - a[2] * b[1], a[2] * b[0] - a[0] * b[2], a[0] * b[1] - a[1] * b[0])


def rotated(s, b, half_turns, hit):
    square = b[0] * b[0] + b[1] * b[1] + b[2] * b[2]
    inverse = lax.rsqrt(jnp.maximum(square, 1e-30))
    angle = (square * inverse) * half_turns
    angle = angle - jnp.round(angle)
    w = angle * angle
    sine = jnp.where(hit, horner(SIN, w) * (angle * inverse), 0.0)
    cosine = horner(COS, w)
    axis = [sine * b[k] for k in range(3)]
    first = crossed(axis, s)
    second = crossed(axis, [cosine * s[k] + first[k] for k in range(3)])
    return [s[k] + second[k] for k in range(3)]


def turns_body(nx, ny, masks, *refs):
    count = len(masks)
    bricks, cbricks = refs[:count], refs[count : 2 * count]
    out = refs[2 * count]
    mc, mh, sc, sh, cc, ch, tc, th, nc, nh = refs[2 * count + 1 :]
    xh_all, groups = 2 * nx, nx // 2
    ix, iy = lax.axis_index("gx"), lax.axis_index("gy")
    lane = iota(1)
    block = lane_block()
    first_half = block < 2
    e0 = odd_mask(0)

    def row_mask(r, par):
        return ((lane + (r + par)) & 1) == 1

    def own_rows(by):
        return pl.ds(pl.multiple_of(by * SUB, SUB), SUB)

    def place(comps, cell, slab):
        for n, (mx, my) in enumerate(masks):
            bx, by = ix ^ mx, iy ^ my
            for k in range(comps):
                for par in range(2):
                    for xh in range(2):
                        sc[par, k, 2 * bx + xh, own_rows(by), :] = cell(n, 2 * par + xh, k)
                sh[k, bx, own_rows(by), :] = slab(n, k)

    def spread(comps, put_c, put_h):
        for k in range(comps):
            for r in range(ny):
                part = pl.ds(r, SUB, stride=ny)
                for par in range(2):
                    for j in range(xh_all):
                        put_c(k, par, r, j, sc[par, k, j, part, :])
                for g in range(groups):
                    even, odd = sh[k, 2 * g, part, :], sh[k, 2 * g + 1, part, :]
                    put_h(k, 0, r, g, jnp.where(first_half, even, lanes(odd, 64)))
                    put_h(k, 1, r, g, jnp.where(first_half, lanes(even, 64), odd))

    def put_mc(k, par, r, j, v):
        mc[k // 4, par, k % 4, r, j] = v

    def put_mh(k, par, r, g, v):
        mh[k // 4, par, k % 4, r, g] = v

    def put_cc(k, par, r, j, v):
        cc[k, par, r, j] = v * (1.0 / second_shell)

    def put_ch(k, par, r, g, v):
        ch[k, par, r, g] = v * (1.0 / second_shell)

    def next_block(tiles, g):
        other = tiles[(g + 1) % groups]
        return lanes(jnp.where(block == 0, other, tiles[g]) if groups > 1 else tiles[g], -SLAB)

    def last_block(tiles, g):
        other = tiles[(g - 1) % groups]
        return lanes(jnp.where(block == 3, other, tiles[g]) if groups > 1 else tiles[g], SLAB)

    def seams(c, h):
        return (
            [lanes(h[x // 4], -SLAB * (x % 4)) for x in range(xh_all)],
            [merge_blocks(c[4 * g : 4 * g + 4]) for g in range(groups)],
        )

    def z_next(c, h, seam):
        cs = [lanes(jnp.where(lane == 0, seam[0][x], c[x]), -1) for x in range(xh_all)]
        at = (lane & (SLAB - 1)) == 0
        return cs, [lanes(jnp.where(at, seam[1][g], h[g]), -1) for g in range(groups)]

    def z_last(c, h, seam):
        cs = [lanes(jnp.where(lane == LANE - 1, seam[0][x], c[x]), 1) for x in range(xh_all)]
        at = (lane & (SLAB - 1)) == SLAB - 1
        return cs, [lanes(jnp.where(at, seam[1][g], h[g]), 1) for g in range(groups)]

    def y_next(ref, head, r, j):
        return rows(ref[*head, 0, j], -1) if r == ny - 1 else ref[*head, r + 1, j]

    def y_last(ref, head, r, j):
        return rows(ref[*head, ny - 1, j], 1) if r == 0 else ref[*head, r - 1, j]

    def near_total(p):
        q = 1 - p
        y_move = y_last if p == 0 else y_next
        z_move = z_last if p == 0 else z_next

        def component(k, carry):
            for r in range(ny):
                e = row_mask(r, 0)
                for ref, to, size in ((mc, tc, xh_all), (mh, th, groups)):
                    zero = [ref[q, 0, k, r, j] for j in range(size)]
                    one = [ref[q, 1, k, r, j] for j in range(size)]
                    even = [jnp.where(e, one[j], zero[j]) for j in range(size)]
                    odd = [jnp.where(e, zero[j], one[j]) for j in range(size)]
                    for j in range(size):
                        to[k, 0, r, j] = zero[j] + one[j]
                        if p == 0:
                            prev = odd[(j - 1) % size] if ref is mc else last_block(odd, j)
                            to[k, 1, r, j] = even[j] + prev
                        else:
                            after = even[(j + 1) % size] if ref is mc else next_block(even, j)
                            to[k, 1, r, j] = odd[j] + after
            for r in range(ny):
                e = row_mask(r, 0)
                got = []
                for t in range(2):
                    c = [tc[k, t, r, j] + y_move(tc, (k, t), r, j) for j in range(xh_all)]
                    h = [th[k, t, r, j] + y_move(th, (k, t), r, j) for j in range(groups)]
                    cs, hs = z_move(c, h, seams(c, h))
                    got.append(
                        ([c[j] + cs[j] for j in range(xh_all)], [h[j] + hs[j] for j in range(groups)])
                    )
                for kind, to, size in ((0, nc, xh_all), (1, nh, groups)):
                    for j in range(size):
                        whole, split = got[0][kind][j], got[1][kind][j]
                        if p == 1:
                            whole, split = split, whole
                        to[0, k, r, j] = jnp.where(e, whole, split)
                        to[1, k, r, j] = jnp.where(e, split, whole)
            return carry

        lax.fori_loop(0, 3, component, 0)

    def turn(p, par, bit, half_turns):
        opp = 1 - par
        for r in range(ny):
            e = row_mask(r, par)
            shell_c, shell_h = [], []
            for k in range(3):
                head = (p, opp, k)
                c = [mc[*head, r, j] for j in range(xh_all)]
                h = [mh[*head, r, g] for g in range(groups)]
                seam = seams(c, h)
                cn, hn = z_next(c, h, seam)
                cl, hl = z_last(c, h, seam)
                one, two = [], []
                for j in range(xh_all):
                    x = c[j] + jnp.where(e, c[(j + 1) % xh_all], c[(j - 1) % xh_all])
                    y = y_next(mc, head, r, j) + y_last(mc, head, r, j)
                    one.append(x + y + (cn[j] + cl[j]))
                for g in range(groups):
                    x = h[g] + jnp.where(e, next_block(h, g), last_block(h, g))
                    y = y_next(mh, head, r, g) + y_last(mh, head, r, g)
                    two.append(x + y + (hn[g] + hl[g]))
                shell_c.append(one)
                shell_h.append(two)
            for state, couple, near, shell, size in (
                (mc, cc, nc, shell_c, xh_all),
                (mh, ch, nh, shell_h, groups),
            ):
                for j in range(size):
                    cpl = couple[p, par, r, j]
                    field = [cpl * near[par, k, r, j] + shell[k][j] for k in range(3)]
                    own = [state[p, par, k, r, j] for k in range(3)]
                    new = rotated(own, field, half_turns, state[p, par, 3, r, j] == bit)
                    for k in range(3):
                        state[p, par, k, r, j] = new[k]

    def last_turn(p, par, bit, half_turns):
        opp = 1 - par
        first = 2 * ix
        before = jnp.where(ix == 0, xh_all - 1, first - 1)
        after = jnp.where(ix == nx - 1, 0, first + 2)
        near_x = (before, first, first + 1, after)
        for r in range(ny):
            e = row_mask(r, par)
            fields = [[], []]
            for k in range(3):
                head = (p, opp, k)
                c = [mc[*head, r, x] for x in near_x]
                for n in (1, 2):
                    x = near_x[n]
                    seam = pltpu.roll(mh[*head, r, x // 4], (LANE - SLAB * (x % 4)) % LANE, 1)
                    up = lanes(jnp.where(lane == 0, seam, c[n]), -1)
                    down = lanes(jnp.where(lane == LANE - 1, seam, c[n]), 1)
                    shell = c[n] + jnp.where(e, c[n + 1], c[n - 1]) + (up + down)
                    shell += y_next(mc, head, r, x) + y_last(mc, head, r, x)
                    fields[n - 1].append(cc[p, par, r, x] * nc[par, k, r, x] + shell)
            for n in (1, 2):
                x = near_x[n]
                own = [mc[p, par, k, r, x] for k in range(3)]
                new = rotated(own, fields[n - 1], half_turns, mc[p, par, 3, r, x] == bit)
                for k in range(3):
                    mc[p, par, k, r, x] = new[k]

    unit = second_shell * half_step / (2.0 * np.pi)

    def sweep(p, sector, half_turns):
        turn(p, sector & 1, (sector >> 1).astype(f32), half_turns)

    def climb(i, carry):
        sweep(0, i, unit)
        return carry

    def middle(i, carry):
        sector = 3 - jnp.abs(3 - i)
        sweep(1, sector, jnp.where(i == 3, 2 * unit, unit).astype(f32))
        return carry

    def descend(i, carry):
        sweep(0, 3 - i, unit)
        return carry

    place(8, lambda n, at, k: bricks[n][at, k], lambda n, k: cbricks[n][10 + k])
    spread(8, put_mc, put_mh)
    place(2, lambda n, at, k: cbricks[n][2 * at + k], lambda n, k: cbricks[n][8 + k])
    spread(2, put_cc, put_ch)
    near_total(0)
    lax.fori_loop(0, 4, climb, 0)
    near_total(1)
    lax.fori_loop(0, 7, middle, 0)
    near_total(0)
    lax.fori_loop(0, 3, descend, 0)
    last_turn(0, 0, 0.0, unit)

    for p in range(2):
        for k in range(3):
            for par in range(2):
                for xh in range(2):
                    for r in range(ny):
                        sc[par, k, xh, pl.ds(r, SUB, stride=ny), :] = mc[p, par, k, r, 2 * ix + xh]
            for xh in range(2):
                zero, one = sc[0, k, xh, own_rows(iy), :], sc[1, k, xh, own_rows(iy), :]
                out[3 * p + k, 2 * xh] = jnp.where(e0, one, zero)
                out[3 * p + k, 2 * xh + 1] = jnp.where(e0, zero, one)


def on_device(nx, ny, nz, displacement, velocity, moments, sector_bit, weight_in, bias_in, weight_mid, weight_out):
    assert displacement.shape == (6, XL, SUB, LANE)
    assert nx % 2 == 0 and nx & (nx - 1) == 0 and ny & (ny - 1) == 0 and ny % 2 == 0
    plane = ("gx", "gy")

    def pairs(move):
        out = []
        for x in range(nx):
            for y in range(ny):
                tx, ty = move(x, y)
                out.append((x * ny + y, tx % nx * ny + ty % ny))
        return out

    def shift(v, dx, dy):
        return lax.ppermute(v, plane, pairs(lambda x, y: (x + dx, y + dy)))

    def swap(v, mx, my):
        return lax.ppermute(v, plane, pairs(lambda x, y: (x ^ mx, y ^ my)))

    def along_z(v, step):
        return lax.ppermute(v, "gz", [(i, (i + step) % nz) for i in range(nz)])

    w_in = (weight_in.T.astype(f32) * 0.5).astype(bf16)
    w_mid = (weight_mid.T.astype(f32) * 0.5).astype(bf16)
    w_out = jnp.pad(weight_out.T, ((0, SUB - 4), (0, 0)))
    hidden = weight_mid.shape[0]
    b_in = jnp.broadcast_to((0.5 * bias_in)[:, None], (hidden, LANE))

    packed, brick = vmem_call(
        pack_body, [((14, *TILE), f32), ((4, 8, *TILE), f32)], displacement, moments, sector_bit,
        space=pltpu.HBM,
        grant=60 << 20,
        scratch=[
            pltpu.VMEM(displacement.shape, f32),
            pltpu.VMEM(moments.shape, f32),
            pltpu.VMEM(sector_bit.shape, sector_bit.dtype),
            pltpu.SemaphoreType.DMA((3,)),
        ],
    )
    low, high = along_z(packed, 1), along_z(packed, -1)
    far = [(mx, my) for mx in range(nx) for my in range(0, ny, 2) if mx or my]
    held = {(0, 0): brick}
    for mask in far:
        held[mask] = swap(brick, *mask)
    slab, faces, yup, ydn = vmem_call(
        halo_body,
        [((14, *TILE), f32), ((2, 12, *TILE), f32)] + [((6, *TILE), f32)] * 2,
        displacement, moments, low, high,
    )
    if nx == 2:
        faces = shift(faces, 1, 0)
        xup, xdn = faces, faces
    else:
        xup, xdn = shift(faces[:1], 1, 0), shift(faces[1:], -1, 0)
    xyup, xydn = shift(yup, 1, 1), shift(ydn, -1, -1)
    yup, ydn = shift(yup, 0, 1), shift(ydn, 0, -1)

    weights = (w_in, b_in, w_mid, w_out)
    work = [
        pltpu.VMEM((6, 4, XL + 3, *TILE), f32),
        pltpu.VMEM((2 * XL + 2, 32 * SUB, LANE), f32),
        pltpu.VMEM((2 * XL + 3, SUB * SUB, LANE), f32),
        pltpu.VMEM((hidden, 2 * LANE), bf16),
        pltpu.VMEM((hidden, 2 * LANE), bf16),
    ]
    (inner,) = vmem_call(
        inner_body, [((2 * XL + 3, SUB * SUB, LANE), f32)], displacement, moments, slab, *weights,
        scratch=work[:2] + work[3:],
        cost=pl.CostEstimate(flops=10**9, bytes_accessed=2 << 20, transcendentals=3 << 20),
    )
    cbrick, force = vmem_call(
        outer_body,
        [((18, *TILE), f32), ((6, XL, *TILE), f32)],
        displacement, moments, slab, xup, xdn, yup, ydn, xyup, xydn, *weights, inner,
        scratch=work,
    )
    disp_out, vel_out = vmem_call(
        move_body, [((6, XL, *TILE), f32)] * 2, displacement, velocity, force,
    )
    near_masks = [(0, 0)] + far
    late = lax.optimization_barrier((cbrick, *[held[m] for m in near_masks]))
    cbrick = late[0]
    held.update(zip(near_masks, late[1:]))
    cheld = {(0, 0): cbrick}
    for mask in far:
        cheld[mask] = swap(cbrick, *mask)
    for mx, my in near_masks:
        held[mx, my + 1] = swap(held[mx, my], 0, 1)
    for mx, my in near_masks:
        cheld[mx, my + 1] = swap(cheld[mx, my], 0, 1)

    masks = sorted(held)
    xh_all, groups = 2 * nx, nx // 2
    (moments_out,) = vmem_call(
        functools.partial(turns_body, nx, ny, masks),
        [((6, XL, *TILE), f32)],
        *[held[m] for m in masks],
        *[cheld[m] for m in masks],
        scratch=[
            pltpu.VMEM((2, 2, 4, ny, xh_all, *TILE), f32),
            pltpu.VMEM((2, 2, 4, ny, groups, *TILE), f32),
            pltpu.VMEM((2, 8, xh_all, ny * SUB, LANE), f32),
            pltpu.VMEM((8, nx, ny * SUB, LANE), f32),
            pltpu.VMEM((2, 2, ny, xh_all, *TILE), f32),
            pltpu.VMEM((2, 2, ny, groups, *TILE), f32),
            pltpu.VMEM((3, 2, ny, xh_all, *TILE), f32),
            pltpu.VMEM((3, 2, ny, groups, *TILE), f32),
            pltpu.VMEM((2, 3, ny, xh_all, *TILE), f32),
            pltpu.VMEM((2, 3, ny, groups, *TILE), f32),
        ],
    )
    return disp_out, vel_out, moments_out


def solution(mesh):
    placed = P(None, "gx", "gy", "gz")
    sizes = [mesh.shape[axis] for axis in ("gx", "gy", "gz")]
    return jax.shard_map(
        functools.partial(on_device, *sizes),
        mesh=mesh,
        in_specs=(placed,) * 4 + (P(),) * 4,
        out_specs=(placed,) * 3,
        check_vma=False,
    )
```

```python
import functools

import jax
import jax.numpy as jnp
import numpy as np
from jax import lax
from jax.experimental import pallas as pl
from jax.experimental.pallas import tpu as pltpu
from jax.sharding import PartitionSpec as P


half_step = 0.1
lattice_step = 0.25
second_shell = 0.5

f32 = jnp.float32
bf16 = jnp.bfloat16
SUB, LANE = 8, 128
SLAB = 32
XL = 4
ORDER = (0, 2, 1, 3)
TILE = (SUB, LANE)


def iota(dim):
    return lax.broadcasted_iota(jnp.int32, TILE, dim)


def odd_mask(par):
    return ((iota(0) + iota(1) + par) & 1) == 1


def lane_block():
    return ((iota(1) + SLAB // 2) // SLAB) & 3


def lanes(v, shift):
    shift = shift % LANE
    return v if shift == 0 else pltpu.roll(v, shift, 1)


def rows(v, shift):
    return pltpu.roll(v, shift % SUB, 0)


def merge_blocks(tiles):
    block = lane_block()
    out = lanes(tiles[0], 0)
    for b in range(1, 4):
        out = jnp.where(block == b, lanes(tiles[b], SLAB * b), out)
    return out


def vmem_call(body, out_shapes, *args, scratch=(), cost=None, space=None, grant=24 << 20):
    spec = pl.BlockSpec(memory_space=pltpu.VMEM)
    given = pl.BlockSpec(memory_space=space or pltpu.VMEM)
    return pl.pallas_call(
        body,
        out_shape=tuple(jax.ShapeDtypeStruct(s, d) for s, d in out_shapes),
        in_specs=[given] * len(args),
        out_specs=tuple(spec for _ in out_shapes),
        scratch_shapes=list(scratch),
        compiler_params=pltpu.CompilerParams(vmem_limit_bytes=grant),
        cost_estimate=cost,
    )(*args)


def pack_body(disp_in, mom_in, bit_in, w_in, out, brick, disp, mom, w, bit, sems):
    copies = [
        pltpu.make_async_copy(source, target, sems.at[n])
        for n, (source, target) in enumerate(((disp_in, disp), (mom_in, mom), (bit_in, bit), (w_in, w)))
    ]
    for copy in copies:
        copy.start()
    for copy in copies[:3]:
        copy.wait()
    for i in range(14):
        if i < 6:
            tiles = [disp[i, x] for x in ORDER]
        elif i < 12:
            tiles = [mom[i - 6, x] for x in ORDER]
        else:
            tiles = [bit[i - 12, x].astype(f32) for x in ORDER]
        out[i] = merge_blocks(tiles)
    e0 = odd_mask(0)
    for p in range(2):
        for k in range(4):
            tiles = [mom[3 * p + k, x] if k < 3 else bit[p, x].astype(f32) for x in range(XL)]
            for xh in range(2):
                even, odd = tiles[2 * xh], tiles[2 * xh + 1]
                brick[xh, 4 * p + k] = jnp.where(e0, odd, even)
                brick[2 + xh, 4 * p + k] = jnp.where(e0, even, odd)
    copies[3].wait()


def halo_body(disp, mom, low, high, slab, faces, yup, ydn):
    upper = (iota(1) & (SLAB - 1)) >= SLAB // 2
    for i in range(14):
        slab[i] = jnp.where(upper, low[i], high[i])
    for i in range(6):
        src = disp if i < 3 else mom
        k = i % 3
        base = 0 if i < 3 else 6
        faces[0, 2 * i] = src[3 + k, XL - 1]
        faces[0, 2 * i + 1] = slab[base + 3 + k]
        faces[1, 2 * i] = src[k, 0]
        faces[1, 2 * i + 1] = slab[base + k]
        yup[i] = jnp.zeros(TILE, f32)
        ydn[i] = jnp.zeros(TILE, f32)
        for x in range(XL):
            yup[i, x : x + 1, :] = src[3 + k, x, SUB - 1 : SUB, :]
            ydn[i, x : x + 1, :] = src[k, x, 0:1, :]
        yup[i, XL : XL + 1, :] = slab[base + 3 + k, SUB - 1 : SUB, :]
        ydn[i, XL : XL + 1, :] = slab[base + k, 0:1, :]


def near_tiles(p, disp, mom, slab, halo, near):
    xf, yr, xyr = halo or (None, None, None)
    q = 1 - p
    lane, sub = iota(1), iota(0)
    block = lane_block()
    edge_x = XL - 1 if p == 0 else 0

    def component(k, carry):
        for half in range(2):
            i = 3 * half + k
            src = mom if half else disp
            c = [src[3 * q + k, x] for x in range(XL)]
            h = slab[6 * half + 3 * q + k]
            fc, fh = (xf[2 * i], xf[2 * i + 1]) if halo else (None, None)

            def wide(row):
                return jnp.broadcast_to(row, TILE)

            for dy in range(2):
                if dy:
                    step = 1 if p == 0 else -1
                    put = sub == (0 if p == 0 else SUB - 1)
                    c = [rows(c[x], step) for x in range(XL)]
                    h = rows(h, step)
                    if halo:
                        c = [jnp.where(put, wide(yr[i, x : x + 1, :]), c[x]) for x in range(XL)]
                        h = jnp.where(put, wide(yr[i, XL : XL + 1, :]), h)
                        fc = jnp.where(put, wide(xyr[i, edge_x : edge_x + 1, :]), rows(fc, step))
                        fh = jnp.where(put, wide(xyr[i, XL : XL + 1, :]), rows(fh, step))
                for dz in range(2):
                    if dz == 0:
                        cs, hs, fcs, fhs = c, h, fc, fh
                    else:
                        step = 1 if p == 0 else -1
                        seam = LANE - 1 if p == 0 else 0
                        at_seam = lane == seam
                        at_seams = (lane & (SLAB - 1)) == (SLAB - 1 if p == 0 else 0)
                        cs = [
                            lanes(jnp.where(at_seam, lanes(h, -SLAB * ORDER[x]), c[x]), step)
                            for x in range(XL)
                        ]
                        if halo:
                            hs = lanes(jnp.where(at_seams, merge_blocks([c[x] for x in ORDER]), h), step)
                            fcs = lanes(jnp.where(at_seam, lanes(fh, -SLAB * ORDER[edge_x]), fc), step)
                            fhs = lanes(jnp.where(at_seams, lanes(fc, SLAB * ORDER[edge_x]), fh), step)
                    at = 2 * dy + dz
                    for x in range(XL):
                        near[i, at, x + 1 - p] = cs[x]
                    if not halo:
                        continue
                    near[i, at, XL * p] = fcs
                    near[i, at, XL + 1] = hs
                    if p == 0:
                        moved = jnp.where(block == 0, lanes(fhs, SLAB), lanes(hs, 2 * SLAB))
                        moved = jnp.where(block == 1, lanes(hs, -SLAB), moved)
                    else:
                        moved = jnp.where(block == 3, lanes(fhs, -SLAB), lanes(hs, 2 * SLAB))
                        moved = jnp.where(block == 2, lanes(hs, SLAB), moved)
                    near[i, at, XL + 2] = moved
        return carry

    if halo:
        lax.fori_loop(0, 3, component, 0)
    else:
        for k in range(3):
            component(k, 0)


def feature_rows(p, disp, mom, slab, near, table, slots):
    for slot in slots:
        if slot < XL:
            own = [disp[3 * p + k, slot] for k in range(3)]
            own += [mom[3 * p + k, slot] for k in range(3)]
        else:
            own = [slab[3 * p + k] for k in range(3)] + [slab[6 + 3 * p + k] for k in range(3)]
        for o in range(8):
            dx, at = o >> 2, o & 3
            if slot == XL:
                j = XL + 1 + dx
            else:
                j = slot + 1 - dx if p == 0 else slot + dx
            for k in range(3):
                table[slot, SUB * (4 * o + k) : SUB * (4 * o + k + 1), :] = near[k, at, j] - own[k]
            dot = own[3] * near[3, at, j] + own[4] * near[4, at, j] + own[5] * near[5, at, j]
            table[slot, SUB * (4 * o + 3) : SUB * (4 * o + 4), :] = dot


def silu_half(u):
    return (u + u * jnp.tanh(u)).astype(bf16)


def perceptron(table, heads, w_in, b_in, w_mid, w_out, one, two, row_of, total, unroll):
    slots = 2 * XL + 2
    chunks = total // 2

    def step(i, carry):
        for c in range(unroll):
            now = i * unroll + c
            source = jnp.minimum(now, chunks - 1)
            parts = []
            for j in range(2):
                slot, y = row_of(2 * source + j)
                parts.append(
                    jnp.concatenate(
                        [table[slot, pl.ds(SUB * SUB * m + y, SUB, stride=SUB), :] for m in range(4)],
                        axis=0,
                    )
                )
            block = jnp.concatenate(parts, axis=1).astype(bf16)
            bias = b_in[...]
            hidden, last = one[...], two[...]
            u = jnp.dot(w_in[...], block, preferred_element_type=f32)
            u = u + jnp.concatenate([bias, bias], axis=1)
            v = jnp.dot(w_mid[...], hidden, preferred_element_type=f32)
            out = jnp.dot(w_out[...], last, preferred_element_type=f32)
            one[...] = silu_half(u)
            two[...] = silu_half(v)
            done = now - 2
            for j in range(2):
                slot, y = row_of(2 * jnp.clip(done, 0, chunks - 1) + j)
                slot = jnp.where((done >= 0) & (done < chunks), slot, slots)
                heads[slot, pl.ds(y, SUB, stride=SUB), :] = out[:, LANE * j : LANE * (j + 1)]
        return carry

    one[...] = jnp.zeros(one.shape, bf16)
    two[...] = jnp.zeros(two.shape, bf16)
    lax.fori_loop(0, -(-(chunks + 2) // unroll), step, 0)


def inner_row(n):
    slot, y = n // (SUB - 1), n % (SUB - 1)
    p = (slot >= XL - 1).astype(jnp.int32)
    return slot + 1 + p, y + 1 - p


def outer_row(n):
    each = 2 * SUB + XL - 1
    p = (n >= each).astype(jnp.int32)
    t = n - p * each
    face, slab = t < SUB, t < 2 * SUB
    slot = jnp.where(face, (XL - 1) * p, jnp.where(slab, XL, t - 2 * SUB + 1 - p))
    y = jnp.where(face, t, jnp.where(slab, t - SUB, (SUB - 1) * p))
    return slot + (XL + 1) * p, y


def inner_body(disp, mom, slab, w_in, b_in, w_mid, w_out, heads, near, table, one, two):
    for p in range(2):
        near_tiles(p, disp, mom, slab, None, near)
        inner = range(1, XL) if p == 0 else range(XL - 1)
        feature_rows(p, disp, mom, slab, near, table.at[pl.ds((XL + 1) * p, XL + 1)], inner)
    total = 2 * (XL - 1) * (SUB - 1)
    perceptron(table, heads, w_in, b_in, w_mid, w_out, one, two, inner_row, total, 4)


def outer_body(
    disp, mom, slab, xup, xdn, yup, ydn, xyup, xydn, w_in, b_in, w_mid, w_out, inner,
    cbrick, force, near, table, heads, one, two,
):
    e0 = odd_mask(0)
    slots = XL + 1
    for n in range(2 * slots):
        heads[n] = inner[n]
    for p in range(2):
        args = (xup.at[0], yup, xyup) if p == 0 else (xdn.at[xdn.shape[0] - 1], ydn, xydn)
        near_tiles(p, disp, mom, slab, args, near)
        part = table.at[pl.ds(slots * p, slots)]
        feature_rows(p, disp, mom, slab, near, part, range(slots))
    total = 2 * (2 * SUB + XL - 1)
    perceptron(table, heads, w_in, b_in, w_mid, w_out, one, two, outer_row, total, 3)
    for p in range(2):
        coupling = []
        for slot in range(slots):
            at = slots * p + slot
            coupling.append(1.0 + 0.5 * jnp.tanh(heads[at, 3 * SUB : 4 * SUB, :]))
            if slot < XL:
                for k in range(3):
                    force[3 * p + k, slot] = heads[at, k * SUB : (k + 1) * SUB, :]
        for xh in range(2):
            even, odd = coupling[2 * xh], coupling[2 * xh + 1]
            cbrick[2 * xh + p] = jnp.where(e0, odd, even)
            cbrick[2 * (2 + xh) + p] = jnp.where(e0, even, odd)
        cbrick[8 + p] = jnp.where(e0, lanes(coupling[4], 64), coupling[4])
        for k in range(4):
            h = slab[6 + 3 * p + k if k < 3 else 12 + p]
            cbrick[10 + 4 * p + k] = jnp.where(e0, lanes(h, 64), h)


def move_body(disp, vel, force, disp_out, vel_out):
    v = vel[...] + lattice_step * force[...]
    vel_out[...] = v
    disp_out[...] = disp[...] + lattice_step * v


def even_fit(func, terms):
    edge = (np.pi / 2) ** 2 * 1.0001
    node = np.cos((np.arange(400) + 0.5) * np.pi / 400)
    w = 0.5 * edge * (1 + node)
    basis = np.stack([w**n for n in range(terms)], 1)
    return [float(c) for c in np.linalg.lstsq(basis, func(np.sqrt(w)), rcond=None)[0]]


ROOT = float(np.sqrt(2.0))
SIN = [ROOT * c * np.pi ** (2 * n + 1) for n, c in enumerate(even_fit(lambda r: np.sin(r) / r, 5))]
COS = [ROOT * c * np.pi ** (2 * n) for n, c in enumerate(even_fit(np.cos, 5))]


def horner(coeffs, w):
    out = float(coeffs[-1])
    for c in reversed(coeffs[:-1]):
        out = out * w + float(c)
    return out


def crossed(a, b):
    return (a[1] * b[2] - a[2] * b[1], a[2] * b[0] - a[0] * b[2], a[0] * b[1] - a[1] * b[0])


def rotated(s, b, half_turns, hit):
    square = b[0] * b[0] + b[1] * b[1] + b[2] * b[2]
    inverse = lax.rsqrt(jnp.maximum(square, 1e-30))
    angle = (square * inverse) * half_turns
    angle = angle - jnp.round(angle)
    w = angle * angle
    sine = jnp.where(hit, horner(SIN, w) * (angle * inverse), 0.0)
    cosine = horner(COS, w)
    axis = [sine * b[k] for k in range(3)]
    first = crossed(axis, s)
    second = crossed(axis, [cosine * s[k] + first[k] for k in range(3)])
    return [s[k] + second[k] for k in range(3)]


def turns_body(nx, ny, masks, *refs):
    count = len(masks)
    bricks, cbricks = refs[:count], refs[count : 2 * count]
    out = refs[2 * count]
    mc, mh, sc, sh, cc, ch, tc, th, nc, nh = refs[2 * count + 1 :]
    xh_all, groups = 2 * nx, nx // 2
    ix, iy = lax.axis_index("gx"), lax.axis_index("gy")
    lane = iota(1)
    block = lane_block()
    first_half = block < 2
    e0 = odd_mask(0)

    def row_mask(r, par):
        return ((lane + (r + par)) & 1) == 1

    def own_rows(by):
        return pl.ds(pl.multiple_of(by * SUB, SUB), SUB)

    def place(comps, cell, slab):
        for n, (mx, my) in enumerate(masks):
            bx, by = ix ^ mx, iy ^ my
            for k in range(comps):
                for par in range(2):
                    for xh in range(2):
                        sc[par, k, 2 * bx + xh, own_rows(by), :] = cell(n, 2 * par + xh, k)
                sh[k, bx, own_rows(by), :] = slab(n, k)

    def spread(comps, put_c, put_h):
        for k in range(comps):
            for r in range(ny):
                part = pl.ds(r, SUB, stride=ny)
                for par in range(2):
                    for j in range(xh_all):
                        put_c(k, par, r, j, sc[par, k, j, part, :])
                for g in range(groups):
                    even, odd = sh[k, 2 * g, part, :], sh[k, 2 * g + 1, part, :]
                    put_h(k, 0, r, g, jnp.where(first_half, even, lanes(odd, 64)))
                    put_h(k, 1, r, g, jnp.where(first_half, lanes(even, 64), odd))

    def put_mc(k, par, r, j, v):
        mc[k // 4, par, k % 4, r, j] = v

    def put_mh(k, par, r, g, v):
        mh[k // 4, par, k % 4, r, g] = v

    def put_cc(k, par, r, j, v):
        cc[k, par, r, j] = v * (1.0 / second_shell)

    def put_ch(k, par, r, g, v):
        ch[k, par, r, g] = v * (1.0 / second_shell)

    def next_block(tiles, g):
        other = tiles[(g + 1) % groups]
        return lanes(jnp.where(block == 0, other, tiles[g]) if groups > 1 else tiles[g], -SLAB)

    def last_block(tiles, g):
        other = tiles[(g - 1) % groups]
        return lanes(jnp.where(block == 3, other, tiles[g]) if groups > 1 else tiles[g], SLAB)

    def seams(c, h):
        return (
            [lanes(h[x // 4], -SLAB * (x % 4)) for x in range(xh_all)],
            [merge_blocks(c[4 * g : 4 * g + 4]) for g in range(groups)],
        )

    def z_next(c, h, seam):
        cs = [lanes(jnp.where(lane == 0, seam[0][x], c[x]), -1) for x in range(xh_all)]
        at = (lane & (SLAB - 1)) == 0
        return cs, [lanes(jnp.where(at, seam[1][g], h[g]), -1) for g in range(groups)]

    def z_last(c, h, seam):
        cs = [lanes(jnp.where(lane == LANE - 1, seam[0][x], c[x]), 1) for x in range(xh_all)]
        at = (lane & (SLAB - 1)) == SLAB - 1
        return cs, [lanes(jnp.where(at, seam[1][g], h[g]), 1) for g in range(groups)]

    def y_next(ref, head, r, j):
        return rows(ref[*head, 0, j], -1) if r == ny - 1 else ref[*head, r + 1, j]

    def y_last(ref, head, r, j):
        return rows(ref[*head, ny - 1, j], 1) if r == 0 else ref[*head, r - 1, j]

    def near_total(p):
        q = 1 - p
        y_move = y_last if p == 0 else y_next
        z_move = z_last if p == 0 else z_next

        def component(k, carry):
            for r in range(ny):
                e = row_mask(r, 0)
                for ref, to, size in ((mc, tc, xh_all), (mh, th, groups)):
                    zero = [ref[q, 0, k, r, j] for j in range(size)]
                    one = [ref[q, 1, k, r, j] for j in range(size)]
                    even = [jnp.where(e, one[j], zero[j]) for j in range(size)]
                    odd = [jnp.where(e, zero[j], one[j]) for j in range(size)]
                    for j in range(size):
                        to[k, 0, r, j] = zero[j] + one[j]
                        if p == 0:
                            prev = odd[(j - 1) % size] if ref is mc else last_block(odd, j)
                            to[k, 1, r, j] = even[j] + prev
                        else:
                            after = even[(j + 1) % size] if ref is mc else next_block(even, j)
                            to[k, 1, r, j] = odd[j] + after
            for r in range(ny):
                e = row_mask(r, 0)
                got = []
                for t in range(2):
                    c = [tc[k, t, r, j] + y_move(tc, (k, t), r, j) for j in range(xh_all)]
                    h = [th[k, t, r, j] + y_move(th, (k, t), r, j) for j in range(groups)]
                    cs, hs = z_move(c, h, seams(c, h))
                    got.append(
                        ([c[j] + cs[j] for j in range(xh_all)], [h[j] + hs[j] for j in range(groups)])
                    )
                for kind, to, size in ((0, nc, xh_all), (1, nh, groups)):
                    for j in range(size):
                        whole, split = got[0][kind][j], got[1][kind][j]
                        if p == 1:
                            whole, split = split, whole
                        to[0, k, r, j] = jnp.where(e, whole, split)
                        to[1, k, r, j] = jnp.where(e, split, whole)
            return carry

        lax.fori_loop(0, 3, component, 0)

    def turn(p, par, bit, half_turns):
        opp = 1 - par
        for r in range(ny):
            e = row_mask(r, par)
            shell_c, shell_h = [], []
            for k in range(3):
                head = (p, opp, k)
                c = [mc[*head, r, j] for j in range(xh_all)]
                h = [mh[*head, r, g] for g in range(groups)]
                seam = seams(c, h)
                cn, hn = z_next(c, h, seam)
                cl, hl = z_last(c, h, seam)
                one, two = [], []
                for j in range(xh_all):
                    x = c[j] + jnp.where(e, c[(j + 1) % xh_all], c[(j - 1) % xh_all])
                    y = y_next(mc, head, r, j) + y_last(mc, head, r, j)
                    one.append(x + y + (cn[j] + cl[j]))
                for g in range(groups):
                    x = h[g] + jnp.where(e, next_block(h, g), last_block(h, g))
                    y = y_next(mh, head, r, g) + y_last(mh, head, r, g)
                    two.append(x + y + (hn[g] + hl[g]))
                shell_c.append(one)
                shell_h.append(two)
            for state, couple, near, shell, size in (
                (mc, cc, nc, shell_c, xh_all),
                (mh, ch, nh, shell_h, groups),
            ):
                for j in range(size):
                    cpl = couple[p, par, r, j]
                    field = [cpl * near[par, k, r, j] + shell[k][j] for k in range(3)]
                    own = [state[p, par, k, r, j] for k in range(3)]
                    new = rotated(own, field, half_turns, state[p, par, 3, r, j] == bit)
                    for k in range(3):
                        state[p, par, k, r, j] = new[k]

    def last_turn(p, par, bit, half_turns):
        opp = 1 - par
        first = 2 * ix
        before = jnp.where(ix == 0, xh_all - 1, first - 1)
        after = jnp.where(ix == nx - 1, 0, first + 2)
        near_x = (before, first, first + 1, after)
        for r in range(ny):
            e = row_mask(r, par)
            fields = [[], []]
            for k in range(3):
                head = (p, opp, k)
                c = [mc[*head, r, x] for x in near_x]
                for n in (1, 2):
                    x = near_x[n]
                    seam = pltpu.roll(mh[*head, r, x // 4], (LANE - SLAB * (x % 4)) % LANE, 1)
                    up = lanes(jnp.where(lane == 0, seam, c[n]), -1)
                    down = lanes(jnp.where(lane == LANE - 1, seam, c[n]), 1)
                    shell = c[n] + jnp.where(e, c[n + 1], c[n - 1]) + (up + down)
                    shell += y_next(mc, head, r, x) + y_last(mc, head, r, x)
                    fields[n - 1].append(cc[p, par, r, x] * nc[par, k, r, x] + shell)
            for n in (1, 2):
                x = near_x[n]
                own = [mc[p, par, k, r, x] for k in range(3)]
                new = rotated(own, fields[n - 1], half_turns, mc[p, par, 3, r, x] == bit)
                for k in range(3):
                    mc[p, par, k, r, x] = new[k]

    unit = second_shell * half_step / (2.0 * np.pi)

    def sweep(p, sector, half_turns):
        turn(p, sector & 1, (sector >> 1).astype(f32), half_turns)

    def climb(i, carry):
        sweep(0, i, unit)
        return carry

    def middle(i, carry):
        sector = 3 - jnp.abs(3 - i)
        sweep(1, sector, jnp.where(i == 3, 2 * unit, unit).astype(f32))
        return carry

    def descend(i, carry):
        sweep(0, 3 - i, unit)
        return carry

    place(8, lambda n, at, k: bricks[n][at, k], lambda n, k: cbricks[n][10 + k])
    spread(8, put_mc, put_mh)
    place(2, lambda n, at, k: cbricks[n][2 * at + k], lambda n, k: cbricks[n][8 + k])
    spread(2, put_cc, put_ch)
    near_total(0)
    lax.fori_loop(0, 4, climb, 0)
    near_total(1)
    lax.fori_loop(0, 7, middle, 0)
    near_total(0)
    lax.fori_loop(0, 3, descend, 0)
    last_turn(0, 0, 0.0, unit)

    for p in range(2):
        for k in range(3):
            for par in range(2):
                for xh in range(2):
                    for r in range(ny):
                        sc[par, k, xh, pl.ds(r, SUB, stride=ny), :] = mc[p, par, k, r, 2 * ix + xh]
            for xh in range(2):
                zero, one = sc[0, k, xh, own_rows(iy), :], sc[1, k, xh, own_rows(iy), :]
                out[3 * p + k, 2 * xh] = jnp.where(e0, one, zero)
                out[3 * p + k, 2 * xh + 1] = jnp.where(e0, zero, one)


def on_device(nx, ny, nz, displacement, velocity, moments, sector_bit, weight_in, bias_in, weight_mid, weight_out):
    assert displacement.shape == (6, XL, SUB, LANE)
    assert nx % 2 == 0 and nx & (nx - 1) == 0 and ny & (ny - 1) == 0 and ny % 2 == 0
    plane = ("gx", "gy")

    def pairs(move):
        out = []
        for x in range(nx):
            for y in range(ny):
                tx, ty = move(x, y)
                out.append((x * ny + y, tx % nx * ny + ty % ny))
        return out

    def shift(v, dx, dy):
        return lax.ppermute(v, plane, pairs(lambda x, y: (x + dx, y + dy)))

    def swap(v, mx, my):
        return lax.ppermute(v, plane, pairs(lambda x, y: (x ^ mx, y ^ my)))

    def along_z(v, step):
        return lax.ppermute(v, "gz", [(i, (i + step) % nz) for i in range(nz)])

    w_in = (weight_in.T.astype(f32) * 0.5).astype(bf16)
    w_out = jnp.pad(weight_out.T, ((0, SUB - 4), (0, 0)))
    hidden = weight_mid.shape[0]
    b_in = jnp.broadcast_to((0.5 * bias_in)[:, None], (hidden, LANE))

    packed, brick, disp_here, mom_here, w_here = vmem_call(
        pack_body,
        [((14, *TILE), f32), ((4, 8, *TILE), f32)] + [(displacement.shape, f32)] * 2
        + [(weight_mid.shape, bf16)],
        *[pltpu.with_memory_space_constraint(x, pltpu.HBM) for x in (displacement, moments, sector_bit, weight_mid)],
        space=pltpu.HBM,
        scratch=[
            pltpu.VMEM(sector_bit.shape, sector_bit.dtype),
            pltpu.SemaphoreType.DMA((4,)),
        ],
    )
    low = along_z(packed, 1)
    high = along_z(packed, -1)
    far = [(mx, my) for mx in range(nx) for my in range(0, ny, 2) if mx or my]
    held = {(0, 0): brick}
    for mask in far:
        held[mask] = swap(brick, *mask)
    slab, faces, yup, ydn = vmem_call(
        halo_body,
        [((14, *TILE), f32), ((2, 12, *TILE), f32)] + [((6, *TILE), f32)] * 2,
        disp_here, mom_here, low, high,
    )
    if nx == 2:
        faces = shift(faces, 1, 0)
        xup, xdn = faces, faces
    else:
        xup, xdn = shift(faces[:1], 1, 0), shift(faces[1:], -1, 0)
    xyup, xydn = shift(yup, 1, 1), shift(ydn, -1, -1)
    yup, ydn = shift(yup, 0, 1), shift(ydn, 0, -1)

    w_mid = (w_here.T.astype(f32) * 0.5).astype(bf16)
    weights = (w_in, b_in, w_mid, w_out)
    work = [
        pltpu.VMEM((6, 4, XL + 3, *TILE), f32),
        pltpu.VMEM((2 * XL + 2, 32 * SUB, LANE), f32),
        pltpu.VMEM((2 * XL + 3, SUB * SUB, LANE), f32),
        pltpu.VMEM((hidden, 2 * LANE), bf16),
        pltpu.VMEM((hidden, 2 * LANE), bf16),
    ]
    (inner,) = vmem_call(
        inner_body, [((2 * XL + 3, SUB * SUB, LANE), f32)], disp_here, mom_here, slab, *weights,
        scratch=work[:2] + work[3:],
        cost=pl.CostEstimate(flops=10**9, bytes_accessed=2 << 20, transcendentals=3 << 20),
    )
    cbrick, force = vmem_call(
        outer_body,
        [((18, *TILE), f32), ((6, XL, *TILE), f32)],
        disp_here, mom_here, slab, xup, xdn, yup, ydn, xyup, xydn, *weights, inner,
        scratch=work,
    )
    disp_out, vel_out = vmem_call(
        move_body, [((6, XL, *TILE), f32)] * 2, disp_here, velocity, force,
    )
    near_masks = [(0, 0)] + far
    late = lax.optimization_barrier((cbrick, *[held[m] for m in near_masks]))
    cbrick = late[0]
    held.update(zip(near_masks, late[1:]))
    cheld = {(0, 0): cbrick}
    for mask in far:
        cheld[mask] = swap(cbrick, *mask)
    for mx, my in near_masks:
        held[mx, my + 1] = swap(held[mx, my], 0, 1)
    for mx, my in near_masks:
        cheld[mx, my + 1] = swap(cheld[mx, my], 0, 1)

    masks = sorted(held)
    xh_all, groups = 2 * nx, nx // 2
    (moments_out,) = vmem_call(
        functools.partial(turns_body, nx, ny, masks),
        [((6, XL, *TILE), f32)],
        *[held[m] for m in masks],
        *[cheld[m] for m in masks],
        scratch=[
            pltpu.VMEM((2, 2, 4, ny, xh_all, *TILE), f32),
            pltpu.VMEM((2, 2, 4, ny, groups, *TILE), f32),
            pltpu.VMEM((2, 8, xh_all, ny * SUB, LANE), f32),
            pltpu.VMEM((8, nx, ny * SUB, LANE), f32),
            pltpu.VMEM((2, 2, ny, xh_all, *TILE), f32),
            pltpu.VMEM((2, 2, ny, groups, *TILE), f32),
            pltpu.VMEM((3, 2, ny, xh_all, *TILE), f32),
            pltpu.VMEM((3, 2, ny, groups, *TILE), f32),
            pltpu.VMEM((2, 3, ny, xh_all, *TILE), f32),
            pltpu.VMEM((2, 3, ny, groups, *TILE), f32),
        ],
    )
    return disp_out, vel_out, moments_out


def solution(mesh):
    placed = P(None, "gx", "gy", "gz")
    sizes = [mesh.shape[axis] for axis in ("gx", "gy", "gz")]
    return jax.shard_map(
        functools.partial(on_device, *sizes),
        mesh=mesh,
        in_specs=(placed,) * 4 + (P(),) * 4,
        out_specs=(placed,) * 3,
        check_vma=False,
    )
```

```python
import functools

import jax
import jax.numpy as jnp
import numpy as np
from jax import lax
from jax.experimental import pallas as pl
from jax.experimental.pallas import tpu as pltpu
from jax.sharding import PartitionSpec as P


half_step = 0.1
lattice_step = 0.25
second_shell = 0.5

f32 = jnp.float32
bf16 = jnp.bfloat16
SUB, LANE = 8, 128
SLAB = 32
XL = 4
ORDER = (0, 2, 1, 3)
TILE = (SUB, LANE)


def iota(dim):
    return lax.broadcasted_iota(jnp.int32, TILE, dim)


def odd_mask(par):
    return ((iota(0) + iota(1) + par) & 1) == 1


def lane_block():
    return ((iota(1) + SLAB // 2) // SLAB) & 3


def lanes(v, shift):
    shift = shift % LANE
    return v if shift == 0 else pltpu.roll(v, shift, 1)


def rows(v, shift):
    return pltpu.roll(v, shift % SUB, 0)


def merge_blocks(tiles):
    block = lane_block()
    out = lanes(tiles[0], 0)
    for b in range(1, 4):
        out = jnp.where(block == b, lanes(tiles[b], SLAB * b), out)
    return out


def vmem_call(body, out_shapes, *args, scratch=(), cost=None, space=None, grant=24 << 20):
    spec = pl.BlockSpec(memory_space=pltpu.VMEM)
    given = pl.BlockSpec(memory_space=space or pltpu.VMEM)
    return pl.pallas_call(
        body,
        out_shape=tuple(jax.ShapeDtypeStruct(s, d) for s, d in out_shapes),
        in_specs=[given] * len(args),
        out_specs=tuple(spec for _ in out_shapes),
        scratch_shapes=list(scratch),
        compiler_params=pltpu.CompilerParams(vmem_limit_bytes=grant),
        cost_estimate=cost,
    )(*args)


def pack_body(disp_in, mom_in, bit_in, w_in, out, brick, disp, mom, w, bit, sems):
    copies = [
        pltpu.make_async_copy(source, target, sems.at[n])
        for n, (source, target) in enumerate(((disp_in, disp), (mom_in, mom), (bit_in, bit), (w_in, w)))
    ]
    for copy in copies:
        copy.start()
    for copy in copies[:3]:
        copy.wait()
    for i in range(14):
        if i < 6:
            tiles = [disp[i, x] for x in ORDER]
        elif i < 12:
            tiles = [mom[i - 6, x] for x in ORDER]
        else:
            tiles = [bit[i - 12, x].astype(f32) for x in ORDER]
        out[i] = merge_blocks(tiles)
    e0 = odd_mask(0)
    for p in range(2):
        for k in range(4):
            tiles = [mom[3 * p + k, x] if k < 3 else bit[p, x].astype(f32) for x in range(XL)]
            for xh in range(2):
                even, odd = tiles[2 * xh], tiles[2 * xh + 1]
                brick[xh, 4 * p + k] = jnp.where(e0, odd, even)
                brick[2 + xh, 4 * p + k] = jnp.where(e0, even, odd)
    copies[3].wait()


def halo_body(disp, mom, low, high, slab, faces, yup, ydn):
    upper = (iota(1) & (SLAB - 1)) >= SLAB // 2
    for i in range(14):
        slab[i] = jnp.where(upper, low[i], high[i])
    for i in range(6):
        src = disp if i < 3 else mom
        k = i % 3
        base = 0 if i < 3 else 6
        faces[0, 2 * i] = src[3 + k, XL - 1]
        faces[0, 2 * i + 1] = slab[base + 3 + k]
        faces[1, 2 * i] = src[k, 0]
        faces[1, 2 * i + 1] = slab[base + k]
        yup[i] = jnp.zeros(TILE, f32)
        ydn[i] = jnp.zeros(TILE, f32)
        for x in range(XL):
            yup[i, x : x + 1, :] = src[3 + k, x, SUB - 1 : SUB, :]
            ydn[i, x : x + 1, :] = src[k, x, 0:1, :]
        yup[i, XL : XL + 1, :] = slab[base + 3 + k, SUB - 1 : SUB, :]
        ydn[i, XL : XL + 1, :] = slab[base + k, 0:1, :]


def near_tiles(p, disp, mom, slab, halo, near):
    xf, yr, xyr = halo or (None, None, None)
    q = 1 - p
    lane, sub = iota(1), iota(0)
    block = lane_block()
    edge_x = XL - 1 if p == 0 else 0

    def component(k, carry):
        for half in range(2):
            i = 3 * half + k
            src = mom if half else disp
            c = [src[3 * q + k, x] for x in range(XL)]
            h = slab[6 * half + 3 * q + k]
            fc, fh = (xf[2 * i], xf[2 * i + 1]) if halo else (None, None)

            def wide(row):
                return jnp.broadcast_to(row, TILE)

            for dy in range(2):
                if dy:
                    step = 1 if p == 0 else -1
                    put = sub == (0 if p == 0 else SUB - 1)
                    c = [rows(c[x], step) for x in range(XL)]
                    h = rows(h, step)
                    if halo:
                        c = [jnp.where(put, wide(yr[i, x : x + 1, :]), c[x]) for x in range(XL)]
                        h = jnp.where(put, wide(yr[i, XL : XL + 1, :]), h)
                        fc = jnp.where(put, wide(xyr[i, edge_x : edge_x + 1, :]), rows(fc, step))
                        fh = jnp.where(put, wide(xyr[i, XL : XL + 1, :]), rows(fh, step))
                for dz in range(2):
                    if dz == 0:
                        cs, hs, fcs, fhs = c, h, fc, fh
                    else:
                        step = 1 if p == 0 else -1
                        seam = LANE - 1 if p == 0 else 0
                        at_seam = lane == seam
                        at_seams = (lane & (SLAB - 1)) == (SLAB - 1 if p == 0 else 0)
                        cs = [
                            lanes(jnp.where(at_seam, lanes(h, -SLAB * ORDER[x]), c[x]), step)
                            for x in range(XL)
                        ]
                        if halo:
                            hs = lanes(jnp.where(at_seams, merge_blocks([c[x] for x in ORDER]), h), step)
                            fcs = lanes(jnp.where(at_seam, lanes(fh, -SLAB * ORDER[edge_x]), fc), step)
                            fhs = lanes(jnp.where(at_seams, lanes(fc, SLAB * ORDER[edge_x]), fh), step)
                    at = 2 * dy + dz
                    for x in range(XL):
                        near[i, at, x + 1 - p] = cs[x]
                    if not halo:
                        continue
                    near[i, at, XL * p] = fcs
                    near[i, at, XL + 1] = hs
                    if p == 0:
                        moved = jnp.where(block == 0, lanes(fhs, SLAB), lanes(hs, 2 * SLAB))
                        moved = jnp.where(block == 1, lanes(hs, -SLAB), moved)
                    else:
                        moved = jnp.where(block == 3, lanes(fhs, -SLAB), lanes(hs, 2 * SLAB))
                        moved = jnp.where(block == 2, lanes(hs, SLAB), moved)
                    near[i, at, XL + 2] = moved
        return carry

    if halo:
        lax.fori_loop(0, 3, component, 0)
    else:
        for k in range(3):
            component(k, 0)


def feature_rows(p, disp, mom, slab, near, table, slots):
    for slot in slots:
        if slot < XL:
            own = [disp[3 * p + k, slot] for k in range(3)]
            own += [mom[3 * p + k, slot] for k in range(3)]
        else:
            own = [slab[3 * p + k] for k in range(3)] + [slab[6 + 3 * p + k] for k in range(3)]
        for o in range(8):
            dx, at = o >> 2, o & 3
            if slot == XL:
                j = XL + 1 + dx
            else:
                j = slot + 1 - dx if p == 0 else slot + dx
            for k in range(3):
                table[slot, SUB * (4 * o + k) : SUB * (4 * o + k + 1), :] = near[k, at, j] - own[k]
            dot = own[3] * near[3, at, j] + own[4] * near[4, at, j] + own[5] * near[5, at, j]
            table[slot, SUB * (4 * o + 3) : SUB * (4 * o + 4), :] = dot


def silu_half(u):
    return (u + u * jnp.tanh(u)).astype(bf16)


def perceptron(table, heads, w_in, b_in, w_mid, w_out, one, two, row_of, total, unroll):
    slots = 2 * XL + 2
    chunks = total // 2

    def step(i, carry):
        for c in range(unroll):
            now = i * unroll + c
            source = jnp.minimum(now, chunks - 1)
            parts = []
            for j in range(2):
                slot, y = row_of(2 * source + j)
                parts.append(
                    jnp.concatenate(
                        [table[slot, pl.ds(SUB * SUB * m + y, SUB, stride=SUB), :] for m in range(4)],
                        axis=0,
                    )
                )
            block = jnp.concatenate(parts, axis=1).astype(bf16)
            bias = b_in[...]
            hidden, last = one[...], two[...]
            u = jnp.dot(w_in[...], block, preferred_element_type=f32)
            u = u + jnp.concatenate([bias, bias], axis=1)
            v = jnp.dot(w_mid[...], hidden, preferred_element_type=f32)
            out = jnp.dot(w_out[...], last, preferred_element_type=f32)
            one[...] = silu_half(u)
            two[...] = silu_half(v)
            done = now - 2
            for j in range(2):
                slot, y = row_of(2 * jnp.clip(done, 0, chunks - 1) + j)
                slot = jnp.where((done >= 0) & (done < chunks), slot, slots)
                heads[slot, pl.ds(y, SUB, stride=SUB), :] = out[:, LANE * j : LANE * (j + 1)]
        return carry

    one[...] = jnp.zeros(one.shape, bf16)
    two[...] = jnp.zeros(two.shape, bf16)
    lax.fori_loop(0, -(-(chunks + 2) // unroll), step, 0)


def inner_row(n):
    slot, y = n // (SUB - 1), n % (SUB - 1)
    p = (slot >= XL - 1).astype(jnp.int32)
    return slot + 1 + p, y + 1 - p


def outer_row(n):
    each = 2 * SUB + XL - 1
    p = (n >= each).astype(jnp.int32)
    t = n - p * each
    face, slab = t < SUB, t < 2 * SUB
    slot = jnp.where(face, (XL - 1) * p, jnp.where(slab, XL, t - 2 * SUB + 1 - p))
    y = jnp.where(face, t, jnp.where(slab, t - SUB, (SUB - 1) * p))
    return slot + (XL + 1) * p, y


def inner_body(disp, mom, slab, w_in, b_in, w_mid, w_out, heads, near, table, one, two):
    for p in range(2):
        near_tiles(p, disp, mom, slab, None, near)
        inner = range(1, XL) if p == 0 else range(XL - 1)
        feature_rows(p, disp, mom, slab, near, table.at[pl.ds((XL + 1) * p, XL + 1)], inner)
    total = 2 * (XL - 1) * (SUB - 1)
    perceptron(table, heads, w_in, b_in, w_mid, w_out, one, two, inner_row, total, 8)


def outer_body(
    disp, mom, slab, xup, xdn, yup, ydn, xyup, xydn, w_in, b_in, w_mid, w_out, inner,
    cbrick, force, near, table, heads, one, two,
):
    e0 = odd_mask(0)
    slots = XL + 1
    for n in range(2 * slots):
        if n % slots != XL and n not in (0, slots + XL - 1):
            heads[n] = inner[n]
    for p in range(2):
        args = (xup.at[0], yup, xyup) if p == 0 else (xdn.at[xdn.shape[0] - 1], ydn, xydn)
        near_tiles(p, disp, mom, slab, args, near)
        part = table.at[pl.ds(slots * p, slots)]
        feature_rows(p, disp, mom, slab, near, part, range(slots))
    total = 2 * (2 * SUB + XL - 1)
    perceptron(table, heads, w_in, b_in, w_mid, w_out, one, two, outer_row, total, 7)
    for p in range(2):
        coupling = []
        for slot in range(slots):
            at = slots * p + slot
            coupling.append(1.0 + 0.5 * jnp.tanh(heads[at, 3 * SUB : 4 * SUB, :]))
            if slot < XL:
                for k in range(3):
                    force[3 * p + k, slot] = heads[at, k * SUB : (k + 1) * SUB, :]
        for xh in range(2):
            even, odd = coupling[2 * xh], coupling[2 * xh + 1]
            cbrick[2 * xh + p] = jnp.where(e0, odd, even)
            cbrick[2 * (2 + xh) + p] = jnp.where(e0, even, odd)
        cbrick[8 + p] = jnp.where(e0, lanes(coupling[4], 64), coupling[4])
        for k in range(4):
            h = slab[6 + 3 * p + k if k < 3 else 12 + p]
            cbrick[10 + 4 * p + k] = jnp.where(e0, lanes(h, 64), h)


def move_body(disp, vel, force, disp_out, vel_out):
    v = vel[...] + lattice_step * force[...]
    vel_out[...] = v
    disp_out[...] = disp[...] + lattice_step * v


def even_fit(func, terms):
    edge = (np.pi / 2) ** 2 * 1.0001
    node = np.cos((np.arange(400) + 0.5) * np.pi / 400)
    w = 0.5 * edge * (1 + node)
    basis = np.stack([w**n for n in range(terms)], 1)
    return [float(c) for c in np.linalg.lstsq(basis, func(np.sqrt(w)), rcond=None)[0]]


ROOT = float(np.sqrt(2.0))
SIN = [ROOT * c * np.pi ** (2 * n + 1) for n, c in enumerate(even_fit(lambda r: np.sin(r) / r, 5))]
COS = [ROOT * c * np.pi ** (2 * n) for n, c in enumerate(even_fit(np.cos, 5))]


def horner(coeffs, w):
    out = float(coeffs[-1])
    for c in reversed(coeffs[:-1]):
        out = out * w + float(c)
    return out


def crossed(a, b):
    return (a[1] * b[2] - a[2] * b[1], a[2] * b[0] - a[0] * b[2], a[0] * b[1] - a[1] * b[0])


def rotated(s, b, half_turns, hit):
    square = b[0] * b[0] + b[1] * b[1] + b[2] * b[2]
    inverse = lax.rsqrt(jnp.maximum(square, 1e-30))
    angle = (square * inverse) * half_turns
    angle = angle - jnp.round(angle)
    w = angle * angle
    sine = jnp.where(hit, horner(SIN, w) * (angle * inverse), 0.0)
    cosine = horner(COS, w)
    axis = [sine * b[k] for k in range(3)]
    first = crossed(axis, s)
    second = crossed(axis, [cosine * s[k] + first[k] for k in range(3)])
    return [s[k] + second[k] for k in range(3)]


def turns_body(nx, ny, masks, *refs):
    count = len(masks)
    bricks, cbricks = refs[:count], refs[count : 2 * count]
    out = refs[2 * count]
    mc, mh, sc, sh, cc, ch, tc, th, nc, nh = refs[2 * count + 1 :]
    xh_all, groups = 2 * nx, nx // 2
    ix, iy = lax.axis_index("gx"), lax.axis_index("gy")
    lane = iota(1)
    block = lane_block()
    first_half = block < 2
    e0 = odd_mask(0)

    def row_mask(r, par):
        return ((lane + (r + par)) & 1) == 1

    def own_rows(by):
        return pl.ds(pl.multiple_of(by * SUB, SUB), SUB)

    def place(comps, cell, slab):
        for n, (mx, my) in enumerate(masks):
            bx, by = ix ^ mx, iy ^ my
            for k in range(comps):
                for par in range(2):
                    for xh in range(2):
                        sc[par, k, 2 * bx + xh, own_rows(by), :] = cell(n, 2 * par + xh, k)
                sh[k, bx, own_rows(by), :] = slab(n, k)

    def spread(comps, put_c, put_h):
        for k in range(comps):
            for r in range(ny):
                part = pl.ds(r, SUB, stride=ny)
                for par in range(2):
                    for j in range(xh_all):
                        put_c(k, par, r, j, sc[par, k, j, part, :])
                for g in range(groups):
                    even, odd = sh[k, 2 * g, part, :], sh[k, 2 * g + 1, part, :]
                    put_h(k, 0, r, g, jnp.where(first_half, even, lanes(odd, 64)))
                    put_h(k, 1, r, g, jnp.where(first_half, lanes(even, 64), odd))

    def put_mc(k, par, r, j, v):
        mc[k // 4, par, k % 4, r, j] = v

    def put_mh(k, par, r, g, v):
        mh[k // 4, par, k % 4, r, g] = v

    def put_cc(k, par, r, j, v):
        cc[k, par, r, j] = v * (1.0 / second_shell)

    def put_ch(k, par, r, g, v):
        ch[k, par, r, g] = v * (1.0 / second_shell)

    def next_block(tiles, g):
        other = tiles[(g + 1) % groups]
        return lanes(jnp.where(block == 0, other, tiles[g]) if groups > 1 else tiles[g], -SLAB)

    def last_block(tiles, g):
        other = tiles[(g - 1) % groups]
        return lanes(jnp.where(block == 3, other, tiles[g]) if groups > 1 else tiles[g], SLAB)

    def seams(c, h):
        return (
            [lanes(h[x // 4], -SLAB * (x % 4)) for x in range(xh_all)],
            [merge_blocks(c[4 * g : 4 * g + 4]) for g in range(groups)],
        )

    def z_next(c, h, seam):
        cs = [lanes(jnp.where(lane == 0, seam[0][x], c[x]), -1) for x in range(xh_all)]
        at = (lane & (SLAB - 1)) == 0
        return cs, [lanes(jnp.where(at, seam[1][g], h[g]), -1) for g in range(groups)]

    def z_last(c, h, seam):
        cs = [lanes(jnp.where(lane == LANE - 1, seam[0][x], c[x]), 1) for x in range(xh_all)]
        at = (lane & (SLAB - 1)) == SLAB - 1
        return cs, [lanes(jnp.where(at, seam[1][g], h[g]), 1) for g in range(groups)]

    def y_next(ref, head, r, j):
        return rows(ref[*head, 0, j], -1) if r == ny - 1 else ref[*head, r + 1, j]

    def y_last(ref, head, r, j):
        return rows(ref[*head, ny - 1, j], 1) if r == 0 else ref[*head, r - 1, j]

    def near_total(p):
        q = 1 - p
        y_move = y_last if p == 0 else y_next
        z_move = z_last if p == 0 else z_next

        def component(k, carry):
            for r in range(ny):
                e = row_mask(r, 0)
                for ref, to, size in ((mc, tc, xh_all), (mh, th, groups)):
                    zero = [ref[q, 0, k, r, j] for j in range(size)]
                    one = [ref[q, 1, k, r, j] for j in range(size)]
                    even = [jnp.where(e, one[j], zero[j]) for j in range(size)]
                    odd = [jnp.where(e, zero[j], one[j]) for j in range(size)]
                    for j in range(size):
                        to[k, 0, r, j] = zero[j] + one[j]
                        if p == 0:
                            prev = odd[(j - 1) % size] if ref is mc else last_block(odd, j)
                            to[k, 1, r, j] = even[j] + prev
                        else:
                            after = even[(j + 1) % size] if ref is mc else next_block(even, j)
                            to[k, 1, r, j] = odd[j] + after
            for r in range(ny):
                e = row_mask(r, 0)
                got = []
                for t in range(2):
                    c = [tc[k, t, r, j] + y_move(tc, (k, t), r, j) for j in range(xh_all)]
                    h = [th[k, t, r, j] + y_move(th, (k, t), r, j) for j in range(groups)]
                    cs, hs = z_move(c, h, seams(c, h))
                    got.append(
                        ([c[j] + cs[j] for j in range(xh_all)], [h[j] + hs[j] for j in range(groups)])
                    )
                for kind, to, size in ((0, nc, xh_all), (1, nh, groups)):
                    for j in range(size):
                        whole, split = got[0][kind][j], got[1][kind][j]
                        if p == 1:
                            whole, split = split, whole
                        to[0, k, r, j] = jnp.where(e, whole, split)
                        to[1, k, r, j] = jnp.where(e, split, whole)
            return carry

        lax.fori_loop(0, 3, component, 0)

    def turn(p, par, bit, half_turns):
        opp = 1 - par
        for r in range(ny):
            e = row_mask(r, par)
            shell_c, shell_h = [], []
            for k in range(3):
                head = (p, opp, k)
                c = [mc[*head, r, j] for j in range(xh_all)]
                h = [mh[*head, r, g] for g in range(groups)]
                seam = seams(c, h)
                cn, hn = z_next(c, h, seam)
                cl, hl = z_last(c, h, seam)
                one, two = [], []
                for j in range(xh_all):
                    x = c[j] + jnp.where(e, c[(j + 1) % xh_all], c[(j - 1) % xh_all])
                    y = y_next(mc, head, r, j) + y_last(mc, head, r, j)
                    one.append(x + y + (cn[j] + cl[j]))
                for g in range(groups):
                    x = h[g] + jnp.where(e, next_block(h, g), last_block(h, g))
                    y = y_next(mh, head, r, g) + y_last(mh, head, r, g)
                    two.append(x + y + (hn[g] + hl[g]))
                shell_c.append(one)
                shell_h.append(two)
            for state, couple, near, shell, size in (
                (mc, cc, nc, shell_c, xh_all),
                (mh, ch, nh, shell_h, groups),
            ):
                for j in range(size):
                    cpl = couple[p, par, r, j]
                    field = [cpl * near[par, k, r, j] + shell[k][j] for k in range(3)]
                    own = [state[p, par, k, r, j] for k in range(3)]
                    new = rotated(own, field, half_turns, state[p, par, 3, r, j] == bit)
                    for k in range(3):
                        state[p, par, k, r, j] = new[k]

    def last_turn(p, par, bit, half_turns):
        opp = 1 - par
        first = 2 * ix
        before = jnp.where(ix == 0, xh_all - 1, first - 1)
        after = jnp.where(ix == nx - 1, 0, first + 2)
        near_x = (before, first, first + 1, after)
        for r in range(ny):
            e = row_mask(r, par)
            fields = [[], []]
            for k in range(3):
                head = (p, opp, k)
                c = [mc[*head, r, x] for x in near_x]
                for n in (1, 2):
                    x = near_x[n]
                    seam = pltpu.roll(mh[*head, r, x // 4], (LANE - SLAB * (x % 4)) % LANE, 1)
                    up = lanes(jnp.where(lane == 0, seam, c[n]), -1)
                    down = lanes(jnp.where(lane == LANE - 1, seam, c[n]), 1)
                    shell = c[n] + jnp.where(e, c[n + 1], c[n - 1]) + (up + down)
                    shell += y_next(mc, head, r, x) + y_last(mc, head, r, x)
                    fields[n - 1].append(cc[p, par, r, x] * nc[par, k, r, x] + shell)
            for n in (1, 2):
                x = near_x[n]
                own = [mc[p, par, k, r, x] for k in range(3)]
                new = rotated(own, fields[n - 1], half_turns, mc[p, par, 3, r, x] == bit)
                for k in range(3):
                    mc[p, par, k, r, x] = new[k]

    unit = second_shell * half_step / (2.0 * np.pi)

    def sweep(p, sector, half_turns):
        turn(p, sector & 1, (sector >> 1).astype(f32), half_turns)

    def climb(i, carry):
        sweep(0, i, unit)
        return carry

    def middle(i, carry):
        sector = 3 - jnp.abs(3 - i)
        sweep(1, sector, jnp.where(i == 3, 2 * unit, unit).astype(f32))
        return carry

    def descend(i, carry):
        sweep(0, 3 - i, unit)
        return carry

    place(8, lambda n, at, k: bricks[n][at, k], lambda n, k: cbricks[n][10 + k])
    spread(8, put_mc, put_mh)
    place(2, lambda n, at, k: cbricks[n][2 * at + k], lambda n, k: cbricks[n][8 + k])
    spread(2, put_cc, put_ch)
    near_total(0)
    lax.fori_loop(0, 4, climb, 0)
    near_total(1)
    lax.fori_loop(0, 7, middle, 0)
    near_total(0)
    lax.fori_loop(0, 3, descend, 0)
    last_turn(0, 0, 0.0, unit)

    for p in range(2):
        for k in range(3):
            for par in range(2):
                for xh in range(2):
                    for r in range(ny):
                        sc[par, k, xh, pl.ds(r, SUB, stride=ny), :] = mc[p, par, k, r, 2 * ix + xh]
            for xh in range(2):
                zero, one = sc[0, k, xh, own_rows(iy), :], sc[1, k, xh, own_rows(iy), :]
                out[3 * p + k, 2 * xh] = jnp.where(e0, one, zero)
                out[3 * p + k, 2 * xh + 1] = jnp.where(e0, zero, one)


def on_device(nx, ny, nz, displacement, velocity, moments, sector_bit, weight_in, bias_in, weight_mid, weight_out):
    assert displacement.shape == (6, XL, SUB, LANE)
    assert nx % 2 == 0 and nx & (nx - 1) == 0 and ny & (ny - 1) == 0 and ny % 2 == 0
    plane = ("gx", "gy")

    def pairs(move):
        out = []
        for x in range(nx):
            for y in range(ny):
                tx, ty = move(x, y)
                out.append((x * ny + y, tx % nx * ny + ty % ny))
        return out

    def shift(v, dx, dy):
        return lax.ppermute(v, plane, pairs(lambda x, y: (x + dx, y + dy)))

    def swap(v, mx, my):
        return lax.ppermute(v, plane, pairs(lambda x, y: (x ^ mx, y ^ my)))

    def along_z(v, step):
        return lax.ppermute(v, "gz", [(i, (i + step) % nz) for i in range(nz)])

    w_in = (weight_in.T.astype(f32) * 0.5).astype(bf16)
    w_out = jnp.pad(weight_out.T, ((0, SUB - 4), (0, 0)))
    hidden = weight_mid.shape[0]
    b_in = jnp.broadcast_to((0.5 * bias_in)[:, None], (hidden, LANE))

    packed, brick, disp_here, mom_here, w_here = vmem_call(
        pack_body,
        [((14, *TILE), f32), ((4, 8, *TILE), f32)] + [(displacement.shape, f32)] * 2
        + [(weight_mid.shape, bf16)],
        *[pltpu.with_memory_space_constraint(x, pltpu.HBM) for x in (displacement, moments, sector_bit, weight_mid)],
        space=pltpu.HBM,
        scratch=[
            pltpu.VMEM(sector_bit.shape, sector_bit.dtype),
            pltpu.SemaphoreType.DMA((4,)),
        ],
    )
    low = along_z(packed, 1)
    high = along_z(packed, -1)
    far = [(mx, my) for mx in range(nx) for my in range(0, ny, 2) if mx or my]
    held = {(0, 0): brick}
    for mask in far:
        held[mask] = swap(brick, *mask)
    slab, faces, yup, ydn = vmem_call(
        halo_body,
        [((14, *TILE), f32), ((2, 12, *TILE), f32)] + [((6, *TILE), f32)] * 2,
        disp_here, mom_here, low, high,
    )
    if nx == 2:
        faces = shift(faces, 1, 0)
        xup, xdn = faces, faces
    else:
        xup, xdn = shift(faces[:1], 1, 0), shift(faces[1:], -1, 0)
    xyup, xydn = shift(yup, 1, 1), shift(ydn, -1, -1)
    yup, ydn = shift(yup, 0, 1), shift(ydn, 0, -1)

    w_mid = (w_here.T.astype(f32) * 0.5).astype(bf16)
    weights = (w_in, b_in, w_mid, w_out)
    work = [
        pltpu.VMEM((6, 4, XL + 3, *TILE), f32),
        pltpu.VMEM((2 * XL + 2, 32 * SUB, LANE), f32),
        pltpu.VMEM((2 * XL + 3, SUB * SUB, LANE), f32),
        pltpu.VMEM((hidden, 2 * LANE), bf16),
        pltpu.VMEM((hidden, 2 * LANE), bf16),
    ]
    (inner,) = vmem_call(
        inner_body, [((2 * XL + 3, SUB * SUB, LANE), f32)], disp_here, mom_here, slab, *weights,
        scratch=work[:2] + work[3:],
        cost=pl.CostEstimate(flops=10**9, bytes_accessed=2 << 20, transcendentals=3 << 20),
    )
    cbrick, force = vmem_call(
        outer_body,
        [((18, *TILE), f32), ((6, XL, *TILE), f32)],
        disp_here, mom_here, slab, xup, xdn, yup, ydn, xyup, xydn, *weights, inner,
        scratch=work,
    )
    disp_out, vel_out = vmem_call(
        move_body, [((6, XL, *TILE), f32)] * 2, disp_here, velocity, force,
    )
    near_masks = [(0, 0)] + far
    late = lax.optimization_barrier((cbrick, *[held[m] for m in near_masks]))
    cbrick = late[0]
    held.update(zip(near_masks, late[1:]))
    cheld = {(0, 0): cbrick}
    for mask in far:
        cheld[mask] = swap(cbrick, *mask)
    for mx, my in near_masks:
        held[mx, my + 1] = swap(held[mx, my], 0, 1)
    for mx, my in near_masks:
        cheld[mx, my + 1] = swap(cheld[mx, my], 0, 1)

    masks = sorted(held)
    xh_all, groups = 2 * nx, nx // 2
    (moments_out,) = vmem_call(
        functools.partial(turns_body, nx, ny, masks),
        [((6, XL, *TILE), f32)],
        *[held[m] for m in masks],
        *[cheld[m] for m in masks],
        scratch=[
            pltpu.VMEM((2, 2, 4, ny, xh_all, *TILE), f32),
            pltpu.VMEM((2, 2, 4, ny, groups, *TILE), f32),
            pltpu.VMEM((2, 8, xh_all, ny * SUB, LANE), f32),
            pltpu.VMEM((8, nx, ny * SUB, LANE), f32),
            pltpu.VMEM((2, 2, ny, xh_all, *TILE), f32),
            pltpu.VMEM((2, 2, ny, groups, *TILE), f32),
            pltpu.VMEM((3, 2, ny, xh_all, *TILE), f32),
            pltpu.VMEM((3, 2, ny, groups, *TILE), f32),
            pltpu.VMEM((2, 3, ny, xh_all, *TILE), f32),
            pltpu.VMEM((2, 3, ny, groups, *TILE), f32),
        ],
    )
    return disp_out, vel_out, moments_out


def solution(mesh):
    placed = P(None, "gx", "gy", "gz")
    sizes = [mesh.shape[axis] for axis in ("gx", "gy", "gz")]
    return jax.shard_map(
        functools.partial(on_device, *sizes),
        mesh=mesh,
        in_specs=(placed,) * 4 + (P(),) * 4,
        out_specs=(placed,) * 3,
        check_vma=False,
    )
```
